256 devices in a mesh: gx: 8 (over z), gy: 8 (over y, core), gz: 4 (over x).
Axes of the slice: x: 4, y: 4, z: 8, core: 2. Of those that a mesh axis runs over, the one named last changes fastest.
Arguments:
- x_block: float32 [16, 64, 32, 512], P(None, 'gx', 'gy', 'gz'), may hold values from -6 to 6
- p_block: float32 [16, 64, 32, 512], P(None, 'gx', 'gy', 'gz'), may hold values from -6 to 6
- voxel_class: int32 [64, 32, 512], P('gx', 'gy', 'gz'), may hold values from 0 to 7
- conductance: float32 [8], replicated, may hold values from 0.25 to 4
Outputs:
- x_next: float32 [16, 64, 32, 512], P(None, 'gx', 'gy', 'gz')
- p_next: float32 [16, 64, 32, 512], P(None, 'gx', 'gy', 'gz')
The draws below stay inside these ranges and needn't reach their ends.
All inputs are finite; a program needn't handle non-finite values.
Results may differ from the reference program's by a relative error of at most 0.0003.
Values sent between devices are 32-bit elements; how exact they have to be, the bound alone decides.
No kernel may reach another device: no remote copies, remote signals or barrier semaphores. Data moves between devices by JAX's collectives and lax.ppermute only.
A program may use at most 64 MiB of HBM per device.

```python
import math
import jax
import jax.numpy as jnp
from jax import lax

VECS = 16
CLASSES = 8
ITERS = 2
INNER = 4
NX = 64
NY = 32
NZ = 512


def plant(drawn, key, least, high):
    longest = drawn.shape.index(max(drawn.shape))
    spots = []
    for shift in (0, 1):
        where = [jax.random.randint(jax.random.fold_in(key, axis), (), 0, length) for axis, length in enumerate(drawn.shape)]
        where[longest] = (where[longest] + shift) % drawn.shape[longest]
        spots.append(tuple(where))
    return drawn.at[spots[0]].set(least).at[spots[1]].set(high)


def block_levels(key, dims, cuts, least, largest):
    level = 1.0
    for dim, shards_of in cuts:
        steps = jax.random.uniform(jax.random.fold_in(jax.random.fold_in(key, 6), dim), (shards_of,), jnp.float32, least / len(cuts), largest / len(cuts))
        level = level * jnp.repeat(jnp.exp(steps), dims[dim] // shards_of).reshape((-1,) + (1,) * (len(dims) - 1 - dim))
    return level


def normal_values(own_key, dims, deviation, most, cuts=(), held_as=jnp.bfloat16):
    array = jax.random.normal(own_key, dims, jnp.float32) * deviation
    if len(cuts) > 0:
        array = block_levels(own_key, dims, cuts, -0.22, 0.18) * array
    return jnp.clip(array, min=-most, max=most).astype(held_as)


def setup_inputs(seed: int = 0) -> dict:
    key_of = jax.random.split(jax.random.key(seed), 5)
    x_block = normal_values(key_of[0], (VECS, NX, NY, NZ), 1.0, 6.0, ((1, 8), (2, 8), (3, 4)), jnp.float32)
    p_block = normal_values(key_of[1], (VECS, NX, NY, NZ), 1.0, 6.0, ((1, 8), (2, 8), (3, 4)), jnp.float32)
    voxel_class = plant(jax.random.randint(key_of[2], (NX, NY, NZ), 0, CLASSES), jax.random.fold_in(key_of[2], 1), 0, CLASSES - 1).astype(jnp.int32)
    conductance = jnp.clip(jnp.exp(jax.random.uniform(key_of[3], (CLASSES,), jnp.float32, math.log(0.25), math.log(4.0))), 0.25, 4.0)
    return dict(x_block=x_block, p_block=p_block, voxel_class=voxel_class, conductance=conductance)


jacobi_weight = 2.0 / 3.0
mass_shift = 0.05

def matmul_high(first_side, second_side):
    return jnp.dot(first_side, second_side, precision=lax.Precision.HIGHEST)

def harmonic(one_side, other_side):
    return 2.0 * one_side * other_side / (one_side + other_side)

def fine_edges(padded):
    edge_x = harmonic(padded[:-1, 1:-1, 1:-1], padded[1:, 1:-1, 1:-1])
    edge_y = harmonic(padded[1:-1, :-1, 1:-1], padded[1:-1, 1:, 1:-1])
    edge_z = harmonic(padded[1:-1, 1:-1, :-1], padded[1:-1, 1:-1, 1:])
    return (edge_x, edge_y, edge_z)

def pair_sum(values, axis_index):
    old_shape = values.shape
    new_shape = old_shape[:axis_index] + (old_shape[axis_index] // 2, 2) + old_shape[axis_index + 1:]
    return lax.optimization_barrier(jnp.sum(values.reshape(new_shape), axis=axis_index + 1))

def coarsen_edges(edges):
    edge_x, edge_y, edge_z = edges
    coarse_x = pair_sum(pair_sum(edge_x[0::2], 1), 2)
    coarse_y = pair_sum(pair_sum(edge_y[:, 0::2], 0), 2)
    coarse_z = pair_sum(pair_sum(edge_z[:, :, 0::2], 0), 1)
    return (coarse_x, coarse_y, coarse_z)

def diagonal_of(edges, shift_term):
    edge_x, edge_y, edge_z = edges
    return shift_term + edge_x[:-1] + edge_x[1:] + edge_y[:, :-1] + edge_y[:, 1:] + edge_z[:, :, :-1] + edge_z[:, :, 1:]

def apply_operator(padded, field, edges, diagonal):
    edge_x, edge_y, edge_z = edges
    beside = edge_x[1:] * padded[:, 2:, 1:-1, 1:-1] + edge_x[:-1] * padded[:, :-2, 1:-1, 1:-1]
    beside = beside + edge_y[:, 1:] * padded[:, 1:-1, 2:, 1:-1] + edge_y[:, :-1] * padded[:, 1:-1, :-2, 1:-1]
    beside = beside + edge_z[:, :, 1:] * padded[:, 1:-1, 1:-1, 2:] + edge_z[:, :, :-1] * padded[:, 1:-1, 1:-1, :-2]
    return diagonal * field - beside

def smooth(residual, level_data, rim_fn):
    edges, diagonal = level_data
    first = jacobi_weight * residual / diagonal
    return first + jacobi_weight * (residual - apply_operator(rim_fn(first), first, edges, diagonal)) / diagonal

def restrict(field):
    return pair_sum(pair_sum(pair_sum(field, 1), 2), 3)

def prolong(field):
    channels, size_x, size_y, size_z = field.shape
    wide = jnp.broadcast_to(field[:, :, None, :, None, :, None], (channels, size_x, 2, size_y, 2, size_z, 2))
    return wide.reshape(channels, 2 * size_x, 2 * size_y, 2 * size_z)

def precondition(residual, levels, rims):
    middle_res = restrict(residual)
    coarse_res = restrict(middle_res)
    fine_part = smooth(residual, levels[0], rims[0])
    middle_part = smooth(middle_res, levels[1], rims[1])
    coarse_part = smooth(coarse_res, levels[2], rims[2])
    return fine_part + prolong(middle_part + prolong(coarse_part))

def solve_small(gram, cross):
    factor = jnp.linalg.cholesky(gram)
    partial_solve = jax.scipy.linalg.solve_triangular(factor, cross, lower=True)
    return jax.scipy.linalg.solve_triangular(factor, partial_solve, lower=True, trans='T')

def ritz_step(gram_b, gram_a, num_vecs, inner_steps):
    inverse_root = 1.0 / jnp.sqrt(jnp.diagonal(gram_b))
    outer_scale = inverse_root[:, None] * inverse_root[None, :]
    sym_a = 0.5 * (gram_a + gram_a.T)
    normed_b = 0.5 * (gram_b + gram_b.T) * outer_scale
    normed_a = sym_a * outer_scale
    factor_b = jnp.linalg.cholesky(normed_b)
    factor_a = jnp.linalg.cholesky(normed_a)
    sub_basis = jnp.eye(normed_b.shape[0], num_vecs, dtype=jnp.float32)
    for inner_step in range(inner_steps):
        lifted = matmul_high(factor_b, sub_basis)
        solved = jax.scipy.linalg.solve_triangular(factor_a, lifted, lower=True)
        solved = jax.scipy.linalg.solve_triangular(factor_a, solved, lower=True, trans='T')
        mapped = matmul_high(factor_b.T, solved)
        small_factor = jnp.linalg.cholesky(matmul_high(mapped.T, mapped))
        sub_basis = jax.scipy.linalg.solve_triangular(small_factor, mapped.T, lower=True).T
    coefficients = inverse_root[:, None] * jax.scipy.linalg.solve_triangular(factor_b, sub_basis, lower=True, trans='T')
    rayleigh = matmul_high(coefficients.T, matmul_high(sym_a, coefficients))
    return (coefficients, rayleigh)

def pad_field(field):
    return jnp.pad(field, ((0, 0), (1, 1), (1, 1), (1, 1)))

def reference(x_block, p_block, voxel_class, conductance):
    all_cells = NX * NY * NZ
    cond_pad = jnp.pad(conductance[voxel_class], 1)
    fine_edge = fine_edges(cond_pad)
    middle_edge = coarsen_edges(fine_edge)
    coarse_edge = coarsen_edges(middle_edge)
    levels = ((fine_edge, diagonal_of(fine_edge, mass_shift)), (middle_edge, diagonal_of(middle_edge, 8.0 * mass_shift)), (coarse_edge, diagonal_of(coarse_edge, 64.0 * mass_shift)))
    rims = (pad_field, pad_field, pad_field)
    block_x, block_p = (x_block, p_block)
    applied_x = apply_operator(pad_field(block_x), block_x, levels[0][0], levels[0][1])
    applied_p = apply_operator(pad_field(block_p), block_p, levels[0][0], levels[0][1])
    for iteration in range(ITERS):
        flat_x = block_x.reshape(VECS, -1)
        flat_ax = applied_x.reshape(VECS, -1)
        gram_x = matmul_high(flat_x, flat_x.T) / all_cells
        cross_x = matmul_high(flat_x, flat_ax.T) / all_cells
        projected = solve_small(gram_x, cross_x)
        residual = applied_x - matmul_high(projected.T, flat_x).reshape(block_x.shape)
        block_w = precondition(residual, levels, rims)
        applied_w = apply_operator(pad_field(block_w), block_w, levels[0][0], levels[0][1])
        search = jnp.concatenate([block_x, block_w, block_p], 0).reshape(3 * VECS, -1)
        applied = jnp.concatenate([applied_x, applied_w, applied_p], 0).reshape(3 * VECS, -1)
        gram_b = matmul_high(search, search.T) / all_cells
        gram_a = matmul_high(search, applied.T) / all_cells
        coefficients, rayleigh = ritz_step(gram_b, gram_a, VECS, INNER)
        tail = coefficients[VECS:]
        block_x = matmul_high(coefficients.T, search).reshape(block_x.shape)
        applied_x = matmul_high(coefficients.T, applied).reshape(block_x.shape)
        block_p = matmul_high(tail.T, search[VECS:]).reshape(block_x.shape)
        applied_p = matmul_high(tail.T, applied[VECS:]).reshape(block_x.shape)
    return (block_x, block_p)
```

```python
import jax
import jax.numpy as jnp
from jax import lax
from jax.sharding import PartitionSpec as P

VECS = 16
CLASSES = 8
ITERS = 2
INNER = 4


jacobi_weight = 2.0 / 3.0
mass_shift = 0.05


def with_halo(array, sides, width):
    for axis, dim in sides:
        peers, length = (lax.axis_size(axis), array.shape[dim])
        up = [(i, (i + 1) % peers) for i in range(peers - 1)]
        down = [(j, i) for i, j in up]
        last = lax.slice_in_dim(array, length - width, length, axis=dim)
        leading = lax.slice_in_dim(array, 0, width, axis=dim)
        before = lax.ppermute(last, axis, up)
        after = lax.ppermute(leading, axis, down)
        array = jnp.concatenate([before, array, after], axis=dim)
    return array


def matmul_high(first_side, second_side):
    return jnp.dot(first_side, second_side, precision=lax.Precision.HIGHEST)


def harmonic(one_side, other_side):
    return 2.0 * one_side * other_side / (one_side + other_side)


def fine_edges(padded):
    edge_x = harmonic(padded[:-1, 1:-1, 1:-1], padded[1:, 1:-1, 1:-1])
    edge_y = harmonic(padded[1:-1, :-1, 1:-1], padded[1:-1, 1:, 1:-1])
    edge_z = harmonic(padded[1:-1, 1:-1, :-1], padded[1:-1, 1:-1, 1:])
    return (edge_x, edge_y, edge_z)


def pair_sum(values, axis_index):
    old_shape = values.shape
    new_shape = (
        old_shape[:axis_index] + (old_shape[axis_index] // 2, 2) + old_shape[axis_index + 1 :]
    )
    return jnp.sum(values.reshape(new_shape), axis=axis_index + 1)


def coarsen_edges(edges):
    edge_x, edge_y, edge_z = edges
    coarse_x = pair_sum(pair_sum(edge_x[0::2], 1), 2)
    coarse_y = pair_sum(pair_sum(edge_y[:, 0::2], 0), 2)
    coarse_z = pair_sum(pair_sum(edge_z[:, :, 0::2], 0), 1)
    return (coarse_x, coarse_y, coarse_z)


def diagonal_of(edges, shift_term):
    edge_x, edge_y, edge_z = edges
    return (
        shift_term
        + edge_x[:-1]
        + edge_x[1:]
        + edge_y[:, :-1]
        + edge_y[:, 1:]
        + edge_z[:, :, :-1]
        + edge_z[:, :, 1:]
    )


def apply_operator(padded, field, edges, diagonal):
    edge_x, edge_y, edge_z = edges
    beside = edge_x[1:] * padded[:, 2:, 1:-1, 1:-1] + edge_x[:-1] * padded[:, :-2, 1:-1, 1:-1]
    beside = (
        beside
        + edge_y[:, 1:] * padded[:, 1:-1, 2:, 1:-1]
        + edge_y[:, :-1] * padded[:, 1:-1, :-2, 1:-1]
    )
    beside = (
        beside
        + edge_z[:, :, 1:] * padded[:, 1:-1, 1:-1, 2:]
        + edge_z[:, :, :-1] * padded[:, 1:-1, 1:-1, :-2]
    )
    return diagonal * field - beside


def smooth(residual, level_data, rim_fn):
    edges, diagonal = level_data
    first = jacobi_weight * residual / diagonal
    return (
        first
        + jacobi_weight
        * (residual - apply_operator(rim_fn(first), first, edges, diagonal))
        / diagonal
    )


def restrict(field):
    return pair_sum(pair_sum(pair_sum(field, 1), 2), 3)


def prolong(field):
    channels, size_x, size_y, size_z = field.shape
    wide = jnp.broadcast_to(
        field[:, :, None, :, None, :, None], (channels, size_x, 2, size_y, 2, size_z, 2)
    )
    return wide.reshape(channels, 2 * size_x, 2 * size_y, 2 * size_z)


def precondition(residual, levels, rims):
    middle_res = restrict(residual)
    coarse_res = restrict(middle_res)
    fine_part = smooth(residual, levels[0], rims[0])
    middle_part = smooth(middle_res, levels[1], rims[1])
    coarse_part = smooth(coarse_res, levels[2], rims[2])
    return fine_part + prolong(middle_part + prolong(coarse_part))


def solve_small(gram, cross):
    factor = jnp.linalg.cholesky(gram)
    partial_solve = jax.scipy.linalg.solve_triangular(factor, cross, lower=True)
    return jax.scipy.linalg.solve_triangular(factor, partial_solve, lower=True, trans="T")


def ritz_step(gram_b, gram_a, num_vecs, inner_steps):
    inverse_root = 1.0 / jnp.sqrt(jnp.diagonal(gram_b))
    outer_scale = inverse_root[:, None] * inverse_root[None, :]
    sym_a = 0.5 * (gram_a + gram_a.T)
    normed_b = 0.5 * (gram_b + gram_b.T) * outer_scale
    normed_a = sym_a * outer_scale
    factor_b = jnp.linalg.cholesky(normed_b)
    factor_a = jnp.linalg.cholesky(normed_a)
    sub_basis = jnp.eye(normed_b.shape[0], num_vecs, dtype=jnp.float32)
    for inner_step in range(inner_steps):
        lifted = matmul_high(factor_b, sub_basis)
        solved = jax.scipy.linalg.solve_triangular(factor_a, lifted, lower=True)
        solved = jax.scipy.linalg.solve_triangular(factor_a, solved, lower=True, trans="T")
        mapped = matmul_high(factor_b.T, solved)
        small_factor = jnp.linalg.cholesky(matmul_high(mapped.T, mapped))
        sub_basis = jax.scipy.linalg.solve_triangular(small_factor, mapped.T, lower=True).T
    coefficients = inverse_root[:, None] * jax.scipy.linalg.solve_triangular(
        factor_b, sub_basis, lower=True, trans="T"
    )
    rayleigh = matmul_high(coefficients.T, matmul_high(sym_a, coefficients))
    return (coefficients, rayleigh)


def fine_rim(field):
    return with_halo(field, (("gx", 1), ("gy", 2), ("gz", 3)), 1)


def middle_rim(field):
    return with_halo(field, (("gx", 1), ("gy", 2), ("gz", 3)), 1)


def coarse_rim(field):
    return with_halo(field, (("gx", 1), ("gy", 2), ("gz", 3)), 1)


def all_sum(values):
    for axis, bit in (
        ("gy", 1), ("gx", 1), ("gz", 1), ("gy", 2), ("gx", 2), ("gz", 2), ("gy", 4), ("gx", 4),
    ):
        peers = lax.axis_size(axis)
        values = values + lax.ppermute(values, axis, [(i, i ^ bit) for i in range(peers)])
    return values


def on_device(x_block, p_block, voxel_class, conductance):
    device_cells = x_block.shape[1] * x_block.shape[2] * x_block.shape[3]
    all_cells = device_cells * lax.axis_size("gx") * lax.axis_size("gy") * lax.axis_size("gz")
    local_cond = jnp.zeros(voxel_class.shape, jnp.float32)
    for class_index in range(CLASSES):
        local_cond = local_cond + jnp.where(
            voxel_class == class_index, conductance[class_index], 0.0
        )
    padded_first = fine_rim(jnp.concatenate([local_cond[None], x_block], 0))
    cond_pad = padded_first[0]
    x_pad = padded_first[1:]
    p_pad = fine_rim(p_block)
    fine_edge = fine_edges(cond_pad)
    middle_edge = coarsen_edges(fine_edge)
    coarse_edge = coarsen_edges(middle_edge)
    levels = (
        (fine_edge, diagonal_of(fine_edge, mass_shift)),
        (middle_edge, diagonal_of(middle_edge, 8.0 * mass_shift)),
        (coarse_edge, diagonal_of(coarse_edge, 64.0 * mass_shift)),
    )
    rims = (fine_rim, middle_rim, coarse_rim)
    block_x, block_p = (x_block, p_block)
    applied_x = apply_operator(x_pad, block_x, levels[0][0], levels[0][1])
    applied_p = apply_operator(p_pad, block_p, levels[0][0], levels[0][1])
    for iteration in range(ITERS):
        flat_x = block_x.reshape(VECS, -1)
        flat_ax = applied_x.reshape(VECS, -1)
        if iteration == 0:
            pair = jnp.concatenate([matmul_high(flat_x, flat_x.T), matmul_high(flat_x, flat_ax.T)], 0)
            pair = all_sum(pair.reshape(4, 128)).reshape(2 * VECS, VECS) / all_cells
            gram_x, cross_x = pair[:VECS], pair[VECS:]
        else:
            gram_x = matmul_high(coefficients.T, matmul_high(gram_b, coefficients))
            cross_x = matmul_high(coefficients.T, matmul_high(gram_a, coefficients))
        projected = solve_small(gram_x, cross_x)
        residual = applied_x - matmul_high(projected.T, flat_x).reshape(block_x.shape)
        block_w = precondition(residual, levels, rims)
        applied_w = apply_operator(fine_rim(block_w), block_w, levels[0][0], levels[0][1])
        search = jnp.concatenate([block_x, block_w, block_p], 0).reshape(3 * VECS, -1)
        applied = jnp.concatenate([applied_x, applied_w, applied_p], 0).reshape(3 * VECS, -1)
        pair = jnp.concatenate([matmul_high(search, search.T), matmul_high(search, applied.T)], 0)
        pair = all_sum(pair.reshape(36, 128)).reshape(6 * VECS, 3 * VECS) / all_cells
        gram_b, gram_a = pair[: 3 * VECS], pair[3 * VECS :]
        coefficients, rayleigh = ritz_step(gram_b, gram_a, VECS, INNER)
        tail = coefficients[VECS:]
        block_x = matmul_high(coefficients.T, search).reshape(x_block.shape)
        applied_x = matmul_high(coefficients.T, applied).reshape(x_block.shape)
        block_p = matmul_high(tail.T, search[VECS:]).reshape(x_block.shape)
        applied_p = matmul_high(tail.T, applied[VECS:]).reshape(x_block.shape)
    return (block_x, block_p)


def solution(mesh):
    in_specs = (P(None, "gx", "gy", "gz"), P(None, "gx", "gy", "gz"), P("gx", "gy", "gz"), P())
    out_specs = (P(None, "gx", "gy", "gz"), P(None, "gx", "gy", "gz"))
    return jax.shard_map(
        on_device, mesh=mesh, in_specs=in_specs, out_specs=out_specs, check_vma=False
    )
```

```python
import jax
import jax.numpy as jnp
from jax import lax
from jax.experimental import pallas as pl
from jax.experimental.pallas import tpu as pltpu
from jax.sharding import PartitionSpec as P

VECS = 16
CLASSES = 8
ITERS = 2
INNER = 4
INTERPRET = False

jacobi_weight = 2.0 / 3.0
mass_shift = 0.05

LX, LY, LANES = 8, 4, 128
MX, MY = LX // 2, LY // 2
CX, CY = LX // 4, LY // 4
FINE, MIDDLE, COARSE = LX * LY, MX * MY, CX * CY
SHAPE = jax.ShapeDtypeStruct
F32 = jnp.float32
HALF = LANES // 2


def tile(ref, index, rows=slice(None)):
    return ref[rows, index * LANES : (index + 1) * LANES]


def lanes_of(rows=8):
    return lax.broadcasted_iota(jnp.int32, (rows, LANES), 1)


def rows_of(rows):
    return lax.broadcasted_iota(jnp.int32, (rows, LANES), 0)


def turn(value, shift):
    shift = shift % LANES
    return value if shift == 0 else pltpu.roll(value, shift, 1)


def dot(left, right, contract=(1, 0)):
    return lax.dot_general(
        left,
        right,
        (((contract[0],), (contract[1],)), ((), ())),
        precision=lax.Precision.HIGHEST,
        preferred_element_type=F32,
    )


def pair_matrix(transposed):
    wide = lax.broadcasted_iota(jnp.int32, (LANES, LANES), 1 if transposed else 0)
    narrow = lax.broadcasted_iota(jnp.int32, (LANES, LANES), 0 if transposed else 1)
    return jnp.where(wide // 2 == narrow, 1.0, 0.0).astype(F32)


def stack(values):
    return jnp.concatenate(values, axis=0)


def run(body, outs, vmem, smem=()):
    in_specs = [pl.BlockSpec(memory_space=pltpu.SMEM)] * len(smem)
    in_specs += [pl.BlockSpec(memory_space=pltpu.VMEM)] * len(vmem)
    return pl.pallas_call(
        body,
        out_shape=[SHAPE(shape, F32) for shape in outs],
        in_specs=in_specs,
        out_specs=[pl.BlockSpec(memory_space=pltpu.VMEM)] * len(outs),
        interpret=INTERPRET,
    )(*smem, *vmem)


def start_kernel(cond_ref, x_ref, p_ref, class_ref, field_ref, zr, zl, yu, yd, xu, xd):
    classes = class_ref[...]
    local = jnp.zeros(classes.shape, F32)
    for index in range(CLASSES):
        local = local + jnp.where(classes == index, cond_ref[index], 0.0)
    lane = lanes_of(40)
    right = jnp.zeros((40, LANES), F32)
    left = jnp.zeros((40, LANES), F32)
    for x in range(LX):
        for y in range(LY):
            p = x * LY + y
            cell = stack(
                [
                    x_ref[pl.ds(p, VECS, stride=FINE), :],
                    p_ref[pl.ds(p, VECS, stride=FINE), :],
                    jnp.broadcast_to(local[p : p + 1], (8, LANES)),
                ]
            )
            field_ref[:, p * LANES : (p + 1) * LANES] = cell
            right = jnp.where(lane == p, turn(cell, p + 1), right)
            left = jnp.where(lane == p, turn(cell, p), left)
            if y == LY - 1:
                yu[:, x * LANES : (x + 1) * LANES] = cell
            if y == 0:
                yd[:, x * LANES : (x + 1) * LANES] = cell
            if x == LX - 1:
                xu[:, y * LANES : (y + 1) * LANES] = cell
            if x == 0:
                xd[:, y * LANES : (y + 1) * LANES] = cell
    zr[...] = right
    zl[...] = left


def finish_weights(weights, shift_term):
    row = rows_of(8)
    weights = jnp.where(row < 6, weights, 0.0)
    diagonal = shift_term + jnp.sum(weights, axis=0, keepdims=True)
    return jnp.where(
        row < 6, weights, jnp.where(row == 6, diagonal, jacobi_weight / diagonal)
    )


def coarsen_weights(fine, size_x, size_y, shift_term, halve):
    row, lane = rows_of(8), lanes_of(8)
    sums = []
    for x in range(size_x):
        for y in range(size_y):
            total = jnp.zeros((8, LANES), F32)
            for i in range(2):
                for j in range(2):
                    keep = (row == i) | (row == 2 + j)
                    keep = keep | ((row == 4) & (lane % 2 == 0)) | ((row == 5) & (lane % 2 == 1))
                    total = total + jnp.where(keep, fine[2 * x + i, 2 * y + j], 0.0)
            sums.append(total)
    paired = dot(stack(sums), halve)
    return {
        (k // size_y, k % size_y): finish_weights(paired[8 * k : 8 * k + 8], shift_term)
        for k in range(size_x * size_y)
    }


def first_kernel(flag_ref, field_ref, zr, zl, yu, yd, xu, xd, xp_ref, axp_ref, cf, cm, cc, gram):
    lane, row = lanes_of(8), rows_of(8)
    lane40 = lanes_of(40)
    from_low, from_high = zr[...], zl[...]
    flags = [flag_ref[k] for k in range(6)]
    ends = jnp.where((row == 4) & (lane == 0), flags[4], 1.0)
    ends = jnp.where((row == 5) & (lane == LANES - 1), flags[5], ends)
    fine = {}
    for x in range(LX):
        for y in range(LY):
            p = x * LY + y
            here = tile(field_ref, p)
            beside = [
                tile(field_ref, p - LY) if x > 0 else tile(xu, y),
                tile(field_ref, p + LY) if x < LX - 1 else tile(xd, y),
                tile(field_ref, p - 1) if y > 0 else tile(yu, x),
                tile(field_ref, p + 1) if y < LY - 1 else tile(yd, x),
                jnp.where(lane40 == 0, turn(from_low, -p), turn(here, 1)),
                jnp.where(lane40 == LANES - 1, turn(from_high, LANES - 1 - p), turn(here, -1)),
            ]
            around = stack([value[32:33] for value in beside] + [here[32:34]])
            own = here[32:40]
            keep = ends
            for side, at_end in enumerate((x == 0, x == LX - 1, y == 0, y == LY - 1)):
                if at_end:
                    keep = jnp.where(row == side, flags[side], keep)
            weights = finish_weights(2.0 * around * own / (around + own) * keep, mass_shift)
            fine[x, y] = weights
            cf[:, p * LANES : (p + 1) * LANES] = weights
            applied = weights[6:7] * here[:32]
            for side in range(6):
                applied = applied - weights[side : side + 1] * beside[side][:32]
            xp_ref[:, p * LANES : (p + 1) * LANES] = here[:32]
            axp_ref[:, p * LANES : (p + 1) * LANES] = applied
    halve = pair_matrix(False)
    middle = coarsen_weights(fine, MX, MY, 8.0 * mass_shift, halve)
    for (x, y), value in middle.items():
        k = x * MY + y
        cm[:, k * LANES : (k + 1) * LANES] = value
    coarse = coarsen_weights(middle, CX, CY, 64.0 * mass_shift, halve)
    for (x, y), value in coarse.items():
        cc[:, x * LANES : (x + 1) * LANES] = value
    flat_x = xp_ref[:VECS]
    other = stack([flat_x, axp_ref[:VECS]])
    pair = dot(flat_x, other, (1, 1))
    gram[...] = jnp.concatenate(
        [pair, jnp.zeros((VECS, LANES - 2 * VECS), F32)], axis=1
    )


def eliminate(rows, size, full):
    tiles = [rows[8 * i : 8 * i + 8] for i in range(rows.shape[0] // 8)]
    row = rows_of(8)
    for k in range(size):
        at, sub = divmod(k, 8)
        pivot_row = tiles[at][sub : sub + 1]
        scaled = pivot_row * (1.0 / pivot_row[:, k : k + 1])
        for i in range(len(tiles)):
            if i < at and not full:
                continue
            factor = tiles[i][:, k : k + 1]
            changed = tiles[i] - factor * scaled
            if i == at:
                keep = row == sub if full else row <= sub
                tiles[i] = jnp.where(keep, tiles[i], changed)
            else:
                tiles[i] = changed
    return stack(tiles)


def diagonal_column(matrix, rows):
    masked = jnp.where(lanes_of(rows) == rows_of(rows), matrix, 0.0)
    return jnp.sum(masked, axis=1, keepdims=True)


def lower_pad(matrix):
    missing = LANES - matrix.shape[0]
    return stack([matrix, jnp.zeros((missing, LANES), F32)])


def solve_projected(gram, cross):
    lane = lanes_of(VECS)
    both = jnp.where(lane < HALF, gram, turn(cross, HALF))
    done = eliminate(both, VECS, True)
    return turn(done, HALF) * (1.0 / diagonal_column(done, VECS))


def ritz(summed):
    size = 3 * VECS
    lane, row = lanes_of(size), rows_of(size)
    flipped = lower_pad(summed).T
    sym_b = jnp.where(lane < size, 0.5 * (summed + flipped[:size]), 0.0)
    sym_a = 0.5 * (turn(summed, HALF) + flipped[HALF : HALF + size])
    sym_a = jnp.where(lane < size, sym_a, 0.0)
    on_diagonal = jnp.where(lane == row, sym_b, 0.0)
    column = 1.0 / jnp.sqrt(jnp.sum(on_diagonal, axis=1, keepdims=True))
    across = jnp.sum(on_diagonal, axis=0, keepdims=True)
    across = jnp.where(lanes_of(1) < size, 1.0 / jnp.sqrt(across), 0.0)
    normed_b = sym_b * column * across
    normed_a = sym_a * column * across
    done = eliminate(jnp.where(lane < HALF, normed_a, turn(normed_b, HALF)), size, True)
    step = turn(done, HALF) * (1.0 / diagonal_column(done, size))
    step = jnp.where(lane < size, step, 0.0)
    weighed = dot(normed_b[:, :size], step)
    step_pad, weighed_pad = lower_pad(step), lower_pad(weighed)
    step_flipped, weighed_flipped = step_pad.T, weighed_pad.T
    short_lane = lanes_of(VECS)
    basis = None
    for inner_step in range(INNER):
        if basis is None:
            mapped, product = step_flipped[:VECS], weighed_flipped[:VECS]
        else:
            mapped = dot(basis, step_pad, (1, 1))
            product = dot(basis, weighed_pad, (1, 1))
        square = dot(product, lower_pad(mapped), (1, 1))
        done = eliminate(jnp.where(short_lane < HALF, square, turn(mapped, HALF)), VECS, False)
        basis = turn(done, HALF) * (1.0 / jnp.sqrt(diagonal_column(done, VECS)))
        basis = jnp.where(short_lane < size, basis, 0.0)
    gram = dot(dot(basis, lower_pad(normed_b), (1, 1)), lower_pad(basis), (1, 1))
    cross = dot(dot(basis, lower_pad(normed_a), (1, 1)), lower_pad(basis), (1, 1))
    return basis * across, gram, cross


def level_parts(x, applied, projected, cf, cm, cc, ef, em, ec):
    small = projected[:, :VECS]
    residual = applied - dot(small, x, (0, 0))
    halve = pair_matrix(False)
    sums = []
    for mx in range(MX):
        for my in range(MY):
            total = jnp.zeros((VECS, LANES), F32)
            for i in range(2):
                for j in range(2):
                    p = (2 * mx + i) * LY + 2 * my + j
                    part = residual[:, p * LANES : (p + 1) * LANES]
                    total = total + part
                    ef[:, p * LANES : (p + 1) * LANES] = part * tile(cf, p, slice(7, 8))
            sums.append(total)
    paired = dot(stack(sums), halve)
    middle = [paired[VECS * k : VECS * (k + 1)] for k in range(MIDDLE)]
    for k in range(MIDDLE):
        em[:, k * LANES : (k + 1) * LANES] = middle[k] * tile(cm, k, slice(7, 8))
    sums = []
    for cx in range(CX):
        sums.append(sum(middle[(2 * cx + i) * MY + j] for i in range(2) for j in range(2)))
    paired = dot(stack(sums), halve)
    for k in range(COARSE):
        coarse = paired[VECS * k : VECS * (k + 1)]
        ec[:, k * LANES : (k + 1) * LANES] = coarse * tile(cc, k, slice(7, 8))


def pack_z(ef, em, ec, cf, cm, cc, zr, zl):
    rows = zr.shape[0]
    lane = lanes_of(rows)

    def cell(values, weights, k):
        here = tile(values, k)
        return stack([here, tile(weights, k)]) if rows > VECS else here

    right = jnp.zeros((rows, LANES), F32)
    left = jnp.zeros((rows, LANES), F32)
    levels = ((ef, cf, FINE, 0, 126), (em, cm, MIDDLE, 64, 62), (ec, cc, COARSE, 80, 30))
    for values, weights, count, base, last in levels:
        for k in range(count):
            here = cell(values, weights, k)
            spot = base + 2 * k
            right = jnp.where(lane // 2 == spot // 2, turn(here, spot - last), right)
            left = jnp.where(lane // 2 == spot // 2, turn(here, spot), left)
    zr[...] = right
    zl[...] = left


def second_kernel(summed, xp_ref, axp_ref, cf, cm, cc, ef, em, ec, zr, zl):
    pair = summed[...]
    lane = lanes_of(VECS)
    gram = jnp.where(lane < VECS, pair, 0.0)
    cross = jnp.where(lane < VECS, turn(pair, -VECS), 0.0)
    projected = solve_projected(gram, cross)
    level_parts(xp_ref[:VECS], axp_ref[:VECS], projected, cf, cm, cc, ef, em, ec)
    pack_z(ef, em, ec, cf, cm, cc, zr, zl)


class Level:
    def __init__(self, own, low, high, rows, yu=None, yd=None, xu=None, xd=None, y2u=None, y2d=None):
        self.own, self.rows = own, rows
        self.low, self.high = low[rows], high[rows]
        self.yu, self.yd, self.xu, self.xd, self.y2u, self.y2d = yu, yd, xu, xd, y2u, y2d
        count = rows.stop - rows.start
        self.count, self.lane = count, lanes_of(count)
        self.kept = {}

    def once(self, key, make):
        if key not in self.kept:
            self.kept[key] = make()
        return self.kept[key]

    def own_rows(self, ref, k):
        if isinstance(ref, tuple):
            return stack([tile(part, k) for part in ref])
        return tile(ref, k)

    def fine(self, x, y):
        if 0 <= x < LX and 0 <= y < LY:
            return self.own_rows(self.own[0], x * LY + y)
        if 0 <= x < LX:
            return tile(self.yu, 2 * x + y + 2, self.rows) if y < 0 else tile(self.yd, 2 * x + y - LY, self.rows)
        ref, near = (self.xu, x == -1) if x < 0 else (self.xd, x == LX)
        return tile(ref, y + 1 if near else 6 + y, self.rows)

    def fine_end(self, x, y):
        def make():
            if 0 <= x < LX and 0 <= y < LY:
                p = x * LY + y
                return jnp.where(
                    self.lane < HALF, turn(self.high, -2 * p), turn(self.low, 126 - 2 * p)
                )
            if 0 <= x < LX:
                return turn(tile(self.yu if y < 0 else self.yd, 16, self.rows), -(1 + 2 * x))
            return turn(tile(self.xu if x < 0 else self.xd, 10, self.rows), -(1 + 2 * y))

        return self.once(("end", x, y), make)

    def middle(self, x, y):
        def make():
            if 0 <= x < MX and 0 <= y < MY:
                k = x * MY + y
                beyond = jnp.where(
                    self.lane < 96, turn(self.high, -2 * k), turn(self.low, 62 - 2 * k)
                )
                return jnp.where(self.lane < 64, self.own_rows(self.own[1], k), beyond)
            if 0 <= x < MX:
                return tile(self.yu, 17 + MY * x + y + MY, self.rows) if y < 0 else tile(
                    self.yd, 17 + MY * x + y - MY, self.rows
                )
            ref, near = (self.xu, x == -1) if x < 0 else (self.xd, x == MX)
            return tile(ref, 12 + y if near else 15 + y, self.rows)

        return self.once(("middle", x, y), make)

    def coarse(self, x, y):
        def make():
            if 0 <= x < CX and y == 0:
                beyond = jnp.where(
                    self.lane < 64, turn(self.high, -48 - 2 * x), turn(self.low, 46 - 2 * x)
                )
                return jnp.where(self.lane < 32, self.own_rows(self.own[2], x), beyond)
            if 0 <= x < CX:
                if abs(y) == 2:
                    return tile(self.y2u if y < 0 else self.y2d, x)
                return tile(self.yu if y < 0 else self.yd, 25 + x, self.rows)
            ref, near = (self.xu, x == -1) if x < 0 else (self.xd, x == CX)
            return tile(ref, 18 + y if near else 20, self.rows)

        return self.once(("coarse", x, y), make)


def put(ref, index, value):
    ref[:, index * LANES : (index + 1) * LANES] = value


def pack_ends(values):
    rows = values[0].shape[0]
    lane = lanes_of(rows)
    packed = jnp.zeros((rows, LANES), F32)
    for k, value in enumerate(values):
        packed = jnp.where(lane // 2 == k, turn(value, 1 + 2 * k), packed)
    return packed


def owns(refs, rows):
    ef, em, ec, cf, cm, cc = refs
    return ((ef, cf), (em, cm), (ec, cc)) if rows > VECS else (ef, em, ec)


def pack_y_kernel(ef, em, ec, cf, cm, cc, zr, zl, yu, yd):
    rows = zr.shape[0]
    level = Level(owns((ef, em, ec, cf, cm, cc), rows), zr, zl, slice(0, rows))
    for ref, first, edge in ((yu, LY - 2, LY - 1), (yd, 0, 0)):
        for x in range(LX):
            for j in range(2):
                put(ref, 2 * x + j, level.fine(x, first + j))
        put(ref, 16, pack_ends([level.fine_end(x, edge) for x in range(LX)]))
        for x in range(MX):
            for y in range(MY):
                put(ref, 17 + MY * x + y, level.middle(x, y))
        for x in range(CX):
            put(ref, 25 + x, level.coarse(x, 0))


def pack_x_kernel(ef, em, ec, cf, cm, cc, zr, zl, ryu, ryd, xu, xd):
    rows = zr.shape[0]
    level = Level(owns((ef, em, ec, cf, cm, cc), rows), zr, zl, slice(0, rows), ryu, ryd)
    for ref, up in ((xu, True), (xd, False)):
        near, far = (LX - 1, LX - 2) if up else (0, 1)
        for y in range(-1, LY + 1):
            put(ref, y + 1, level.fine(near, y))
        for y in range(LY):
            put(ref, 6 + y, level.fine(far, y))
        put(ref, 10, pack_ends([level.fine_end(near, y) for y in range(LY)]))
        near, far = (MX - 1, MX - 2) if up else (0, 1)
        for y in range(-1, MY + 1):
            put(ref, 12 + y, level.middle(near, y))
        for y in range(MY):
            put(ref, 15 + y, level.middle(far, y))
        near, far = (CX - 1, CX - 2) if up else (0, 1)
        for y in range(-1, 2):
            put(ref, 18 + y, level.coarse(near, y))
        put(ref, 20, level.coarse(far, 0))


def faces(size_x, size_y):
    own = [(x, y) for x in range(size_x) for y in range(size_y)]
    beyond = [(x, y) for x in (-1, size_x) for y in range(size_y)]
    beyond += [(x, y) for x in range(size_x) for y in (-1, size_y)]
    return own, beyond


def neighbours(x, y):
    return ((x - 1, y), (x + 1, y), (x, y - 1), (x, y + 1))


def spread(weights, values):
    total = weights[0:1] * values[0]
    for side in range(1, 6):
        total = total + weights[side : side + 1] * values[side]
    return total


def smooth_tile(weights, here, values):
    return (2.0 * jacobi_weight) * here + weights[7:8] * spread(weights, values)


def search_kernel(
    xp_ref, axp_ref, ef, em, ec, cf, cm, cc,
    zr, zl, yu, yd, xu, xd, y2u, y2d,
    wzr, wzl, wyu, wyd, wxu, wxd,
    wa_ref, gram, basis_ref,
):
    values = Level((ef, em, ec), zr, zl, slice(0, VECS), yu, yd, xu, xd, y2u, y2d)
    weights = Level((cf, cm, cc), wzr, wzl, slice(VECS, VECS + 8), wyu, wyd, wxu, wxd)
    lane = lanes_of(VECS)
    double = pair_matrix(True)

    own, beyond = faces(CX, CY)
    coarse_cells = own + beyond
    smoothed = []
    for cell in coarse_cells:
        here = values.coarse(*cell)
        around = [values.coarse(*other) for other in neighbours(*cell)]
        around += [turn(here, 1), turn(here, -1)]
        smoothed.append(smooth_tile(weights.coarse(*cell), here, around))
    doubled = dot(stack(smoothed), double)
    to_middle = {}
    for k, cell in enumerate(coarse_cells):
        ends = jnp.where(lane < 96, turn(smoothed[k], 32), smoothed[k])
        inner = doubled[VECS * k : VECS * (k + 1)]
        to_middle[cell] = jnp.where(lane < 64, inner, ends)

    own, beyond = faces(MX, MY)
    middle_cells = own + beyond
    smoothed = []
    for cell in middle_cells:
        here = values.middle(*cell)
        around = [values.middle(*other) for other in neighbours(*cell)]
        around += [turn(here, 1), turn(here, -1)]
        part = smooth_tile(weights.middle(*cell), here, around)
        smoothed.append(part + to_middle[cell[0] // 2, cell[1] // 2])
    doubled = dot(stack(smoothed), double)
    to_fine, to_end = {}, {}
    for k, cell in enumerate(middle_cells):
        to_fine[cell] = doubled[VECS * k : VECS * (k + 1)]
        to_end[cell] = jnp.where(lane < HALF, turn(smoothed[k], 64), smoothed[k])

    def zs(main, end):
        low = jnp.where(lane > 0, turn(main, 1), turn(end, 1))
        high = jnp.where(lane < LANES - 1, turn(main, -1), turn(end, -1))
        return [low, high]

    own, beyond = faces(LX, LY)
    found, found_end = {}, {}
    for cell in beyond + own:
        here, end = values.fine(*cell), values.fine_end(*cell)
        around = [values.fine(*other) for other in neighbours(*cell)] + zs(here, end)
        part = smooth_tile(weights.fine(*cell), here, around)
        found[cell] = part + to_fine[cell[0] // 2, cell[1] // 2]
    for cell in own:
        here, end = values.fine(*cell), values.fine_end(*cell)
        around = [values.fine_end(*other) for other in neighbours(*cell)] + zs(end, here)
        part = smooth_tile(weights.fine_end(*cell), end, around)
        found_end[cell] = part + to_end[cell[0] // 2, cell[1] // 2]
    basis_ref[: 2 * VECS] = xp_ref[...]
    basis_ref[3 * VECS : 4 * VECS] = jnp.zeros((VECS, FINE * LANES), F32)
    basis_ref[4 * VECS : 6 * VECS] = axp_ref[...]
    for cell in own:
        k = cell[0] * LY + cell[1]
        here = found[cell]
        factors = tile(cf, k)
        around = [found[other] for other in neighbours(*cell)] + zs(here, found_end[cell])
        applied = factors[6:7] * here - spread(factors, around)
        columns = slice(k * LANES, (k + 1) * LANES)
        wa_ref[:VECS, columns] = here
        wa_ref[VECS:, columns] = applied
        basis_ref[2 * VECS : 3 * VECS, columns] = here
        basis_ref[6 * VECS : 7 * VECS, columns] = applied
    pair = dot(basis_ref[: 3 * VECS], basis_ref[...], (1, 1))
    gram[...] = jnp.concatenate([pair, jnp.zeros((3 * VECS, VECS), F32)], axis=1)


def combine(coefficients, xp_ref, wa_ref, axp_ref):
    lane = lanes_of(VECS)
    both = stack([coefficients, jnp.where(lane >= VECS, coefficients, 0.0)])[:, : 3 * VECS]
    search = stack([xp_ref[...], wa_ref[:VECS]])
    moved = dot(both, search)
    if axp_ref is None:
        return moved, None
    applied = stack([axp_ref[...], wa_ref[VECS:]])
    return moved, dot(both, applied)


def third_kernel(summed, xp_ref, axp_ref, wa_ref, cf, cm, cc, nxp, naxp, ef, em, ec, zr, zl):
    coefficients, gram, cross = ritz(summed[...])
    moved, applied = combine(coefficients, xp_ref, wa_ref, axp_ref)
    nxp[...] = moved
    naxp[...] = applied
    projected = solve_projected(gram, cross)
    level_parts(moved[:VECS], applied[:VECS], projected, cf, cm, cc, ef, em, ec)
    pack_z(ef, em, ec, cf, cm, cc, zr, zl)


def last_kernel(summed, xp_ref, wa_ref, x_out, p_out):
    coefficients, _, _ = ritz(summed[...])
    moved, _ = combine(coefficients, xp_ref, wa_ref, None)
    for k in range(FINE):
        columns = slice(k * LANES, (k + 1) * LANES)
        x_out[pl.ds(k, VECS, stride=FINE), :] = moved[:VECS, columns]
        p_out[pl.ds(k, VECS, stride=FINE), :] = moved[VECS:, columns]


def shifted(values, axis, by):
    peers = lax.axis_size(axis)
    return lax.ppermute(values, axis, [(i, (i + by) % peers) for i in range(peers)])


def all_sum(values):
    bit = 1
    while bit < max(lax.axis_size(axis) for axis in ("gy", "gx", "gz")):
        for axis in ("gy", "gx", "gz"):
            peers = lax.axis_size(axis)
            if bit < peers:
                values = values + lax.ppermute(values, axis, [(i, i ^ bit) for i in range(peers)])
        bit *= 2
    return values


def exchange(parts, weights, zr, zl):
    rows = zr.shape[0]
    ec = parts[2]
    zr, zl = shifted(zr, "gz", 1), shifted(zl, "gz", -1)
    y2u, y2d = shifted(ec, "gy", 2), shifted(ec, "gy", -2)
    yu, yd = run(pack_y_kernel, [(rows, 27 * LANES)] * 2, (*parts, *weights, zr, zl))
    yu, yd = shifted(yu, "gy", 1), shifted(yd, "gy", -1)
    xu, xd = run(pack_x_kernel, [(rows, 21 * LANES)] * 2, (*parts, *weights, zr, zl, yu, yd))
    xu, xd = shifted(xu, "gx", 1), shifted(xd, "gx", -1)
    return (zr, zl, yu, yd, xu, xd), (y2u, y2d)


def on_device(x_block, p_block, voxel_class, conductance):
    sizes = [lax.axis_size(axis) for axis in ("gx", "gy", "gz")]
    all_cells = FINE * LANES * sizes[0] * sizes[1] * sizes[2]
    wide = FINE * LANES
    flags = []
    for axis, size in zip(("gx", "gy", "gz"), sizes):
        at = lax.axis_index(axis)
        flags += [at > 0, at < size - 1]
    flags = jnp.stack(flags).astype(F32)
    field, zr, zl, yu, yd, xu, xd = run(
        start_kernel,
        [(40, wide)] + [(40, LANES)] * 2 + [(40, LX * LANES)] * 2 + [(40, LY * LANES)] * 2,
        (
            x_block.reshape(VECS * FINE, LANES),
            p_block.reshape(VECS * FINE, LANES),
            voxel_class.reshape(FINE, LANES),
        ),
        (conductance,),
    )
    arrived = (
        shifted(zr, "gz", 1), shifted(zl, "gz", -1), shifted(yu, "gy", 1),
        shifted(yd, "gy", -1), shifted(xu, "gx", 1), shifted(xd, "gx", -1),
    )
    fields = [(2 * VECS, wide)] * 2
    weight_shapes = [(8, wide), (8, MIDDLE * LANES), (8, COARSE * LANES)]
    xp, axp, cf, cm, cc, gram = run(
        first_kernel, fields + weight_shapes + [(VECS, LANES)], (field, *arrived), (flags,)
    )
    weights = (cf, cm, cc)
    part_shapes = [(VECS, wide), (VECS, MIDDLE * LANES), (VECS, COARSE * LANES)]
    gram = all_sum(gram) * (1.0 / all_cells)
    rows = VECS + 8
    *parts, zr, zl = run(
        second_kernel, part_shapes + [(rows, LANES)] * 2, (gram, xp, axp, *weights)
    )
    sent_weights = None
    for iteration in range(ITERS):
        sent, far = exchange(parts, weights, zr, zl)
        if sent_weights is None:
            sent_weights = sent
        wa, gram = search(xp, axp, parts, weights, sent, far, sent_weights, wide)
        gram = all_sum(gram) * (1.0 / all_cells)
        if iteration < ITERS - 1:
            xp, axp, *parts, zr, zl = run(
                third_kernel,
                fields + part_shapes + [(VECS, LANES)] * 2,
                (gram, xp, axp, wa, *weights),
            )
    x_out, p_out = run(last_kernel, [(VECS * FINE, LANES)] * 2, (gram, xp, wa))
    return (x_out.reshape(x_block.shape), p_out.reshape(x_block.shape))


def search(xp, axp, parts, weights, sent, far, sent_weights, wide):
    inputs = (xp, axp, *parts, *weights, *sent, *far, *sent_weights)
    return pl.pallas_call(
        search_kernel,
        out_shape=[SHAPE((2 * VECS, wide), F32), SHAPE((3 * VECS, LANES), F32)],
        in_specs=[pl.BlockSpec(memory_space=pltpu.VMEM)] * len(inputs),
        out_specs=[pl.BlockSpec(memory_space=pltpu.VMEM)] * 2,
        scratch_shapes=[pltpu.VMEM((7 * VECS, wide), F32)],
        interpret=INTERPRET,
    )(*inputs)


def solution(mesh):
    in_specs = (P(None, "gx", "gy", "gz"), P(None, "gx", "gy", "gz"), P("gx", "gy", "gz"), P())
    out_specs = (P(None, "gx", "gy", "gz"), P(None, "gx", "gy", "gz"))
    return jax.shard_map(
        on_device, mesh=mesh, in_specs=in_specs, out_specs=out_specs, check_vma=False
    )
```

```python
import jax
import jax.numpy as jnp
from jax import lax
from jax.experimental import pallas as pl
from jax.experimental.pallas import tpu as pltpu
from jax.sharding import PartitionSpec as P

VECS = 16
CLASSES = 8
ITERS = 2
INNER = 4
INTERPRET = False
GRANT = 24 * 1024 * 1024

jacobi_weight = 2.0 / 3.0
mass_shift = 0.05

LX, LY, LANES = 8, 4, 128
MX, MY = LX // 2, LY // 2
CX, CY = LX // 4, LY // 4
FINE, MIDDLE, COARSE = LX * LY, MX * MY, CX * CY
SHAPE = jax.ShapeDtypeStruct
F32 = jnp.float32
HALF = LANES // 2


def tile(ref, index, rows=slice(None)):
    return ref[rows, index * LANES : (index + 1) * LANES]


def lanes_of(rows=8):
    return lax.broadcasted_iota(jnp.int32, (rows, LANES), 1)


def rows_of(rows):
    return lax.broadcasted_iota(jnp.int32, (rows, LANES), 0)


def turn(value, shift):
    shift = shift % LANES
    return value if shift == 0 else pltpu.roll(value, shift, 1)


def dot(left, right, contract=(1, 0)):
    return lax.dot_general(
        left,
        right,
        (((contract[0],), (contract[1],)), ((), ())),
        precision=lax.Precision.HIGHEST,
        preferred_element_type=F32,
    )


def pair_matrix(transposed):
    wide = lax.broadcasted_iota(jnp.int32, (LANES, LANES), 1 if transposed else 0)
    narrow = lax.broadcasted_iota(jnp.int32, (LANES, LANES), 0 if transposed else 1)
    return jnp.where(wide // 2 == narrow, 1.0, 0.0).astype(F32)


def stack(values):
    return jnp.concatenate(values, axis=0)


def run(body, outs, vmem, smem=()):
    in_specs = [pl.BlockSpec(memory_space=pltpu.SMEM)] * len(smem)
    in_specs += [pl.BlockSpec(memory_space=pltpu.VMEM)] * len(vmem)
    return pl.pallas_call(
        body,
        out_shape=[SHAPE(shape, F32) for shape in outs],
        in_specs=in_specs,
        out_specs=[pl.BlockSpec(memory_space=pltpu.VMEM)] * len(outs),
        compiler_params=pltpu.CompilerParams(vmem_limit_bytes=GRANT),
        interpret=INTERPRET,
    )(*smem, *vmem)


def start_kernel(cond_ref, x_ref, p_ref, class_ref, field_ref, zr, zl, yu, yd, xu, xd):
    classes = class_ref[...]
    local = jnp.zeros(classes.shape, F32)
    for index in range(CLASSES):
        local = local + jnp.where(classes == index, cond_ref[index], 0.0)
    lane = lanes_of(40)
    right = jnp.zeros((40, LANES), F32)
    left = jnp.zeros((40, LANES), F32)
    for x in range(LX):
        for y in range(LY):
            p = x * LY + y
            cell = stack(
                [
                    x_ref[pl.ds(p, VECS, stride=FINE), :],
                    p_ref[pl.ds(p, VECS, stride=FINE), :],
                    jnp.broadcast_to(local[p : p + 1], (8, LANES)),
                ]
            )
            field_ref[:, p * LANES : (p + 1) * LANES] = cell
            right = jnp.where(lane == p, turn(cell, p + 1), right)
            left = jnp.where(lane == p, turn(cell, p), left)
            if y == LY - 1:
                yu[:, x * LANES : (x + 1) * LANES] = cell
            if y == 0:
                yd[:, x * LANES : (x + 1) * LANES] = cell
            if x == LX - 1:
                xu[:, y * LANES : (y + 1) * LANES] = cell
            if x == 0:
                xd[:, y * LANES : (y + 1) * LANES] = cell
    zr[...] = right
    zl[...] = left


def finish_weights(weights, shift_term):
    row = rows_of(8)
    weights = jnp.where(row < 6, weights, 0.0)
    diagonal = shift_term + jnp.sum(weights, axis=0, keepdims=True)
    return jnp.where(
        row < 6, weights, jnp.where(row == 6, diagonal, jacobi_weight / diagonal)
    )


def coarsen_weights(fine, size_x, size_y, shift_term, halve):
    row, lane = rows_of(8), lanes_of(8)
    sums = []
    for x in range(size_x):
        for y in range(size_y):
            total = jnp.zeros((8, LANES), F32)
            for i in range(2):
                for j in range(2):
                    keep = (row == i) | (row == 2 + j)
                    keep = keep | ((row == 4) & (lane % 2 == 0)) | ((row == 5) & (lane % 2 == 1))
                    total = total + jnp.where(keep, fine[2 * x + i, 2 * y + j], 0.0)
            sums.append(total)
    paired = dot(stack(sums), halve)
    return {
        (k // size_y, k % size_y): finish_weights(paired[8 * k : 8 * k + 8], shift_term)
        for k in range(size_x * size_y)
    }


def first_kernel(flag_ref, field_ref, zr, zl, yu, yd, xu, xd, xp_ref, axp_ref, cf, cm, cc, gram):
    lane, row = lanes_of(8), rows_of(8)
    lane40 = lanes_of(40)
    from_low, from_high = zr[...], zl[...]
    flags = [flag_ref[k] for k in range(6)]
    ends = jnp.where((row == 4) & (lane == 0), flags[4], 1.0)
    ends = jnp.where((row == 5) & (lane == LANES - 1), flags[5], ends)
    fine = {}
    for x in range(LX):
        for y in range(LY):
            p = x * LY + y
            here = tile(field_ref, p)
            beside = [
                tile(field_ref, p - LY) if x > 0 else tile(xu, y),
                tile(field_ref, p + LY) if x < LX - 1 else tile(xd, y),
                tile(field_ref, p - 1) if y > 0 else tile(yu, x),
                tile(field_ref, p + 1) if y < LY - 1 else tile(yd, x),
                jnp.where(lane40 == 0, turn(from_low, -p), turn(here, 1)),
                jnp.where(lane40 == LANES - 1, turn(from_high, LANES - 1 - p), turn(here, -1)),
            ]
            around = stack([value[32:33] for value in beside] + [here[32:34]])
            own = here[32:40]
            keep = ends
            for side, at_end in enumerate((x == 0, x == LX - 1, y == 0, y == LY - 1)):
                if at_end:
                    keep = jnp.where(row == side, flags[side], keep)
            weights = finish_weights(2.0 * around * own / (around + own) * keep, mass_shift)
            fine[x, y] = weights
            cf[:, p * LANES : (p + 1) * LANES] = weights
            applied = weights[6:7] * here[:32]
            for side in range(6):
                applied = applied - weights[side : side + 1] * beside[side][:32]
            xp_ref[:, p * LANES : (p + 1) * LANES] = here[:32]
            axp_ref[:, p * LANES : (p + 1) * LANES] = applied
    halve = pair_matrix(False)
    middle = coarsen_weights(fine, MX, MY, 8.0 * mass_shift, halve)
    for (x, y), value in middle.items():
        k = x * MY + y
        cm[:, k * LANES : (k + 1) * LANES] = value
    coarse = coarsen_weights(middle, CX, CY, 64.0 * mass_shift, halve)
    for (x, y), value in coarse.items():
        cc[:, x * LANES : (x + 1) * LANES] = value
    flat_x = xp_ref[:VECS]
    other = stack([flat_x, axp_ref[:VECS]])
    pair = dot(flat_x, other, (1, 1))
    gram[...] = jnp.concatenate(
        [pair, jnp.zeros((VECS, LANES - 2 * VECS), F32)], axis=1
    )


def eliminate(rows, size, full):
    tiles = [rows[8 * i : 8 * i + 8] for i in range(rows.shape[0] // 8)]
    row = rows_of(8)
    kept = [tile_rows for tile_rows in tiles]
    for k in range(0, size, 2):
        at, sub = divmod(k, 8)
        first, second = tiles[at][sub : sub + 1], tiles[at][sub + 1 : sub + 2]
        a, b = first[:, k : k + 1], first[:, k + 1 : k + 2]
        c, d = second[:, k : k + 1], second[:, k + 1 : k + 2]
        inverse = 1.0 / (a * d - b * c)
        solved_first = (d * first - b * second) * inverse
        solved_second = (a * second - c * first) * inverse
        if not full:
            root = 1.0 / jnp.sqrt(a)
            kept_first = first * root
            kept_second = (a * second - c * first) * (root * jnp.sqrt(inverse))
            kept[at] = jnp.where(row == sub, kept_first, kept[at])
            kept[at] = jnp.where(row == sub + 1, kept_second, kept[at])
        for i in range(len(tiles)):
            if i < at and not full:
                continue
            left, right = tiles[i][:, k : k + 1], tiles[i][:, k + 1 : k + 2]
            changed = tiles[i] - (left * solved_first + right * solved_second)
            if i == at:
                changed = jnp.where(row == sub, solved_first, changed)
                changed = jnp.where(row == sub + 1, solved_second, changed)
            tiles[i] = changed
    return stack(tiles if full else kept)


def lower_pad(matrix):
    missing = LANES - matrix.shape[0]
    return stack([matrix, jnp.zeros((missing, LANES), F32)])


def solve_projected(gram, cross):
    lane = lanes_of(VECS)
    on_diagonal = jnp.where((lane == rows_of(VECS)) & (lane < VECS), gram, 0.0)
    column = 1.0 / jnp.sqrt(jnp.sum(on_diagonal, axis=1, keepdims=True))
    across = jnp.sum(on_diagonal, axis=0, keepdims=True)
    across = jnp.where(lanes_of(1) < VECS, 1.0 / jnp.sqrt(across), 0.0)
    both = jnp.where(lane < HALF, gram * across, turn(cross, HALF)) * column
    return turn(eliminate(both, VECS, True), HALF) * column


def ritz(summed):
    size = 3 * VECS
    lane, row = lanes_of(size), rows_of(size)
    flipped = lower_pad(summed).T
    sym_b = jnp.where(lane < size, 0.5 * (summed + flipped[:size]), 0.0)
    sym_a = 0.5 * (turn(summed, HALF) + flipped[HALF : HALF + size])
    sym_a = jnp.where(lane < size, sym_a, 0.0)
    on_diagonal = jnp.where(lane == row, sym_b, 0.0)
    column = 1.0 / jnp.sqrt(jnp.sum(on_diagonal, axis=1, keepdims=True))
    across = jnp.sum(on_diagonal, axis=0, keepdims=True)
    across = jnp.where(lanes_of(1) < size, 1.0 / jnp.sqrt(across), 0.0)
    normed_b = sym_b * column * across
    normed_a = sym_a * column * across
    done = eliminate(jnp.where(lane < HALF, normed_a, turn(normed_b, HALF)), size, True)
    step = jnp.where(lane < size, turn(done, HALF), 0.0)
    weighed = dot(normed_b[:, :size], step)
    step_pad, weighed_pad = lower_pad(step), lower_pad(weighed)
    step_flipped, weighed_flipped = step_pad.T, weighed_pad.T
    short_lane = lanes_of(VECS)
    basis = None
    for inner_step in range(INNER):
        if basis is None:
            mapped, product = step_flipped[:VECS], weighed_flipped[:VECS]
        else:
            mapped = dot(basis, step_pad, (1, 1))
            product = dot(basis, weighed_pad, (1, 1))
        square = dot(product, lower_pad(mapped), (1, 1))
        done = eliminate(jnp.where(short_lane < HALF, square, turn(mapped, HALF)), VECS, False)
        basis = jnp.where(short_lane < size, turn(done, HALF), 0.0)
    cross = dot(dot(basis, lower_pad(normed_a), (1, 1)), lower_pad(basis), (1, 1))
    return basis * across, cross


def level_parts(x, applied, projected, cf, cm, cc, ef, em, ec):
    small = projected[:, :VECS]
    residual = applied - dot(small, x, (0, 0))
    halve = pair_matrix(False)
    sums = []
    for mx in range(MX):
        for my in range(MY):
            total = jnp.zeros((VECS, LANES), F32)
            for i in range(2):
                for j in range(2):
                    p = (2 * mx + i) * LY + 2 * my + j
                    part = residual[:, p * LANES : (p + 1) * LANES]
                    total = total + part
                    ef[:, p * LANES : (p + 1) * LANES] = part * tile(cf, p, slice(7, 8))
            sums.append(total)
    paired = dot(stack(sums), halve)
    middle = [paired[VECS * k : VECS * (k + 1)] for k in range(MIDDLE)]
    for k in range(MIDDLE):
        em[:, k * LANES : (k + 1) * LANES] = middle[k] * tile(cm, k, slice(7, 8))
    sums = []
    for cx in range(CX):
        sums.append(sum(middle[(2 * cx + i) * MY + j] for i in range(2) for j in range(2)))
    paired = dot(stack(sums), halve)
    for k in range(COARSE):
        coarse = paired[VECS * k : VECS * (k + 1)]
        ec[:, k * LANES : (k + 1) * LANES] = coarse * tile(cc, k, slice(7, 8))


def pack_z(ef, em, ec, cf, cm, cc, zr, zl):
    rows = zr.shape[0]
    lane = lanes_of(rows)

    def cell(values, weights, k):
        here = tile(values, k)
        return stack([here, tile(weights, k)]) if rows > VECS else here

    right = jnp.zeros((rows, LANES), F32)
    left = jnp.zeros((rows, LANES), F32)
    levels = ((ef, cf, FINE, 0, 126), (em, cm, MIDDLE, 64, 62), (ec, cc, COARSE, 80, 30))
    for values, weights, count, base, last in levels:
        for k in range(count):
            here = cell(values, weights, k)
            spot = base + 2 * k
            right = jnp.where(lane // 2 == spot // 2, turn(here, spot - last), right)
            left = jnp.where(lane // 2 == spot // 2, turn(here, spot), left)
    zr[...] = right
    zl[...] = left


def second_kernel(summed, xp_ref, axp_ref, cf, cm, cc, ef, em, ec, zr, zl):
    pair = summed[...]
    lane = lanes_of(VECS)
    gram = jnp.where(lane < VECS, pair, 0.0)
    cross = jnp.where(lane < VECS, turn(pair, -VECS), 0.0)
    projected = solve_projected(gram, cross)
    level_parts(xp_ref[:VECS], axp_ref[:VECS], projected, cf, cm, cc, ef, em, ec)
    pack_z(ef, em, ec, cf, cm, cc, zr, zl)


class Level:
    def __init__(self, own, low, high, rows, yu=None, yd=None, xu=None, xd=None, y2u=None, y2d=None):
        self.own, self.rows = own, rows
        self.low, self.high = low[rows], high[rows]
        self.yu, self.yd, self.xu, self.xd, self.y2u, self.y2d = yu, yd, xu, xd, y2u, y2d
        count = rows.stop - rows.start
        self.count, self.lane = count, lanes_of(count)
        self.kept = {}

    def once(self, key, make):
        if key not in self.kept:
            self.kept[key] = make()
        return self.kept[key]

    def own_rows(self, ref, k):
        if isinstance(ref, tuple):
            return stack([tile(part, k) for part in ref])
        return tile(ref, k)

    def fine(self, x, y):
        if 0 <= x < LX and 0 <= y < LY:
            return self.own_rows(self.own[0], x * LY + y)
        if 0 <= x < LX:
            return tile(self.yu, 2 * x + y + 2, self.rows) if y < 0 else tile(self.yd, 2 * x + y - LY, self.rows)
        ref, near = (self.xu, x == -1) if x < 0 else (self.xd, x == LX)
        return tile(ref, y + 1 if near else 6 + y, self.rows)

    def fine_end(self, x, y):
        def make():
            if 0 <= x < LX and 0 <= y < LY:
                p = x * LY + y
                return jnp.where(
                    self.lane < HALF, turn(self.high, -2 * p), turn(self.low, 126 - 2 * p)
                )
            if 0 <= x < LX:
                return turn(tile(self.yu if y < 0 else self.yd, 16, self.rows), -(1 + 2 * x))
            return turn(tile(self.xu if x < 0 else self.xd, 10, self.rows), -(1 + 2 * y))

        return self.once(("end", x, y), make)

    def middle(self, x, y):
        def make():
            if 0 <= x < MX and 0 <= y < MY:
                k = x * MY + y
                beyond = jnp.where(
                    self.lane < 96, turn(self.high, -2 * k), turn(self.low, 62 - 2 * k)
                )
                return jnp.where(self.lane < 64, self.own_rows(self.own[1], k), beyond)
            if 0 <= x < MX:
                return tile(self.yu, 17 + MY * x + y + MY, self.rows) if y < 0 else tile(
                    self.yd, 17 + MY * x + y - MY, self.rows
                )
            ref, near = (self.xu, x == -1) if x < 0 else (self.xd, x == MX)
            return tile(ref, 12 + y if near else 15 + y, self.rows)

        return self.once(("middle", x, y), make)

    def coarse(self, x, y):
        def make():
            if 0 <= x < CX and y == 0:
                beyond = jnp.where(
                    self.lane < 64, turn(self.high, -48 - 2 * x), turn(self.low, 46 - 2 * x)
                )
                return jnp.where(self.lane < 32, self.own_rows(self.own[2], x), beyond)
            if 0 <= x < CX:
                if abs(y) == 2:
                    return tile(self.y2u if y < 0 else self.y2d, x)
                return tile(self.yu if y < 0 else self.yd, 25 + x, self.rows)
            ref, near = (self.xu, x == -1) if x < 0 else (self.xd, x == CX)
            return tile(ref, 18 + y if near else 20, self.rows)

        return self.once(("coarse", x, y), make)


def put(ref, index, value):
    ref[:, index * LANES : (index + 1) * LANES] = value


def pack_ends(values):
    rows = values[0].shape[0]
    lane = lanes_of(rows)
    packed = jnp.zeros((rows, LANES), F32)
    for k, value in enumerate(values):
        packed = jnp.where(lane // 2 == k, turn(value, 1 + 2 * k), packed)
    return packed


def owns(refs, rows):
    ef, em, ec, cf, cm, cc = refs
    return ((ef, cf), (em, cm), (ec, cc)) if rows > VECS else (ef, em, ec)


def pack_y_kernel(ef, em, ec, cf, cm, cc, zr, zl, yu, yd):
    rows = zr.shape[0]
    level = Level(owns((ef, em, ec, cf, cm, cc), rows), zr, zl, slice(0, rows))
    for ref, first, edge in ((yu, LY - 2, LY - 1), (yd, 0, 0)):
        for x in range(LX):
            for j in range(2):
                put(ref, 2 * x + j, level.fine(x, first + j))
        put(ref, 16, pack_ends([level.fine_end(x, edge) for x in range(LX)]))
        for x in range(MX):
            for y in range(MY):
                put(ref, 17 + MY * x + y, level.middle(x, y))
        for x in range(CX):
            put(ref, 25 + x, level.coarse(x, 0))


def pack_x_kernel(ef, em, ec, cf, cm, cc, zr, zl, ryu, ryd, y2u, y2d, xu, xd):
    rows = zr.shape[0]
    level = Level(owns((ef, em, ec, cf, cm, cc), rows), zr, zl, slice(0, rows), ryu, ryd)
    for ref, up in ((xu, True), (xd, False)):
        near, far = (LX - 1, LX - 2) if up else (0, 1)
        for y in range(-1, LY + 1):
            put(ref, y + 1, level.fine(near, y))
        for y in range(LY):
            put(ref, 6 + y, level.fine(far, y))
        put(ref, 10, pack_ends([level.fine_end(near, y) for y in range(LY)]))
        near, far = (MX - 1, MX - 2) if up else (0, 1)
        for y in range(-1, MY + 1):
            put(ref, 12 + y, level.middle(near, y))
        for y in range(MY):
            put(ref, 15 + y, level.middle(far, y))
        near, far = (CX - 1, CX - 2) if up else (0, 1)
        for y in range(-1, 2):
            put(ref, 18 + y, level.coarse(near, y))
        put(ref, 20, level.coarse(far, 0))


def faces(size_x, size_y):
    own = [(x, y) for x in range(size_x) for y in range(size_y)]
    beyond = [(x, y) for x in (-1, size_x) for y in range(size_y)]
    beyond += [(x, y) for x in range(size_x) for y in (-1, size_y)]
    return own, beyond


def neighbours(x, y):
    return ((x - 1, y), (x + 1, y), (x, y - 1), (x, y + 1))


def spread(weights, values):
    total = weights[0:1] * values[0]
    for side in range(1, 6):
        total = total + weights[side : side + 1] * values[side]
    return total


def smooth_tile(weights, here, values):
    return (2.0 * jacobi_weight) * here + weights[7:8] * spread(weights, values)


def search_kernel(
    xp_ref, axp_ref, ef, em, ec, cf, cm, cc,
    zr, zl, yu, yd, xu, xd, y2u, y2d,
    wzr, wzl, wyu, wyd, wxu, wxd,
    wa_ref, gram, basis_ref,
):
    values = Level((ef, em, ec), zr, zl, slice(0, VECS), yu, yd, xu, xd, y2u, y2d)
    weights = Level((cf, cm, cc), wzr, wzl, slice(VECS, VECS + 8), wyu, wyd, wxu, wxd)
    lane = lanes_of(VECS)
    double = pair_matrix(True)

    own, beyond = faces(CX, CY)
    coarse_cells = own + beyond
    smoothed = []
    for cell in coarse_cells:
        here = values.coarse(*cell)
        around = [values.coarse(*other) for other in neighbours(*cell)]
        around += [turn(here, 1), turn(here, -1)]
        smoothed.append(smooth_tile(weights.coarse(*cell), here, around))
    doubled = dot(stack(smoothed), double)
    to_middle = {}
    for k, cell in enumerate(coarse_cells):
        ends = jnp.where(lane < 96, turn(smoothed[k], 32), smoothed[k])
        inner = doubled[VECS * k : VECS * (k + 1)]
        to_middle[cell] = jnp.where(lane < 64, inner, ends)

    own, beyond = faces(MX, MY)
    middle_cells = own + beyond
    smoothed = []
    for cell in middle_cells:
        here = values.middle(*cell)
        around = [values.middle(*other) for other in neighbours(*cell)]
        around += [turn(here, 1), turn(here, -1)]
        part = smooth_tile(weights.middle(*cell), here, around)
        smoothed.append(part + to_middle[cell[0] // 2, cell[1] // 2])
    doubled = dot(stack(smoothed), double)
    to_fine, to_end = {}, {}
    for k, cell in enumerate(middle_cells):
        to_fine[cell] = doubled[VECS * k : VECS * (k + 1)]
        to_end[cell] = jnp.where(lane < HALF, turn(smoothed[k], 64), smoothed[k])

    def zs(main, end):
        low = jnp.where(lane > 0, turn(main, 1), turn(end, 1))
        high = jnp.where(lane < LANES - 1, turn(main, -1), turn(end, -1))
        return [low, high]

    own, beyond = faces(LX, LY)
    found, found_end = {}, {}
    for cell in beyond + own:
        here, end = values.fine(*cell), values.fine_end(*cell)
        around = [values.fine(*other) for other in neighbours(*cell)] + zs(here, end)
        part = smooth_tile(weights.fine(*cell), here, around)
        found[cell] = part + to_fine[cell[0] // 2, cell[1] // 2]
    for cell in own:
        here, end = values.fine(*cell), values.fine_end(*cell)
        around = [values.fine_end(*other) for other in neighbours(*cell)] + zs(end, here)
        part = smooth_tile(weights.fine_end(*cell), end, around)
        found_end[cell] = part + to_end[cell[0] // 2, cell[1] // 2]
    basis_ref[: 2 * VECS] = xp_ref[...]
    basis_ref[3 * VECS : 4 * VECS] = jnp.zeros((VECS, FINE * LANES), F32)
    basis_ref[4 * VECS : 6 * VECS] = axp_ref[...]
    for cell in own:
        k = cell[0] * LY + cell[1]
        here = found[cell]
        factors = tile(cf, k)
        around = [found[other] for other in neighbours(*cell)] + zs(here, found_end[cell])
        applied = factors[6:7] * here - spread(factors, around)
        columns = slice(k * LANES, (k + 1) * LANES)
        wa_ref[:VECS, columns] = here
        wa_ref[VECS:, columns] = applied
        basis_ref[2 * VECS : 3 * VECS, columns] = here
        basis_ref[6 * VECS : 7 * VECS, columns] = applied
    pair = dot(basis_ref[: 3 * VECS], basis_ref[...], (1, 1))
    gram[...] = jnp.concatenate([pair, jnp.zeros((3 * VECS, VECS), F32)], axis=1)


def combine(coefficients, xp_ref, wa_ref, axp_ref):
    lane = lanes_of(VECS)
    both = stack([coefficients, jnp.where(lane >= VECS, coefficients, 0.0)])[:, : 3 * VECS]
    search = stack([xp_ref[...], wa_ref[:VECS]])
    moved = dot(both, search)
    if axp_ref is None:
        return moved, None
    applied = stack([axp_ref[...], wa_ref[VECS:]])
    return moved, dot(both, applied)


def third_kernel(summed, xp_ref, axp_ref, wa_ref, cf, cm, cc, nxp, naxp, ef, em, ec, zr, zl):
    coefficients, projected = ritz(summed[...])
    moved, applied = combine(coefficients, xp_ref, wa_ref, axp_ref)
    nxp[...] = moved
    naxp[...] = applied
    level_parts(moved[:VECS], applied[:VECS], projected, cf, cm, cc, ef, em, ec)
    pack_z(ef, em, ec, cf, cm, cc, zr, zl)


def last_kernel(summed, xp_ref, wa_ref, x_out, p_out):
    coefficients, _ = ritz(summed[...])
    moved, _ = combine(coefficients, xp_ref, wa_ref, None)
    for k in range(FINE):
        columns = slice(k * LANES, (k + 1) * LANES)
        x_out[pl.ds(k, VECS, stride=FINE), :] = moved[:VECS, columns]
        p_out[pl.ds(k, VECS, stride=FINE), :] = moved[VECS:, columns]


def shifted(values, axis, by):
    peers = lax.axis_size(axis)
    return lax.ppermute(values, axis, [(i, (i + by) % peers) for i in range(peers)])


def all_sum(values):
    axes = ("gx", "gy", "gz")
    sizes = [lax.axis_size(axis) for axis in axes]
    cells = [
        (x, y, z) for x in range(sizes[0]) for y in range(sizes[1]) for z in range(sizes[2])
    ]

    def number(x, y, z):
        return (x * sizes[1] + y) * sizes[2] + z

    def send(array, pairs):
        return lax.ppermute(array, axes, [(number(*i), number(*j)) for i, j in pairs])

    odd = [cell for cell in cells if cell[1] % 2 == 1]
    is_odd = (lax.axis_index("gy") % 2).astype(F32)
    values = (values + send(values, [((x, y - 1, z), (x, y, z)) for x, y, z in odd])) * is_odd
    bit = 1
    while bit < max(sizes):
        for axis in (0, 2, 1):
            if bit < sizes[axis] and (axis, bit) != (1, 1):
                pairs = []
                for cell in odd:
                    other = list(cell)
                    other[axis] ^= bit
                    pairs.append((cell, tuple(other)))
                values = values + send(values, pairs)
        bit *= 2
    return values + send(values, [((x, y, z), (x, y - 1, z)) for x, y, z in odd])


def exchange(parts, weights, zr, zl):
    rows = zr.shape[0]
    ec = parts[2]
    zr, zl = shifted(zr, "gz", 1), shifted(zl, "gz", -1)
    y2u, y2d = shifted(ec, "gy", 2), shifted(ec, "gy", -2)
    yu, yd = run(pack_y_kernel, [(rows, 27 * LANES)] * 2, (*parts, *weights, zr, zl))
    yu, yd = shifted(yu, "gy", 1), shifted(yd, "gy", -1)
    xu, xd = run(pack_x_kernel, [(rows, 21 * LANES)] * 2, (*parts, *weights, zr, zl, yu, yd, y2u, y2d))
    xu, xd = shifted(xu, "gx", 1), shifted(xd, "gx", -1)
    return (zr, zl, yu, yd, xu, xd), (y2u, y2d)


def on_device(x_block, p_block, voxel_class, conductance):
    sizes = [lax.axis_size(axis) for axis in ("gx", "gy", "gz")]
    all_cells = FINE * LANES * sizes[0] * sizes[1] * sizes[2]
    wide = FINE * LANES
    flags = []
    for axis, size in zip(("gx", "gy", "gz"), sizes):
        at = lax.axis_index(axis)
        flags += [at > 0, at < size - 1]
    flags = jnp.stack(flags).astype(F32)
    field, zr, zl, yu, yd, xu, xd = run(
        start_kernel,
        [(40, wide)] + [(40, LANES)] * 2 + [(40, LX * LANES)] * 2 + [(40, LY * LANES)] * 2,
        (
            x_block.reshape(VECS * FINE, LANES),
            p_block.reshape(VECS * FINE, LANES),
            voxel_class.reshape(FINE, LANES),
        ),
        (conductance,),
    )
    arrived = (
        shifted(zr, "gz", 1), shifted(zl, "gz", -1), shifted(yu, "gy", 1),
        shifted(yd, "gy", -1), shifted(xu, "gx", 1), shifted(xd, "gx", -1),
    )
    fields = [(2 * VECS, wide)] * 2
    weight_shapes = [(8, wide), (8, MIDDLE * LANES), (8, COARSE * LANES)]
    xp, axp, cf, cm, cc, gram = run(
        first_kernel, fields + weight_shapes + [(VECS, LANES)], (field, *arrived), (flags,)
    )
    weights = (cf, cm, cc)
    part_shapes = [(VECS, wide), (VECS, MIDDLE * LANES), (VECS, COARSE * LANES)]
    gram = all_sum(gram) * (1.0 / all_cells)
    rows = VECS + 8
    *parts, zr, zl = run(
        second_kernel, part_shapes + [(rows, LANES)] * 2, (gram, xp, axp, *weights)
    )
    sent_weights = None
    for iteration in range(ITERS):
        sent, far = exchange(parts, weights, zr, zl)
        if sent_weights is None:
            sent_weights = sent
        wa, gram = search(xp, axp, parts, weights, sent, far, sent_weights, wide)
        gram = all_sum(gram) * (1.0 / all_cells)
        if iteration < ITERS - 1:
            xp, axp, *parts, zr, zl = run(
                third_kernel,
                fields + part_shapes + [(VECS, LANES)] * 2,
                (gram, xp, axp, wa, *weights),
            )
    x_out, p_out = run(last_kernel, [(VECS * FINE, LANES)] * 2, (gram, xp, wa))
    return (x_out.reshape(x_block.shape), p_out.reshape(x_block.shape))


def search(xp, axp, parts, weights, sent, far, sent_weights, wide):
    inputs = (xp, axp, *parts, *weights, *sent, *far, *sent_weights)
    return pl.pallas_call(
        search_kernel,
        out_shape=[SHAPE((2 * VECS, wide), F32), SHAPE((3 * VECS, LANES), F32)],
        in_specs=[pl.BlockSpec(memory_space=pltpu.VMEM)] * len(inputs),
        out_specs=[pl.BlockSpec(memory_space=pltpu.VMEM)] * 2,
        scratch_shapes=[pltpu.VMEM((7 * VECS, wide), F32)],
        compiler_params=pltpu.CompilerParams(vmem_limit_bytes=GRANT),
        interpret=INTERPRET,
    )(*inputs)


def solution(mesh):
    in_specs = (P(None, "gx", "gy", "gz"), P(None, "gx", "gy", "gz"), P("gx", "gy", "gz"), P())
    out_specs = (P(None, "gx", "gy", "gz"), P(None, "gx", "gy", "gz"))
    return jax.shard_map(
        on_device, mesh=mesh, in_specs=in_specs, out_specs=out_specs, check_vma=False
    )
```

```python
import jax
import jax.numpy as jnp
from jax import lax
from jax.experimental import pallas as pl
from jax.experimental.pallas import tpu as pltpu
from jax.sharding import PartitionSpec as P

VECS = 16
CLASSES = 8
ITERS = 2
INNER = 4
INTERPRET = False
GRANT = 24 * 1024 * 1024

jacobi_weight = 2.0 / 3.0
mass_shift = 0.05

LX, LY, LANES = 8, 4, 128
MX, MY = LX // 2, LY // 2
CX, CY = LX // 4, LY // 4
FINE, MIDDLE, COARSE = LX * LY, MX * MY, CX * CY
SHAPE = jax.ShapeDtypeStruct
F32 = jnp.float32
HALF = LANES // 2


def tile(ref, index, rows=slice(None)):
    return ref[rows, index * LANES : (index + 1) * LANES]


def lanes_of(rows=8):
    return lax.broadcasted_iota(jnp.int32, (rows, LANES), 1)


def rows_of(rows):
    return lax.broadcasted_iota(jnp.int32, (rows, LANES), 0)


def turn(value, shift):
    shift = shift % LANES
    return value if shift == 0 else pltpu.roll(value, shift, 1)


def dot(left, right, contract=(1, 0)):
    return lax.dot_general(
        left,
        right,
        (((contract[0],), (contract[1],)), ((), ())),
        precision=lax.Precision.HIGHEST,
        preferred_element_type=F32,
    )


def pair_matrix(transposed):
    wide = lax.broadcasted_iota(jnp.int32, (LANES, LANES), 1 if transposed else 0)
    narrow = lax.broadcasted_iota(jnp.int32, (LANES, LANES), 0 if transposed else 1)
    return jnp.where(wide // 2 == narrow, 1.0, 0.0).astype(F32)


def stack(values):
    return jnp.concatenate(values, axis=0)


def run(body, outs, vmem, smem=()):
    in_specs = [pl.BlockSpec(memory_space=pltpu.SMEM)] * len(smem)
    in_specs += [pl.BlockSpec(memory_space=pltpu.VMEM)] * len(vmem)
    return pl.pallas_call(
        body,
        out_shape=[SHAPE(shape, F32) for shape in outs],
        in_specs=in_specs,
        out_specs=[pl.BlockSpec(memory_space=pltpu.VMEM)] * len(outs),
        compiler_params=pltpu.CompilerParams(vmem_limit_bytes=GRANT),
        interpret=INTERPRET,
    )(*smem, *vmem)


def start_kernel(cond_ref, x_ref, p_ref, class_ref, field_ref, zr, zl, yu, yd, xu, xd):
    classes = class_ref[...]
    local = jnp.zeros(classes.shape, F32)
    for index in range(CLASSES):
        local = local + jnp.where(classes == index, cond_ref[index], 0.0)
    lane = lanes_of(40)
    right = jnp.zeros((40, LANES), F32)
    left = jnp.zeros((40, LANES), F32)
    for x in range(LX):
        for y in range(LY):
            p = x * LY + y
            cell = stack(
                [
                    x_ref[pl.ds(p, VECS, stride=FINE), :],
                    p_ref[pl.ds(p, VECS, stride=FINE), :],
                    jnp.broadcast_to(local[p : p + 1], (8, LANES)),
                ]
            )
            field_ref[:, p * LANES : (p + 1) * LANES] = cell
            right = jnp.where(lane == p, turn(cell, p + 1), right)
            left = jnp.where(lane == p, turn(cell, p), left)
            if y == LY - 1:
                yu[:, x * LANES : (x + 1) * LANES] = cell
            if y == 0:
                yd[:, x * LANES : (x + 1) * LANES] = cell
            if x == LX - 1:
                xu[:, y * LANES : (y + 1) * LANES] = cell
            if x == 0:
                xd[:, y * LANES : (y + 1) * LANES] = cell
    zr[...] = right
    zl[...] = left


def finish_weights(weights, shift_term):
    row = rows_of(8)
    weights = jnp.where(row < 6, weights, 0.0)
    diagonal = shift_term + jnp.sum(weights, axis=0, keepdims=True)
    return jnp.where(
        row < 6, weights, jnp.where(row == 6, diagonal, jacobi_weight / diagonal)
    )


def coarsen_weights(fine, size_x, size_y, shift_term, halve):
    row, lane = rows_of(8), lanes_of(8)
    sums = []
    for x in range(size_x):
        for y in range(size_y):
            total = jnp.zeros((8, LANES), F32)
            for i in range(2):
                for j in range(2):
                    keep = (row == i) | (row == 2 + j)
                    keep = keep | ((row == 4) & (lane % 2 == 0)) | ((row == 5) & (lane % 2 == 1))
                    total = total + jnp.where(keep, fine[2 * x + i, 2 * y + j], 0.0)
            sums.append(total)
    paired = dot(stack(sums), halve)
    return {
        (k // size_y, k % size_y): finish_weights(paired[8 * k : 8 * k + 8], shift_term)
        for k in range(size_x * size_y)
    }


def first_kernel(flag_ref, field_ref, zr, zl, yu, yd, xu, xd, xp_ref, axp_ref, cf, cm, cc, gram):
    lane, row = lanes_of(8), rows_of(8)
    lane40 = lanes_of(40)
    from_low, from_high = zr[...], zl[...]
    flags = [flag_ref[k] for k in range(6)]
    ends = jnp.where((row == 4) & (lane == 0), flags[4], 1.0)
    ends = jnp.where((row == 5) & (lane == LANES - 1), flags[5], ends)
    fine = {}
    for x in range(LX):
        for y in range(LY):
            p = x * LY + y
            here = tile(field_ref, p)
            beside = [
                tile(field_ref, p - LY) if x > 0 else tile(xu, y),
                tile(field_ref, p + LY) if x < LX - 1 else tile(xd, y),
                tile(field_ref, p - 1) if y > 0 else tile(yu, x),
                tile(field_ref, p + 1) if y < LY - 1 else tile(yd, x),
                jnp.where(lane40 == 0, turn(from_low, -p), turn(here, 1)),
                jnp.where(lane40 == LANES - 1, turn(from_high, LANES - 1 - p), turn(here, -1)),
            ]
            around = stack([value[32:33] for value in beside] + [here[32:34]])
            own = here[32:40]
            keep = ends
            for side, at_end in enumerate((x == 0, x == LX - 1, y == 0, y == LY - 1)):
                if at_end:
                    keep = jnp.where(row == side, flags[side], keep)
            weights = finish_weights(2.0 * around * own / (around + own) * keep, mass_shift)
            fine[x, y] = weights
            cf[:, p * LANES : (p + 1) * LANES] = weights
            applied = weights[6:7] * here[:32]
            for side in range(6):
                applied = applied - weights[side : side + 1] * beside[side][:32]
            xp_ref[:, p * LANES : (p + 1) * LANES] = here[:32]
            axp_ref[:, p * LANES : (p + 1) * LANES] = applied
    halve = pair_matrix(False)
    middle = coarsen_weights(fine, MX, MY, 8.0 * mass_shift, halve)
    for (x, y), value in middle.items():
        k = x * MY + y
        cm[:, k * LANES : (k + 1) * LANES] = value
    coarse = coarsen_weights(middle, CX, CY, 64.0 * mass_shift, halve)
    for (x, y), value in coarse.items():
        cc[:, x * LANES : (x + 1) * LANES] = value
    flat_x = xp_ref[:VECS]
    other = stack([flat_x, axp_ref[:VECS]])
    pair = dot(flat_x, other, (1, 1))
    gram[...] = jnp.concatenate(
        [pair, jnp.zeros((VECS, LANES - 2 * VECS), F32)], axis=1
    )


def eliminate(rows, size, full):
    tiles = [rows[8 * i : 8 * i + 8] for i in range(rows.shape[0] // 8)]
    row = rows_of(8)
    kept = [tile_rows for tile_rows in tiles]
    for k in range(0, size, 2):
        at, sub = divmod(k, 8)
        spread_left = jnp.broadcast_to(tiles[at][:, k : k + 1], (8, LANES))
        spread_right = jnp.broadcast_to(tiles[at][:, k + 1 : k + 2], (8, LANES))

        def line(value, which):
            return jnp.broadcast_to(value[sub + which : sub + which + 1], (8, LANES))

        first, second = line(tiles[at], 0), line(tiles[at], 1)
        a, b = line(spread_left, 0), line(spread_right, 0)
        c, d = line(spread_left, 1), line(spread_right, 1)
        crossed = a * second - c * first
        inverse = 1.0 / (a * d - b * c)
        solved_first = (d * first - b * second) * inverse
        solved_second = crossed * inverse
        if not full:
            kept[at] = jnp.where(row == sub, first * (1.0 / jnp.sqrt(a)), kept[at])
            root = jnp.sqrt(inverse) * (1.0 / jnp.sqrt(a))
            kept[at] = jnp.where(row == sub + 1, crossed * root, kept[at])
        for i in range(len(tiles)):
            if i < at and not full:
                continue
            if i == at:
                left, right = spread_left, spread_right
            else:
                left, right = tiles[i][:, k : k + 1], tiles[i][:, k + 1 : k + 2]
            changed = tiles[i] - (left * solved_first + right * solved_second)
            if i == at:
                changed = jnp.where(row == sub, solved_first, changed)
                changed = jnp.where(row == sub + 1, solved_second, changed)
            tiles[i] = changed
    return stack(tiles if full else kept)


def lower_pad(matrix):
    missing = LANES - matrix.shape[0]
    return stack([matrix, jnp.zeros((missing, LANES), F32)])


def solve_projected(gram, cross):
    lane = lanes_of(VECS)
    on_diagonal = jnp.where((lane == rows_of(VECS)) & (lane < VECS), gram, 0.0)
    column = 1.0 / jnp.sqrt(jnp.sum(on_diagonal, axis=1, keepdims=True))
    across = jnp.sum(on_diagonal, axis=0, keepdims=True)
    across = jnp.where(lanes_of(1) < VECS, 1.0 / jnp.sqrt(across), 0.0)
    both = jnp.where(lane < HALF, gram * across, turn(cross, HALF)) * column
    return turn(eliminate(both, VECS, True), HALF) * column


def ritz(summed):
    size = 3 * VECS
    lane, row = lanes_of(size), rows_of(size)
    flipped = lower_pad(summed).T
    sym_b = jnp.where(lane < size, 0.5 * (summed + flipped[:size]), 0.0)
    sym_a = 0.5 * (turn(summed, HALF) + flipped[HALF : HALF + size])
    sym_a = jnp.where(lane < size, sym_a, 0.0)
    on_diagonal = jnp.where(lane == row, sym_b, 0.0)
    column = 1.0 / jnp.sqrt(jnp.sum(on_diagonal, axis=1, keepdims=True))
    across = jnp.sum(on_diagonal, axis=0, keepdims=True)
    across = jnp.where(lanes_of(1) < size, 1.0 / jnp.sqrt(across), 0.0)
    normed_b = sym_b * column * across
    normed_a = sym_a * column * across
    done = eliminate(jnp.where(lane < HALF, normed_a, turn(normed_b, HALF)), size, True)
    step = jnp.where(lane < size, turn(done, HALF), 0.0)
    weighed = dot(normed_b[:, :size], step)
    step_pad, weighed_pad = lower_pad(step), lower_pad(weighed)
    step_flipped, weighed_flipped = step_pad.T, weighed_pad.T
    short_lane = lanes_of(VECS)
    basis = None
    for inner_step in range(INNER):
        if basis is None:
            mapped, product = step_flipped[:VECS], weighed_flipped[:VECS]
        else:
            mapped = dot(basis, step_pad, (1, 1))
            product = dot(basis, weighed_pad, (1, 1))
        square = dot(product, lower_pad(mapped), (1, 1))
        done = eliminate(jnp.where(short_lane < HALF, square, turn(mapped, HALF)), VECS, False)
        basis = jnp.where(short_lane < size, turn(done, HALF), 0.0)
    cross = dot(dot(basis, lower_pad(normed_a), (1, 1)), lower_pad(basis), (1, 1))
    return basis * across, cross


def level_parts(x, applied, projected, cf, cm, cc, ef, em, ec):
    small = projected[:, :VECS]
    residual = applied - dot(small, x, (0, 0))
    halve = pair_matrix(False)
    sums = []
    for mx in range(MX):
        for my in range(MY):
            total = jnp.zeros((VECS, LANES), F32)
            for i in range(2):
                for j in range(2):
                    p = (2 * mx + i) * LY + 2 * my + j
                    part = residual[:, p * LANES : (p + 1) * LANES]
                    total = total + part
                    ef[:, p * LANES : (p + 1) * LANES] = part * tile(cf, p, slice(7, 8))
            sums.append(total)
    paired = dot(stack(sums), halve)
    middle = [paired[VECS * k : VECS * (k + 1)] for k in range(MIDDLE)]
    for k in range(MIDDLE):
        em[:, k * LANES : (k + 1) * LANES] = middle[k] * tile(cm, k, slice(7, 8))
    sums = []
    for cx in range(CX):
        sums.append(sum(middle[(2 * cx + i) * MY + j] for i in range(2) for j in range(2)))
    paired = dot(stack(sums), halve)
    for k in range(COARSE):
        coarse = paired[VECS * k : VECS * (k + 1)]
        ec[:, k * LANES : (k + 1) * LANES] = coarse * tile(cc, k, slice(7, 8))


def pack_z(ef, em, ec, cf, cm, cc, zr, zl):
    rows = zr.shape[0]
    lane = lanes_of(rows)

    def cell(values, weights, k):
        here = tile(values, k)
        return stack([here, tile(weights, k)]) if rows > VECS else here

    right = jnp.zeros((rows, LANES), F32)
    left = jnp.zeros((rows, LANES), F32)
    levels = ((ef, cf, FINE, 0, 126), (em, cm, MIDDLE, 64, 62), (ec, cc, COARSE, 80, 30))
    for values, weights, count, base, last in levels:
        for k in range(count):
            here = cell(values, weights, k)
            spot = base + 2 * k
            right = jnp.where(lane // 2 == spot // 2, turn(here, spot - last), right)
            left = jnp.where(lane // 2 == spot // 2, turn(here, spot), left)
    zr[...] = right
    zl[...] = left


def second_kernel(summed, xp_ref, axp_ref, cf, cm, cc, ef, em, ec, zr, zl):
    pair = summed[...]
    lane = lanes_of(VECS)
    gram = jnp.where(lane < VECS, pair, 0.0)
    cross = jnp.where(lane < VECS, turn(pair, -VECS), 0.0)
    projected = solve_projected(gram, cross)
    level_parts(xp_ref[:VECS], axp_ref[:VECS], projected, cf, cm, cc, ef, em, ec)
    pack_z(ef, em, ec, cf, cm, cc, zr, zl)


class Level:
    def __init__(self, own, low, high, rows, yu=None, yd=None, xu=None, xd=None, y2u=None, y2d=None):
        self.own, self.rows = own, rows
        self.low, self.high = low[rows], high[rows]
        self.yu, self.yd, self.xu, self.xd, self.y2u, self.y2d = yu, yd, xu, xd, y2u, y2d
        count = rows.stop - rows.start
        self.count, self.lane = count, lanes_of(count)
        self.kept = {}

    def once(self, key, make):
        if key not in self.kept:
            self.kept[key] = make()
        return self.kept[key]

    def own_rows(self, ref, k):
        if isinstance(ref, tuple):
            return stack([tile(part, k) for part in ref])
        return tile(ref, k)

    def fine(self, x, y):
        if 0 <= x < LX and 0 <= y < LY:
            return self.own_rows(self.own[0], x * LY + y)
        if 0 <= x < LX:
            return tile(self.yu, 2 * x + y + 2, self.rows) if y < 0 else tile(self.yd, 2 * x + y - LY, self.rows)
        ref, near = (self.xu, x == -1) if x < 0 else (self.xd, x == LX)
        return tile(ref, y + 1 if near else 6 + y, self.rows)

    def fine_end(self, x, y):
        def make():
            if 0 <= x < LX and 0 <= y < LY:
                p = x * LY + y
                return jnp.where(
                    self.lane < HALF, turn(self.high, -2 * p), turn(self.low, 126 - 2 * p)
                )
            if 0 <= x < LX:
                return turn(tile(self.yu if y < 0 else self.yd, 16, self.rows), -(1 + 2 * x))
            return turn(tile(self.xu if x < 0 else self.xd, 10, self.rows), -(1 + 2 * y))

        return self.once(("end", x, y), make)

    def middle(self, x, y):
        def make():
            if 0 <= x < MX and 0 <= y < MY:
                k = x * MY + y
                beyond = jnp.where(
                    self.lane < 96, turn(self.high, -2 * k), turn(self.low, 62 - 2 * k)
                )
                return jnp.where(self.lane < 64, self.own_rows(self.own[1], k), beyond)
            if 0 <= x < MX:
                return tile(self.yu, 17 + MY * x + y + MY, self.rows) if y < 0 else tile(
                    self.yd, 17 + MY * x + y - MY, self.rows
                )
            ref, near = (self.xu, x == -1) if x < 0 else (self.xd, x == MX)
            return tile(ref, 12 + y if near else 15 + y, self.rows)

        return self.once(("middle", x, y), make)

    def coarse(self, x, y):
        def make():
            if 0 <= x < CX and y == 0:
                beyond = jnp.where(
                    self.lane < 64, turn(self.high, -48 - 2 * x), turn(self.low, 46 - 2 * x)
                )
                return jnp.where(self.lane < 32, self.own_rows(self.own[2], x), beyond)
            if 0 <= x < CX:
                if abs(y) == 2:
                    return tile(self.y2u if y < 0 else self.y2d, x)
                return tile(self.yu if y < 0 else self.yd, 25 + x, self.rows)
            ref, near = (self.xu, x == -1) if x < 0 else (self.xd, x == CX)
            return tile(ref, 18 + y if near else 20, self.rows)

        return self.once(("coarse", x, y), make)


def put(ref, index, value):
    ref[:, index * LANES : (index + 1) * LANES] = value


def pack_ends(values):
    rows = values[0].shape[0]
    lane = lanes_of(rows)
    packed = jnp.zeros((rows, LANES), F32)
    for k, value in enumerate(values):
        packed = jnp.where(lane // 2 == k, turn(value, 1 + 2 * k), packed)
    return packed


def owns(refs, rows):
    ef, em, ec, cf, cm, cc = refs
    return ((ef, cf), (em, cm), (ec, cc)) if rows > VECS else (ef, em, ec)


def pack_y_kernel(ef, em, ec, cf, cm, cc, zr, zl, yu, yd):
    rows = zr.shape[0]
    level = Level(owns((ef, em, ec, cf, cm, cc), rows), zr, zl, slice(0, rows))
    for ref, first, edge in ((yu, LY - 2, LY - 1), (yd, 0, 0)):
        for x in range(LX):
            for j in range(2):
                put(ref, 2 * x + j, level.fine(x, first + j))
        put(ref, 16, pack_ends([level.fine_end(x, edge) for x in range(LX)]))
        for x in range(MX):
            for y in range(MY):
                put(ref, 17 + MY * x + y, level.middle(x, y))
        for x in range(CX):
            put(ref, 25 + x, level.coarse(x, 0))


def pack_x_kernel(ef, em, ec, cf, cm, cc, zr, zl, ryu, ryd, y2u, y2d, xu, xd):
    rows = zr.shape[0]
    level = Level(owns((ef, em, ec, cf, cm, cc), rows), zr, zl, slice(0, rows), ryu, ryd)
    for ref, up in ((xu, True), (xd, False)):
        near, far = (LX - 1, LX - 2) if up else (0, 1)
        for y in range(-1, LY + 1):
            put(ref, y + 1, level.fine(near, y))
        for y in range(LY):
            put(ref, 6 + y, level.fine(far, y))
        put(ref, 10, pack_ends([level.fine_end(near, y) for y in range(LY)]))
        near, far = (MX - 1, MX - 2) if up else (0, 1)
        for y in range(-1, MY + 1):
            put(ref, 12 + y, level.middle(near, y))
        for y in range(MY):
            put(ref, 15 + y, level.middle(far, y))
        near, far = (CX - 1, CX - 2) if up else (0, 1)
        for y in range(-1, 2):
            put(ref, 18 + y, level.coarse(near, y))
        put(ref, 20, level.coarse(far, 0))


def faces(size_x, size_y):
    own = [(x, y) for x in range(size_x) for y in range(size_y)]
    beyond = [(x, y) for x in (-1, size_x) for y in range(size_y)]
    beyond += [(x, y) for x in range(size_x) for y in (-1, size_y)]
    return own, beyond


def neighbours(x, y):
    return ((x - 1, y), (x + 1, y), (x, y - 1), (x, y + 1))


def spread(weights, values):
    total = weights[0:1] * values[0]
    for side in range(1, 6):
        total = total + weights[side : side + 1] * values[side]
    return total


def smooth_tile(weights, here, values):
    return (2.0 * jacobi_weight) * here + weights[7:8] * spread(weights, values)


def search_kernel(
    xp_ref, axp_ref, ef, em, ec, cf, cm, cc,
    zr, zl, yu, yd, xu, xd, y2u, y2d,
    wzr, wzl, wyu, wyd, wxu, wxd,
    wa_ref, gram, basis_ref,
):
    values = Level((ef, em, ec), zr, zl, slice(0, VECS), yu, yd, xu, xd, y2u, y2d)
    weights = Level((cf, cm, cc), wzr, wzl, slice(VECS, VECS + 8), wyu, wyd, wxu, wxd)
    lane = lanes_of(VECS)
    double = pair_matrix(True)

    own, beyond = faces(CX, CY)
    coarse_cells = own + beyond
    smoothed = []
    for cell in coarse_cells:
        here = values.coarse(*cell)
        around = [values.coarse(*other) for other in neighbours(*cell)]
        around += [turn(here, 1), turn(here, -1)]
        smoothed.append(smooth_tile(weights.coarse(*cell), here, around))
    doubled = dot(stack(smoothed), double)
    to_middle = {}
    for k, cell in enumerate(coarse_cells):
        ends = jnp.where(lane < 96, turn(smoothed[k], 32), smoothed[k])
        inner = doubled[VECS * k : VECS * (k + 1)]
        to_middle[cell] = jnp.where(lane < 64, inner, ends)

    own, beyond = faces(MX, MY)
    middle_cells = own + beyond
    smoothed = []
    for cell in middle_cells:
        here = values.middle(*cell)
        around = [values.middle(*other) for other in neighbours(*cell)]
        around += [turn(here, 1), turn(here, -1)]
        part = smooth_tile(weights.middle(*cell), here, around)
        smoothed.append(part + to_middle[cell[0] // 2, cell[1] // 2])
    doubled = dot(stack(smoothed), double)
    to_fine, to_end = {}, {}
    for k, cell in enumerate(middle_cells):
        to_fine[cell] = doubled[VECS * k : VECS * (k + 1)]
        to_end[cell] = jnp.where(lane < HALF, turn(smoothed[k], 64), smoothed[k])

    def zs(main, end):
        low = jnp.where(lane > 0, turn(main, 1), turn(end, 1))
        high = jnp.where(lane < LANES - 1, turn(main, -1), turn(end, -1))
        return [low, high]

    own, beyond = faces(LX, LY)
    found, found_end = {}, {}
    for cell in beyond + own:
        here, end = values.fine(*cell), values.fine_end(*cell)
        around = [values.fine(*other) for other in neighbours(*cell)] + zs(here, end)
        part = smooth_tile(weights.fine(*cell), here, around)
        found[cell] = part + to_fine[cell[0] // 2, cell[1] // 2]
    for cell in own:
        here, end = values.fine(*cell), values.fine_end(*cell)
        around = [values.fine_end(*other) for other in neighbours(*cell)] + zs(end, here)
        part = smooth_tile(weights.fine_end(*cell), end, around)
        found_end[cell] = part + to_end[cell[0] // 2, cell[1] // 2]
    basis_ref[: 2 * VECS] = xp_ref[...]
    basis_ref[3 * VECS : 4 * VECS] = jnp.zeros((VECS, FINE * LANES), F32)
    basis_ref[4 * VECS : 6 * VECS] = axp_ref[...]
    for cell in own:
        k = cell[0] * LY + cell[1]
        here = found[cell]
        factors = tile(cf, k)
        around = [found[other] for other in neighbours(*cell)] + zs(here, found_end[cell])
        applied = factors[6:7] * here - spread(factors, around)
        columns = slice(k * LANES, (k + 1) * LANES)
        wa_ref[:VECS, columns] = here
        wa_ref[VECS:, columns] = applied
        basis_ref[2 * VECS : 3 * VECS, columns] = here
        basis_ref[6 * VECS : 7 * VECS, columns] = applied
    pair = dot(basis_ref[: 3 * VECS], basis_ref[...], (1, 1))
    gram[...] = jnp.concatenate([pair, jnp.zeros((3 * VECS, VECS), F32)], axis=1)


def combine(coefficients, xp_ref, wa_ref, axp_ref):
    lane = lanes_of(VECS)
    both = stack([coefficients, jnp.where(lane >= VECS, coefficients, 0.0)])[:, : 3 * VECS]
    search = stack([xp_ref[...], wa_ref[:VECS]])
    moved = dot(both, search)
    if axp_ref is None:
        return moved, None
    applied = stack([axp_ref[...], wa_ref[VECS:]])
    return moved, dot(both, applied)


def third_kernel(summed, xp_ref, axp_ref, wa_ref, cf, cm, cc, nxp, naxp, ef, em, ec, zr, zl):
    coefficients, projected = ritz(summed[...])
    moved, applied = combine(coefficients, xp_ref, wa_ref, axp_ref)
    nxp[...] = moved
    naxp[...] = applied
    level_parts(moved[:VECS], applied[:VECS], projected, cf, cm, cc, ef, em, ec)
    pack_z(ef, em, ec, cf, cm, cc, zr, zl)


def last_kernel(summed, xp_ref, wa_ref, x_out, p_out):
    coefficients, _ = ritz(summed[...])
    moved, _ = combine(coefficients, xp_ref, wa_ref, None)
    for k in range(FINE):
        columns = slice(k * LANES, (k + 1) * LANES)
        x_out[pl.ds(k, VECS, stride=FINE), :] = moved[:VECS, columns]
        p_out[pl.ds(k, VECS, stride=FINE), :] = moved[VECS:, columns]


def shifted(values, axis, by):
    peers = lax.axis_size(axis)
    return lax.ppermute(values, axis, [(i, (i + by) % peers) for i in range(peers)])


def all_sum(values):
    bit = 1
    while bit < max(lax.axis_size(axis) for axis in ("gy", "gx", "gz")):
        for axis in ("gy", "gx", "gz"):
            peers = lax.axis_size(axis)
            if bit < peers:
                values = values + lax.ppermute(values, axis, [(i, i ^ bit) for i in range(peers)])
        bit *= 2
    return values


def exchange(parts, weights, zr, zl):
    rows = zr.shape[0]
    ec = parts[2]
    zr, zl = shifted(zr, "gz", 1), shifted(zl, "gz", -1)
    y2u, y2d = shifted(ec, "gy", 2), shifted(ec, "gy", -2)
    yu, yd = run(pack_y_kernel, [(rows, 27 * LANES)] * 2, (*parts, *weights, zr, zl))
    yu, yd = shifted(yu, "gy", 1), shifted(yd, "gy", -1)
    xu, xd = run(pack_x_kernel, [(rows, 21 * LANES)] * 2, (*parts, *weights, zr, zl, yu, yd, y2u, y2d))
    xu, xd = shifted(xu, "gx", 1), shifted(xd, "gx", -1)
    return (zr, zl, yu, yd, xu, xd), (y2u, y2d)


def on_device(x_block, p_block, voxel_class, conductance):
    sizes = [lax.axis_size(axis) for axis in ("gx", "gy", "gz")]
    all_cells = FINE * LANES * sizes[0] * sizes[1] * sizes[2]
    wide = FINE * LANES
    flags = []
    for axis, size in zip(("gx", "gy", "gz"), sizes):
        at = lax.axis_index(axis)
        flags += [at > 0, at < size - 1]
    flags = jnp.stack(flags).astype(F32)
    field, zr, zl, yu, yd, xu, xd = run(
        start_kernel,
        [(40, wide)] + [(40, LANES)] * 2 + [(40, LX * LANES)] * 2 + [(40, LY * LANES)] * 2,
        (
            x_block.reshape(VECS * FINE, LANES),
            p_block.reshape(VECS * FINE, LANES),
            voxel_class.reshape(FINE, LANES),
        ),
        (conductance,),
    )
    arrived = (
        shifted(zr, "gz", 1), shifted(zl, "gz", -1), shifted(yu, "gy", 1),
        shifted(yd, "gy", -1), shifted(xu, "gx", 1), shifted(xd, "gx", -1),
    )
    fields = [(2 * VECS, wide)] * 2
    weight_shapes = [(8, wide), (8, MIDDLE * LANES), (8, COARSE * LANES)]
    xp, axp, cf, cm, cc, gram = run(
        first_kernel, fields + weight_shapes + [(VECS, LANES)], (field, *arrived), (flags,)
    )
    weights = (cf, cm, cc)
    part_shapes = [(VECS, wide), (VECS, MIDDLE * LANES), (VECS, COARSE * LANES)]
    gram = all_sum(gram) * (1.0 / all_cells)
    rows = VECS + 8
    *parts, zr, zl = run(
        second_kernel, part_shapes + [(rows, LANES)] * 2, (gram, xp, axp, *weights)
    )
    sent_weights = None
    for iteration in range(ITERS):
        sent, far = exchange(parts, weights, zr, zl)
        if sent_weights is None:
            sent_weights = sent
        wa, gram = search(xp, axp, parts, weights, sent, far, sent_weights, wide)
        gram = all_sum(gram) * (1.0 / all_cells)
        if iteration < ITERS - 1:
            xp, axp, *parts, zr, zl = run(
                third_kernel,
                fields + part_shapes + [(VECS, LANES)] * 2,
                (gram, xp, axp, wa, *weights),
            )
    x_out, p_out = run(last_kernel, [(VECS * FINE, LANES)] * 2, (gram, xp, wa))
    return (x_out.reshape(x_block.shape), p_out.reshape(x_block.shape))


def search(xp, axp, parts, weights, sent, far, sent_weights, wide):
    inputs = (xp, axp, *parts, *weights, *sent, *far, *sent_weights)
    return pl.pallas_call(
        search_kernel,
        out_shape=[SHAPE((2 * VECS, wide), F32), SHAPE((3 * VECS, LANES), F32)],
        in_specs=[pl.BlockSpec(memory_space=pltpu.VMEM)] * len(inputs),
        out_specs=[pl.BlockSpec(memory_space=pltpu.VMEM)] * 2,
        scratch_shapes=[pltpu.VMEM((7 * VECS, wide), F32)],
        compiler_params=pltpu.CompilerParams(vmem_limit_bytes=GRANT),
        interpret=INTERPRET,
    )(*inputs)


def solution(mesh):
    in_specs = (P(None, "gx", "gy", "gz"), P(None, "gx", "gy", "gz"), P("gx", "gy", "gz"), P())
    out_specs = (P(None, "gx", "gy", "gz"), P(None, "gx", "gy", "gz"))
    return jax.shard_map(
        on_device, mesh=mesh, in_specs=in_specs, out_specs=out_specs, check_vma=False
    )
```

```python
import jax
import jax.numpy as jnp
from jax import lax
from jax.experimental import pallas as pl
from jax.experimental.pallas import tpu as pltpu
from jax.sharding import PartitionSpec as P

VECS = 16
CLASSES = 8
ITERS = 2
INNER = 4
INTERPRET = False
GRANT = 24 * 1024 * 1024

jacobi_weight = 2.0 / 3.0
mass_shift = 0.05

LX, LY, LANES = 8, 4, 128
MX, MY = LX // 2, LY // 2
CX, CY = LX // 4, LY // 4
FINE, MIDDLE, COARSE = LX * LY, MX * MY, CX * CY
SHAPE = jax.ShapeDtypeStruct
F32 = jnp.float32
HALF = LANES // 2


def tile(ref, index, rows=slice(None)):
    return ref[rows, index * LANES : (index + 1) * LANES]


def lanes_of(rows=8):
    return lax.broadcasted_iota(jnp.int32, (rows, LANES), 1)


def rows_of(rows):
    return lax.broadcasted_iota(jnp.int32, (rows, LANES), 0)


def turn(value, shift):
    shift = shift % LANES
    return value if shift == 0 else pltpu.roll(value, shift, 1)


def dot(left, right, contract=(1, 0)):
    return lax.dot_general(
        left,
        right,
        (((contract[0],), (contract[1],)), ((), ())),
        precision=lax.Precision.HIGHEST,
        preferred_element_type=F32,
    )


def pair_matrix(transposed):
    wide = lax.broadcasted_iota(jnp.int32, (LANES, LANES), 1 if transposed else 0)
    narrow = lax.broadcasted_iota(jnp.int32, (LANES, LANES), 0 if transposed else 1)
    return jnp.where(wide // 2 == narrow, 1.0, 0.0).astype(F32)


def stack(values):
    return jnp.concatenate(values, axis=0)


def run(body, outs, vmem, smem=()):
    in_specs = [pl.BlockSpec(memory_space=pltpu.SMEM)] * len(smem)
    in_specs += [pl.BlockSpec(memory_space=pltpu.VMEM)] * len(vmem)
    return pl.pallas_call(
        body,
        out_shape=[SHAPE(shape, F32) for shape in outs],
        in_specs=in_specs,
        out_specs=[pl.BlockSpec(memory_space=pltpu.VMEM)] * len(outs),
        compiler_params=pltpu.CompilerParams(vmem_limit_bytes=GRANT),
        interpret=INTERPRET,
    )(*smem, *vmem)


def start_kernel(cond_ref, x_ref, p_ref, class_ref, field_ref, zr, zl, yu, yd, xu, xd):
    classes = class_ref[...]
    local = jnp.zeros(classes.shape, F32)
    for index in range(CLASSES):
        local = local + jnp.where(classes == index, cond_ref[index], 0.0)
    lane = lanes_of(40)
    right = jnp.zeros((40, LANES), F32)
    left = jnp.zeros((40, LANES), F32)
    for x in range(LX):
        for y in range(LY):
            p = x * LY + y
            cell = stack(
                [
                    x_ref[pl.ds(p, VECS, stride=FINE), :],
                    p_ref[pl.ds(p, VECS, stride=FINE), :],
                    jnp.broadcast_to(local[p : p + 1], (8, LANES)),
                ]
            )
            field_ref[:, p * LANES : (p + 1) * LANES] = cell
            right = jnp.where(lane == p, turn(cell, p + 1), right)
            left = jnp.where(lane == p, turn(cell, p), left)
            if y == LY - 1:
                yu[:, x * LANES : (x + 1) * LANES] = cell
            if y == 0:
                yd[:, x * LANES : (x + 1) * LANES] = cell
            if x == LX - 1:
                xu[:, y * LANES : (y + 1) * LANES] = cell
            if x == 0:
                xd[:, y * LANES : (y + 1) * LANES] = cell
    zr[...] = right
    zl[...] = left


def finish_weights(weights, shift_term):
    row = rows_of(8)
    weights = jnp.where(row < 6, weights, 0.0)
    diagonal = shift_term + jnp.sum(weights, axis=0, keepdims=True)
    return jnp.where(
        row < 6, weights, jnp.where(row == 6, diagonal, jacobi_weight / diagonal)
    )


def coarsen_weights(fine, size_x, size_y, shift_term, halve):
    row, lane = rows_of(8), lanes_of(8)
    sums = []
    for x in range(size_x):
        for y in range(size_y):
            total = jnp.zeros((8, LANES), F32)
            for i in range(2):
                for j in range(2):
                    keep = (row == i) | (row == 2 + j)
                    keep = keep | ((row == 4) & (lane % 2 == 0)) | ((row == 5) & (lane % 2 == 1))
                    total = total + jnp.where(keep, fine[2 * x + i, 2 * y + j], 0.0)
            sums.append(total)
    paired = dot(stack(sums), halve)
    return {
        (k // size_y, k % size_y): finish_weights(paired[8 * k : 8 * k + 8], shift_term)
        for k in range(size_x * size_y)
    }


def first_kernel(flag_ref, field_ref, zr, zl, yu, yd, xu, xd, xp_ref, axp_ref, cf, cm, cc, gram):
    lane, row = lanes_of(8), rows_of(8)
    lane40 = lanes_of(40)
    from_low, from_high = zr[...], zl[...]
    flags = [flag_ref[k] for k in range(6)]
    ends = jnp.where((row == 4) & (lane == 0), flags[4], 1.0)
    ends = jnp.where((row == 5) & (lane == LANES - 1), flags[5], ends)
    fine = {}
    for x in range(LX):
        for y in range(LY):
            p = x * LY + y
            here = tile(field_ref, p)
            beside = [
                tile(field_ref, p - LY) if x > 0 else tile(xu, y),
                tile(field_ref, p + LY) if x < LX - 1 else tile(xd, y),
                tile(field_ref, p - 1) if y > 0 else tile(yu, x),
                tile(field_ref, p + 1) if y < LY - 1 else tile(yd, x),
                jnp.where(lane40 == 0, turn(from_low, -p), turn(here, 1)),
                jnp.where(lane40 == LANES - 1, turn(from_high, LANES - 1 - p), turn(here, -1)),
            ]
            around = stack([value[32:33] for value in beside] + [here[32:34]])
            own = here[32:40]
            keep = ends
            for side, at_end in enumerate((x == 0, x == LX - 1, y == 0, y == LY - 1)):
                if at_end:
                    keep = jnp.where(row == side, flags[side], keep)
            weights = finish_weights(2.0 * around * own / (around + own) * keep, mass_shift)
            fine[x, y] = weights
            cf[:, p * LANES : (p + 1) * LANES] = weights
            applied = weights[6:7] * here[:32]
            for side in range(6):
                applied = applied - weights[side : side + 1] * beside[side][:32]
            xp_ref[:, p * LANES : (p + 1) * LANES] = here[:32]
            axp_ref[:, p * LANES : (p + 1) * LANES] = applied
    halve = pair_matrix(False)
    middle = coarsen_weights(fine, MX, MY, 8.0 * mass_shift, halve)
    for (x, y), value in middle.items():
        k = x * MY + y
        cm[:, k * LANES : (k + 1) * LANES] = value
    coarse = coarsen_weights(middle, CX, CY, 64.0 * mass_shift, halve)
    for (x, y), value in coarse.items():
        cc[:, x * LANES : (x + 1) * LANES] = value
    flat_x = xp_ref[:VECS]
    other = stack([flat_x, axp_ref[:VECS]])
    pair = dot(flat_x, other, (1, 1))
    gram[...] = jnp.concatenate(
        [pair, jnp.zeros((VECS, LANES - 2 * VECS), F32)], axis=1
    )


def eliminate(rows, size, full):
    tiles = [rows[8 * i : 8 * i + 8] for i in range(rows.shape[0] // 8)]
    row = rows_of(8)
    kept = list(tiles)
    nothing = rows[:8] * 0.0
    for k in range(0, size, 2):
        at, sub = divmod(k, 8)
        spread_left = tiles[at][:, k : k + 1] + nothing
        spread_right = tiles[at][:, k + 1 : k + 2] + nothing

        def line(value, which):
            return jnp.broadcast_to(value[sub + which : sub + which + 1], (8, LANES))

        first, second = line(tiles[at], 0), line(tiles[at], 1)
        a, b = line(spread_left, 0), line(spread_right, 0)
        c, d = line(spread_left, 1), line(spread_right, 1)
        crossed = a * second - c * first
        inverse = 1.0 / (a * d - b * c)
        solved_first = (d * first - b * second) * inverse
        solved_second = crossed * inverse
        if not full:
            kept[at] = jnp.where(row == sub, first * (1.0 / jnp.sqrt(a)), kept[at])
            root = jnp.sqrt(inverse) * (1.0 / jnp.sqrt(a))
            kept[at] = jnp.where(row == sub + 1, crossed * root, kept[at])
        for i in range(len(tiles)):
            if i < at and not full:
                continue
            if i == at:
                left, right = spread_left, spread_right
            else:
                left, right = tiles[i][:, k : k + 1], tiles[i][:, k + 1 : k + 2]
            changed = tiles[i] - (left * solved_first + right * solved_second)
            if i == at:
                changed = jnp.where(row == sub, solved_first, changed)
                changed = jnp.where(row == sub + 1, solved_second, changed)
            tiles[i] = changed
    return stack(tiles if full else kept)


def lower_pad(matrix):
    missing = LANES - matrix.shape[0]
    return stack([matrix, jnp.zeros((missing, LANES), F32)])


def solve_projected(gram, cross):
    lane = lanes_of(VECS)
    on_diagonal = jnp.where((lane == rows_of(VECS)) & (lane < VECS), gram, 0.0)
    column = 1.0 / jnp.sqrt(jnp.sum(on_diagonal, axis=1, keepdims=True))
    across = jnp.sum(on_diagonal, axis=0, keepdims=True)
    across = jnp.where(lanes_of(1) < VECS, 1.0 / jnp.sqrt(across), 0.0)
    both = jnp.where(lane < HALF, gram * across, turn(cross, HALF)) * column
    return turn(eliminate(both, VECS, True), HALF) * column


def ritz(summed):
    size = 3 * VECS
    lane, row = lanes_of(size), rows_of(size)
    flipped = lower_pad(summed).T
    sym_b = jnp.where(lane < size, 0.5 * (summed + flipped[:size]), 0.0)
    sym_a = 0.5 * (turn(summed, HALF) + flipped[HALF : HALF + size])
    sym_a = jnp.where(lane < size, sym_a, 0.0)
    on_diagonal = jnp.where(lane == row, sym_b, 0.0)
    column = 1.0 / jnp.sqrt(jnp.sum(on_diagonal, axis=1, keepdims=True))
    across = jnp.sum(on_diagonal, axis=0, keepdims=True)
    across = jnp.where(lanes_of(1) < size, 1.0 / jnp.sqrt(across), 0.0)
    normed_b = sym_b * column * across
    normed_a = sym_a * column * across
    done = eliminate(jnp.where(lane < HALF, normed_a, turn(normed_b, HALF)), size, True)
    step = jnp.where(lane < size, turn(done, HALF), 0.0)
    weighed = dot(normed_b[:, :size], step)
    step_pad, weighed_pad = lower_pad(step), lower_pad(weighed)
    step_flipped, weighed_flipped = step_pad.T, weighed_pad.T
    short_lane = lanes_of(VECS)
    basis = None
    for inner_step in range(INNER):
        if basis is None:
            mapped, product = step_flipped[:VECS], weighed_flipped[:VECS]
        else:
            mapped = dot(basis, step_pad, (1, 1))
            product = dot(basis, weighed_pad, (1, 1))
        square = dot(product, lower_pad(mapped), (1, 1))
        done = eliminate(jnp.where(short_lane < HALF, square, turn(mapped, HALF)), VECS, False)
        basis = jnp.where(short_lane < size, turn(done, HALF), 0.0)
    cross = dot(dot(basis, lower_pad(normed_a), (1, 1)), lower_pad(basis), (1, 1))
    return basis * across, cross


def level_parts(x, applied, projected, cf, cm, cc, ef, em, ec):
    small = projected[:, :VECS]
    residual = applied - dot(small, x, (0, 0))
    halve = pair_matrix(False)
    sums = []
    for mx in range(MX):
        for my in range(MY):
            total = jnp.zeros((VECS, LANES), F32)
            for i in range(2):
                for j in range(2):
                    p = (2 * mx + i) * LY + 2 * my + j
                    part = residual[:, p * LANES : (p + 1) * LANES]
                    total = total + part
                    ef[:, p * LANES : (p + 1) * LANES] = part * tile(cf, p, slice(7, 8))
            sums.append(total)
    paired = dot(stack(sums), halve)
    middle = [paired[VECS * k : VECS * (k + 1)] for k in range(MIDDLE)]
    for k in range(MIDDLE):
        em[:, k * LANES : (k + 1) * LANES] = middle[k] * tile(cm, k, slice(7, 8))
    sums = []
    for cx in range(CX):
        sums.append(sum(middle[(2 * cx + i) * MY + j] for i in range(2) for j in range(2)))
    paired = dot(stack(sums), halve)
    for k in range(COARSE):
        coarse = paired[VECS * k : VECS * (k + 1)]
        ec[:, k * LANES : (k + 1) * LANES] = coarse * tile(cc, k, slice(7, 8))


def pack_z(ef, em, ec, cf, cm, cc, zr, zl):
    rows = zr.shape[0]
    lane = lanes_of(rows)

    def cell(values, weights, k):
        here = tile(values, k)
        return stack([here, tile(weights, k)]) if rows > VECS else here

    right = jnp.zeros((rows, LANES), F32)
    left = jnp.zeros((rows, LANES), F32)
    levels = ((ef, cf, FINE, 0, 126), (em, cm, MIDDLE, 64, 62), (ec, cc, COARSE, 80, 30))
    for values, weights, count, base, last in levels:
        for k in range(count):
            here = cell(values, weights, k)
            spot = base + 2 * k
            right = jnp.where(lane // 2 == spot // 2, turn(here, spot - last), right)
            left = jnp.where(lane // 2 == spot // 2, turn(here, spot), left)
    zr[...] = right
    zl[...] = left


def second_kernel(summed, xp_ref, axp_ref, cf, cm, cc, ef, em, ec, zr, zl):
    pair = summed[...]
    lane = lanes_of(VECS)
    gram = jnp.where(lane < VECS, pair, 0.0)
    cross = jnp.where(lane < VECS, turn(pair, -VECS), 0.0)
    projected = solve_projected(gram, cross)
    level_parts(xp_ref[:VECS], axp_ref[:VECS], projected, cf, cm, cc, ef, em, ec)
    pack_z(ef, em, ec, cf, cm, cc, zr, zl)


class Level:
    def __init__(self, own, low, high, rows, yu=None, yd=None, xu=None, xd=None, y2u=None, y2d=None):
        self.own, self.rows = own, rows
        self.low, self.high = low[rows], high[rows]
        self.yu, self.yd, self.xu, self.xd, self.y2u, self.y2d = yu, yd, xu, xd, y2u, y2d
        count = rows.stop - rows.start
        self.count, self.lane = count, lanes_of(count)
        self.kept = {}

    def once(self, key, make):
        if key not in self.kept:
            self.kept[key] = make()
        return self.kept[key]

    def own_rows(self, ref, k):
        if isinstance(ref, tuple):
            return stack([tile(part, k) for part in ref])
        return tile(ref, k)

    def fine(self, x, y):
        if 0 <= x < LX and 0 <= y < LY:
            return self.own_rows(self.own[0], x * LY + y)
        if 0 <= x < LX:
            return tile(self.yu, 2 * x + y + 2, self.rows) if y < 0 else tile(self.yd, 2 * x + y - LY, self.rows)
        ref, near = (self.xu, x == -1) if x < 0 else (self.xd, x == LX)
        return tile(ref, y + 1 if near else 6 + y, self.rows)

    def fine_end(self, x, y):
        def make():
            if 0 <= x < LX and 0 <= y < LY:
                p = x * LY + y
                return jnp.where(
                    self.lane < HALF, turn(self.high, -2 * p), turn(self.low, 126 - 2 * p)
                )
            if 0 <= x < LX:
                return turn(tile(self.yu if y < 0 else self.yd, 16, self.rows), -(1 + 2 * x))
            return turn(tile(self.xu if x < 0 else self.xd, 10, self.rows), -(1 + 2 * y))

        return self.once(("end", x, y), make)

    def middle(self, x, y):
        def make():
            if 0 <= x < MX and 0 <= y < MY:
                k = x * MY + y
                beyond = jnp.where(
                    self.lane < 96, turn(self.high, -2 * k), turn(self.low, 62 - 2 * k)
                )
                return jnp.where(self.lane < 64, self.own_rows(self.own[1], k), beyond)
            if 0 <= x < MX:
                return tile(self.yu, 17 + MY * x + y + MY, self.rows) if y < 0 else tile(
                    self.yd, 17 + MY * x + y - MY, self.rows
                )
            ref, near = (self.xu, x == -1) if x < 0 else (self.xd, x == MX)
            return tile(ref, 12 + y if near else 15 + y, self.rows)

        return self.once(("middle", x, y), make)

    def coarse(self, x, y):
        def make():
            if 0 <= x < CX and y == 0:
                beyond = jnp.where(
                    self.lane < 64, turn(self.high, -48 - 2 * x), turn(self.low, 46 - 2 * x)
                )
                return jnp.where(self.lane < 32, self.own_rows(self.own[2], x), beyond)
            if 0 <= x < CX:
                if abs(y) == 2:
                    return tile(self.y2u if y < 0 else self.y2d, x)
                return tile(self.yu if y < 0 else self.yd, 25 + x, self.rows)
            ref, near = (self.xu, x == -1) if x < 0 else (self.xd, x == CX)
            return tile(ref, 18 + y if near else 20, self.rows)

        return self.once(("coarse", x, y), make)


def put(ref, index, value):
    ref[:, index * LANES : (index + 1) * LANES] = value


def pack_ends(values):
    rows = values[0].shape[0]
    lane = lanes_of(rows)
    packed = jnp.zeros((rows, LANES), F32)
    for k, value in enumerate(values):
        packed = jnp.where(lane // 2 == k, turn(value, 1 + 2 * k), packed)
    return packed


def owns(refs, rows):
    ef, em, ec, cf, cm, cc = refs
    return ((ef, cf), (em, cm), (ec, cc)) if rows > VECS else (ef, em, ec)


def pack_y_kernel(ef, em, ec, cf, cm, cc, zr, zl, yu, yd):
    rows = zr.shape[0]
    level = Level(owns((ef, em, ec, cf, cm, cc), rows), zr, zl, slice(0, rows))
    for ref, first, edge in ((yu, LY - 2, LY - 1), (yd, 0, 0)):
        for x in range(LX):
            for j in range(2):
                put(ref, 2 * x + j, level.fine(x, first + j))
        put(ref, 16, pack_ends([level.fine_end(x, edge) for x in range(LX)]))
        for x in range(MX):
            for y in range(MY):
                put(ref, 17 + MY * x + y, level.middle(x, y))
        for x in range(CX):
            put(ref, 25 + x, level.coarse(x, 0))


def pack_x_kernel(ef, em, ec, cf, cm, cc, zr, zl, ryu, ryd, y2u, y2d, xu, xd):
    rows = zr.shape[0]
    level = Level(owns((ef, em, ec, cf, cm, cc), rows), zr, zl, slice(0, rows), ryu, ryd)
    for ref, up in ((xu, True), (xd, False)):
        near, far = (LX - 1, LX - 2) if up else (0, 1)
        for y in range(-1, LY + 1):
            put(ref, y + 1, level.fine(near, y))
        for y in range(LY):
            put(ref, 6 + y, level.fine(far, y))
        put(ref, 10, pack_ends([level.fine_end(near, y) for y in range(LY)]))
        near, far = (MX - 1, MX - 2) if up else (0, 1)
        for y in range(-1, MY + 1):
            put(ref, 12 + y, level.middle(near, y))
        for y in range(MY):
            put(ref, 15 + y, level.middle(far, y))
        near, far = (CX - 1, CX - 2) if up else (0, 1)
        for y in range(-1, 2):
            put(ref, 18 + y, level.coarse(near, y))
        put(ref, 20, level.coarse(far, 0))


def faces(size_x, size_y):
    own = [(x, y) for x in range(size_x) for y in range(size_y)]
    beyond = [(x, y) for x in (-1, size_x) for y in range(size_y)]
    beyond += [(x, y) for x in range(size_x) for y in (-1, size_y)]
    return own, beyond


def neighbours(x, y):
    return ((x - 1, y), (x + 1, y), (x, y - 1), (x, y + 1))


def spread(weights, values):
    total = weights[0:1] * values[0]
    for side in range(1, 6):
        total = total + weights[side : side + 1] * values[side]
    return total


def smooth_tile(weights, here, values):
    return (2.0 * jacobi_weight) * here + weights[7:8] * spread(weights, values)


def search_kernel(
    xp_ref, axp_ref, ef, em, ec, cf, cm, cc,
    zr, zl, yu, yd, xu, xd, y2u, y2d,
    wzr, wzl, wyu, wyd, wxu, wxd,
    wa_ref, gram, basis_ref,
):
    values = Level((ef, em, ec), zr, zl, slice(0, VECS), yu, yd, xu, xd, y2u, y2d)
    weights = Level((cf, cm, cc), wzr, wzl, slice(VECS, VECS + 8), wyu, wyd, wxu, wxd)
    lane = lanes_of(VECS)
    double = pair_matrix(True)

    own, beyond = faces(CX, CY)
    coarse_cells = own + beyond
    smoothed = []
    for cell in coarse_cells:
        here = values.coarse(*cell)
        around = [values.coarse(*other) for other in neighbours(*cell)]
        around += [turn(here, 1), turn(here, -1)]
        smoothed.append(smooth_tile(weights.coarse(*cell), here, around))
    doubled = dot(stack(smoothed), double)
    to_middle = {}
    for k, cell in enumerate(coarse_cells):
        ends = jnp.where(lane < 96, turn(smoothed[k], 32), smoothed[k])
        inner = doubled[VECS * k : VECS * (k + 1)]
        to_middle[cell] = jnp.where(lane < 64, inner, ends)

    own, beyond = faces(MX, MY)
    middle_cells = own + beyond
    smoothed = []
    for cell in middle_cells:
        here = values.middle(*cell)
        around = [values.middle(*other) for other in neighbours(*cell)]
        around += [turn(here, 1), turn(here, -1)]
        part = smooth_tile(weights.middle(*cell), here, around)
        smoothed.append(part + to_middle[cell[0] // 2, cell[1] // 2])
    doubled = dot(stack(smoothed), double)
    to_fine, to_end = {}, {}
    for k, cell in enumerate(middle_cells):
        to_fine[cell] = doubled[VECS * k : VECS * (k + 1)]
        to_end[cell] = jnp.where(lane < HALF, turn(smoothed[k], 64), smoothed[k])

    def zs(main, end):
        low = jnp.where(lane > 0, turn(main, 1), turn(end, 1))
        high = jnp.where(lane < LANES - 1, turn(main, -1), turn(end, -1))
        return [low, high]

    own, beyond = faces(LX, LY)
    found, found_end = {}, {}
    for cell in beyond + own:
        here, end = values.fine(*cell), values.fine_end(*cell)
        around = [values.fine(*other) for other in neighbours(*cell)] + zs(here, end)
        part = smooth_tile(weights.fine(*cell), here, around)
        found[cell] = part + to_fine[cell[0] // 2, cell[1] // 2]
    for cell in own:
        here, end = values.fine(*cell), values.fine_end(*cell)
        around = [values.fine_end(*other) for other in neighbours(*cell)] + zs(end, here)
        part = smooth_tile(weights.fine_end(*cell), end, around)
        found_end[cell] = part + to_end[cell[0] // 2, cell[1] // 2]
    basis_ref[: 2 * VECS] = xp_ref[...]
    basis_ref[3 * VECS : 4 * VECS] = jnp.zeros((VECS, FINE * LANES), F32)
    basis_ref[4 * VECS : 6 * VECS] = axp_ref[...]
    for cell in own:
        k = cell[0] * LY + cell[1]
        here = found[cell]
        factors = tile(cf, k)
        around = [found[other] for other in neighbours(*cell)] + zs(here, found_end[cell])
        applied = factors[6:7] * here - spread(factors, around)
        columns = slice(k * LANES, (k + 1) * LANES)
        wa_ref[:VECS, columns] = here
        wa_ref[VECS:, columns] = applied
        basis_ref[2 * VECS : 3 * VECS, columns] = here
        basis_ref[6 * VECS : 7 * VECS, columns] = applied
    pair = dot(basis_ref[: 3 * VECS], basis_ref[...], (1, 1))
    gram[...] = jnp.concatenate([pair, jnp.zeros((3 * VECS, VECS), F32)], axis=1)


def combine(coefficients, xp_ref, wa_ref, axp_ref):
    lane = lanes_of(VECS)
    both = stack([coefficients, jnp.where(lane >= VECS, coefficients, 0.0)])[:, : 3 * VECS]
    search = stack([xp_ref[...], wa_ref[:VECS]])
    moved = dot(both, search)
    if axp_ref is None:
        return moved, None
    applied = stack([axp_ref[...], wa_ref[VECS:]])
    return moved, dot(both, applied)


def third_kernel(summed, xp_ref, axp_ref, wa_ref, cf, cm, cc, nxp, naxp, ef, em, ec, zr, zl):
    coefficients, projected = ritz(summed[...])
    moved, applied = combine(coefficients, xp_ref, wa_ref, axp_ref)
    nxp[...] = moved
    naxp[...] = applied
    level_parts(moved[:VECS], applied[:VECS], projected, cf, cm, cc, ef, em, ec)
    pack_z(ef, em, ec, cf, cm, cc, zr, zl)


def last_kernel(summed, xp_ref, wa_ref, x_out, p_out):
    coefficients, _ = ritz(summed[...])
    moved, _ = combine(coefficients, xp_ref, wa_ref, None)
    for k in range(FINE):
        columns = slice(k * LANES, (k + 1) * LANES)
        x_out[pl.ds(k, VECS, stride=FINE), :] = moved[:VECS, columns]
        p_out[pl.ds(k, VECS, stride=FINE), :] = moved[VECS:, columns]


def shifted(values, axis, by):
    peers = lax.axis_size(axis)
    return lax.ppermute(values, axis, [(i, (i + by) % peers) for i in range(peers)])


def all_sum(values):
    bit = 1
    while bit < max(lax.axis_size(axis) for axis in ("gy", "gx", "gz")):
        for axis in ("gy", "gx", "gz"):
            peers = lax.axis_size(axis)
            if bit < peers:
                values = values + lax.ppermute(values, axis, [(i, i ^ bit) for i in range(peers)])
        bit *= 2
    return values


def exchange(parts, weights, zr, zl):
    rows = zr.shape[0]
    ec = parts[2]
    zr, zl = shifted(zr, "gz", 1), shifted(zl, "gz", -1)
    y2u, y2d = shifted(ec, "gy", 2), shifted(ec, "gy", -2)
    yu, yd = run(pack_y_kernel, [(rows, 27 * LANES)] * 2, (*parts, *weights, zr, zl))
    yu, yd = shifted(yu, "gy", 1), shifted(yd, "gy", -1)
    xu, xd = run(pack_x_kernel, [(rows, 21 * LANES)] * 2, (*parts, *weights, zr, zl, yu, yd, y2u, y2d))
    xu, xd = shifted(xu, "gx", 1), shifted(xd, "gx", -1)
    return (zr, zl, yu, yd, xu, xd), (y2u, y2d)


def on_device(x_block, p_block, voxel_class, conductance):
    sizes = [lax.axis_size(axis) for axis in ("gx", "gy", "gz")]
    all_cells = FINE * LANES * sizes[0] * sizes[1] * sizes[2]
    wide = FINE * LANES
    flags = []
    for axis, size in zip(("gx", "gy", "gz"), sizes):
        at = lax.axis_index(axis)
        flags += [at > 0, at < size - 1]
    flags = jnp.stack(flags).astype(F32)
    field, zr, zl, yu, yd, xu, xd = run(
        start_kernel,
        [(40, wide)] + [(40, LANES)] * 2 + [(40, LX * LANES)] * 2 + [(40, LY * LANES)] * 2,
        (
            x_block.reshape(VECS * FINE, LANES),
            p_block.reshape(VECS * FINE, LANES),
            voxel_class.reshape(FINE, LANES),
        ),
        (conductance,),
    )
    arrived = (
        shifted(zr, "gz", 1), shifted(zl, "gz", -1), shifted(yu, "gy", 1),
        shifted(yd, "gy", -1), shifted(xu, "gx", 1), shifted(xd, "gx", -1),
    )
    fields = [(2 * VECS, wide)] * 2
    weight_shapes = [(8, wide), (8, MIDDLE * LANES), (8, COARSE * LANES)]
    xp, axp, cf, cm, cc, gram = run(
        first_kernel, fields + weight_shapes + [(VECS, LANES)], (field, *arrived), (flags,)
    )
    weights = (cf, cm, cc)
    part_shapes = [(VECS, wide), (VECS, MIDDLE * LANES), (VECS, COARSE * LANES)]
    gram = all_sum(gram) * (1.0 / all_cells)
    rows = VECS + 8
    *parts, zr, zl = run(
        second_kernel, part_shapes + [(rows, LANES)] * 2, (gram, xp, axp, *weights)
    )
    sent_weights = None
    for iteration in range(ITERS):
        sent, far = exchange(parts, weights, zr, zl)
        if sent_weights is None:
            sent_weights = sent
        wa, gram = search(xp, axp, parts, weights, sent, far, sent_weights, wide)
        gram = all_sum(gram) * (1.0 / all_cells)
        if iteration < ITERS - 1:
            xp, axp, *parts, zr, zl = run(
                third_kernel,
                fields + part_shapes + [(VECS, LANES)] * 2,
                (gram, xp, axp, wa, *weights),
            )
    x_out, p_out = run(last_kernel, [(VECS * FINE, LANES)] * 2, (gram, xp, wa))
    return (x_out.reshape(x_block.shape), p_out.reshape(x_block.shape))


def search(xp, axp, parts, weights, sent, far, sent_weights, wide):
    inputs = (xp, axp, *parts, *weights, *sent, *far, *sent_weights)
    return pl.pallas_call(
        search_kernel,
        out_shape=[SHAPE((2 * VECS, wide), F32), SHAPE((3 * VECS, LANES), F32)],
        in_specs=[pl.BlockSpec(memory_space=pltpu.VMEM)] * len(inputs),
        out_specs=[pl.BlockSpec(memory_space=pltpu.VMEM)] * 2,
        scratch_shapes=[pltpu.VMEM((7 * VECS, wide), F32)],
        compiler_params=pltpu.CompilerParams(vmem_limit_bytes=GRANT),
        interpret=INTERPRET,
    )(*inputs)


def solution(mesh):
    in_specs = (P(None, "gx", "gy", "gz"), P(None, "gx", "gy", "gz"), P("gx", "gy", "gz"), P())
    out_specs = (P(None, "gx", "gy", "gz"), P(None, "gx", "gy", "gz"))
    return jax.shard_map(
        on_device, mesh=mesh, in_specs=in_specs, out_specs=out_specs, check_vma=False
    )
```

```python
import jax
import jax.numpy as jnp
from jax import lax
from jax.experimental import pallas as pl
from jax.experimental.pallas import tpu as pltpu
from jax.sharding import PartitionSpec as P

VECS = 16
CLASSES = 8
ITERS = 2
INNER = 4
INTERPRET = False
GRANT = 24 * 1024 * 1024
PAIR = 2 * VECS
KEEP = 0.02

jacobi_weight = 2.0 / 3.0
mass_shift = 0.05

LX, LY, LANES = 8, 4, 128
MX, MY = LX // 2, LY // 2
CX, CY = LX // 4, LY // 4
FINE, MIDDLE, COARSE = LX * LY, MX * MY, CX * CY
SHAPE = jax.ShapeDtypeStruct
F32 = jnp.float32
HALF = LANES // 2


def tile(ref, index, rows=slice(None)):
    return ref[rows, index * LANES : (index + 1) * LANES]


def lanes_of(rows=8):
    return lax.broadcasted_iota(jnp.int32, (rows, LANES), 1)


def rows_of(rows):
    return lax.broadcasted_iota(jnp.int32, (rows, LANES), 0)


def turn(value, shift):
    shift = shift % LANES
    return value if shift == 0 else pltpu.roll(value, shift, 1)


def dot(left, right, contract=(1, 0)):
    return lax.dot_general(
        left,
        right,
        (((contract[0],), (contract[1],)), ((), ())),
        precision=lax.Precision.HIGHEST,
        preferred_element_type=F32,
    )


def pair_matrix(transposed):
    wide = lax.broadcasted_iota(jnp.int32, (LANES, LANES), 1 if transposed else 0)
    narrow = lax.broadcasted_iota(jnp.int32, (LANES, LANES), 0 if transposed else 1)
    return jnp.where(wide // 2 == narrow, 1.0, 0.0).astype(F32)


def stack(values):
    return jnp.concatenate(values, axis=0)


def run(body, outs, vmem, smem=(), scratch=()):
    in_specs = [pl.BlockSpec(memory_space=pltpu.SMEM)] * len(smem)
    in_specs += [pl.BlockSpec(memory_space=pltpu.VMEM)] * len(vmem)
    return pl.pallas_call(
        body,
        out_shape=[SHAPE(shape, F32) for shape in outs],
        in_specs=in_specs,
        out_specs=[pl.BlockSpec(memory_space=pltpu.VMEM)] * len(outs),
        scratch_shapes=[pltpu.VMEM(shape, F32) for shape in scratch],
        compiler_params=pltpu.CompilerParams(vmem_limit_bytes=GRANT),
        interpret=INTERPRET,
    )(*smem, *vmem)


def start_kernel(cond_ref, x_ref, p_ref, class_ref, field_ref, zr, zl, yu, yd, xu, xd):
    classes = class_ref[...]
    local = jnp.zeros(classes.shape, F32)
    for index in range(CLASSES):
        local = local + jnp.where(classes == index, cond_ref[index], 0.0)
    lane = lanes_of(40)
    right = jnp.zeros((40, LANES), F32)
    left = jnp.zeros((40, LANES), F32)
    for x in range(LX):
        for y in range(LY):
            p = x * LY + y
            cell = stack(
                [
                    x_ref[pl.ds(p, VECS, stride=FINE), :],
                    p_ref[pl.ds(p, VECS, stride=FINE), :],
                    jnp.broadcast_to(local[p : p + 1], (8, LANES)),
                ]
            )
            field_ref[:, p * LANES : (p + 1) * LANES] = cell
            right = jnp.where(lane == p, turn(cell, p + 1), right)
            left = jnp.where(lane == p, turn(cell, p), left)
            if y == LY - 1:
                yu[:, x * LANES : (x + 1) * LANES] = cell
            if y == 0:
                yd[:, x * LANES : (x + 1) * LANES] = cell
            if x == LX - 1:
                xu[:, y * LANES : (y + 1) * LANES] = cell
            if x == 0:
                xd[:, y * LANES : (y + 1) * LANES] = cell
    zr[...] = right
    zl[...] = left


def finish_weights(weights, shift_term):
    row = rows_of(8)
    weights = jnp.where(row < 6, weights, 0.0)
    diagonal = shift_term + jnp.sum(weights, axis=0, keepdims=True)
    return jnp.where(
        row < 6, weights, jnp.where(row == 6, diagonal, jacobi_weight / diagonal)
    )


def coarsen_weights(fine, size_x, size_y, shift_term, halve):
    row, lane = rows_of(8), lanes_of(8)
    sums = []
    for x in range(size_x):
        for y in range(size_y):
            total = jnp.zeros((8, LANES), F32)
            for i in range(2):
                for j in range(2):
                    keep = (row == i) | (row == 2 + j)
                    keep = keep | ((row == 4) & (lane % 2 == 0)) | ((row == 5) & (lane % 2 == 1))
                    total = total + jnp.where(keep, fine[2 * x + i, 2 * y + j], 0.0)
            sums.append(total)
    paired = dot(stack(sums), halve)
    return {
        (k // size_y, k % size_y): finish_weights(paired[8 * k : 8 * k + 8], shift_term)
        for k in range(size_x * size_y)
    }


def first_kernel(flag_ref, field_ref, zr, zl, yu, yd, xu, xd, xp_ref, axp_ref, cf, cm, cc, ef, em, ec, szr, szl):
    lane, row = lanes_of(8), rows_of(8)
    lane40 = lanes_of(40)
    from_low, from_high = zr[...], zl[...]
    flags = [flag_ref[k] for k in range(6)]
    ends = jnp.where((row == 4) & (lane == 0), flags[4], 1.0)
    ends = jnp.where((row == 5) & (lane == LANES - 1), flags[5], ends)
    fine = {}
    for x in range(LX):
        for y in range(LY):
            p = x * LY + y
            here = tile(field_ref, p)
            beside = [
                tile(field_ref, p - LY) if x > 0 else tile(xu, y),
                tile(field_ref, p + LY) if x < LX - 1 else tile(xd, y),
                tile(field_ref, p - 1) if y > 0 else tile(yu, x),
                tile(field_ref, p + 1) if y < LY - 1 else tile(yd, x),
                jnp.where(lane40 == 0, turn(from_low, -p), turn(here, 1)),
                jnp.where(lane40 == LANES - 1, turn(from_high, LANES - 1 - p), turn(here, -1)),
            ]
            around = stack([value[32:33] for value in beside] + [here[32:34]])
            own = here[32:40]
            keep = ends
            for side, at_end in enumerate((x == 0, x == LX - 1, y == 0, y == LY - 1)):
                if at_end:
                    keep = jnp.where(row == side, flags[side], keep)
            weights = finish_weights(2.0 * around * own / (around + own) * keep, mass_shift)
            fine[x, y] = weights
            cf[:, p * LANES : (p + 1) * LANES] = weights
            applied = weights[6:7] * here[:32]
            for side in range(6):
                applied = applied - weights[side : side + 1] * beside[side][:32]
            xp_ref[:, p * LANES : (p + 1) * LANES] = here[:32]
            axp_ref[:, p * LANES : (p + 1) * LANES] = applied
    halve = pair_matrix(False)
    middle = coarsen_weights(fine, MX, MY, 8.0 * mass_shift, halve)
    for (x, y), value in middle.items():
        k = x * MY + y
        cm[:, k * LANES : (k + 1) * LANES] = value
    coarse = coarsen_weights(middle, CX, CY, 64.0 * mass_shift, halve)
    for (x, y), value in coarse.items():
        cc[:, x * LANES : (x + 1) * LANES] = value
    level_parts(stack([xp_ref[:VECS], axp_ref[:VECS]]), cf, cm, cc, ef, em, ec)
    pack_z(ef, em, ec, cf, cm, cc, szr, szl)


def eliminate(rows, size, full):
    tiles = [rows[8 * i : 8 * i + 8] for i in range(rows.shape[0] // 8)]
    row = rows_of(8)
    kept = list(tiles)
    nothing = rows[:8] * 0.0
    for k in range(0, size, 2):
        at, sub = divmod(k, 8)
        spread_left = tiles[at][:, k : k + 1] + nothing
        spread_right = tiles[at][:, k + 1 : k + 2] + nothing

        def line(value, which):
            return jnp.broadcast_to(value[sub + which : sub + which + 1], (8, LANES))

        first, second = line(tiles[at], 0), line(tiles[at], 1)
        a, b = line(spread_left, 0), line(spread_right, 0)
        c, d = line(spread_left, 1), line(spread_right, 1)
        crossed = a * second - c * first
        inverse = 1.0 / (a * d - b * c)
        solved_first = (d * first - b * second) * inverse
        solved_second = crossed * inverse
        if not full:
            kept[at] = jnp.where(row == sub, first * (1.0 / jnp.sqrt(a)), kept[at])
            root = jnp.sqrt(inverse) * (1.0 / jnp.sqrt(a))
            kept[at] = jnp.where(row == sub + 1, crossed * root, kept[at])
        for i in range(len(tiles)):
            if i < at and not full:
                continue
            if i == at:
                left, right = spread_left, spread_right
            else:
                left, right = tiles[i][:, k : k + 1], tiles[i][:, k + 1 : k + 2]
            changed = tiles[i] - (left * solved_first + right * solved_second)
            if i == at:
                changed = jnp.where(row == sub, solved_first, changed)
                changed = jnp.where(row == sub + 1, solved_second, changed)
            tiles[i] = changed
    return stack(tiles if full else kept)


def lower_pad(matrix):
    missing = LANES - matrix.shape[0]
    return stack([matrix, jnp.zeros((missing, LANES), F32)])


def solve_projected(gram, cross):
    lane = lanes_of(VECS)
    on_diagonal = jnp.where((lane == rows_of(VECS)) & (lane < VECS), gram, 0.0)
    column = 1.0 / jnp.sqrt(jnp.sum(on_diagonal, axis=1, keepdims=True))
    across = jnp.sum(on_diagonal, axis=0, keepdims=True)
    across = jnp.where(lanes_of(1) < VECS, 1.0 / jnp.sqrt(across), 0.0)
    both = jnp.where(lane < HALF, gram * across, turn(cross, HALF)) * column
    return turn(eliminate(both, VECS, True), HALF) * column


def ritz(summed):
    size = 3 * VECS
    lane, row = lanes_of(size), rows_of(size)
    sym_b, sym_a = symmetric(summed)
    on_diagonal = jnp.where(lane == row, sym_b, 0.0)
    column = 1.0 / jnp.sqrt(jnp.sum(on_diagonal, axis=1, keepdims=True))
    across = jnp.sum(on_diagonal, axis=0, keepdims=True)
    across = jnp.where(lanes_of(1) < size, 1.0 / jnp.sqrt(across), 0.0)
    normed_b = sym_b * column * across
    normed_a = sym_a * column * across
    done = eliminate(jnp.where(lane < HALF, normed_a, turn(normed_b, HALF)), size, True)
    step = jnp.where(lane < size, turn(done, HALF), 0.0)
    weighed = dot(normed_b[:, :size], step)
    step_pad, weighed_pad = lower_pad(step), lower_pad(weighed)
    step_flipped, weighed_flipped = step_pad.T, weighed_pad.T
    short_lane = lanes_of(VECS)
    basis = None
    for inner_step in range(INNER):
        if basis is None:
            mapped, product = step_flipped[:VECS], weighed_flipped[:VECS]
        else:
            mapped = dot(basis, step_pad, (1, 1))
            product = dot(basis, weighed_pad, (1, 1))
        square = dot(product, lower_pad(mapped), (1, 1))
        done = eliminate(jnp.where(short_lane < HALF, square, turn(mapped, HALF)), VECS, False)
        basis = jnp.where(short_lane < size, turn(done, HALF), 0.0)
    cross = dot(dot(basis, lower_pad(normed_a), (1, 1)), lower_pad(basis), (1, 1))
    return basis * across, cross


def level_parts(residual, cf, cm, cc, ef, em, ec):
    count = residual.shape[0]
    halve = pair_matrix(False)
    sums = []
    for mx in range(MX):
        for my in range(MY):
            total = jnp.zeros((count, LANES), F32)
            for i in range(2):
                for j in range(2):
                    p = (2 * mx + i) * LY + 2 * my + j
                    part = residual[:, p * LANES : (p + 1) * LANES]
                    total = total + part
                    ef[:, p * LANES : (p + 1) * LANES] = part * tile(cf, p, slice(7, 8))
            sums.append(total)
    paired = dot(stack(sums), halve)
    middle = [paired[count * k : count * (k + 1)] for k in range(MIDDLE)]
    for k in range(MIDDLE):
        em[:, k * LANES : (k + 1) * LANES] = middle[k] * tile(cm, k, slice(7, 8))
    sums = []
    for cx in range(CX):
        sums.append(sum(middle[(2 * cx + i) * MY + j] for i in range(2) for j in range(2)))
    paired = dot(stack(sums), halve)
    for k in range(COARSE):
        coarse = paired[count * k : count * (k + 1)]
        ec[:, k * LANES : (k + 1) * LANES] = coarse * tile(cc, k, slice(7, 8))


def pack_z(ef, em, ec, cf, cm, cc, zr, zl):
    rows = zr.shape[0]
    lane = lanes_of(rows)

    def cell(values, weights, k):
        here = tile(values, k)
        return stack([here, tile(weights, k)]) if rows > values.shape[0] else here

    right = jnp.zeros((rows, LANES), F32)
    left = jnp.zeros((rows, LANES), F32)
    levels = ((ef, cf, FINE, 0, 126), (em, cm, MIDDLE, 64, 62), (ec, cc, COARSE, 80, 30))
    for values, weights, count, base, last in levels:
        for k in range(count):
            here = cell(values, weights, k)
            spot = base + 2 * k
            right = jnp.where(lane // 2 == spot // 2, turn(here, spot - last), right)
            left = jnp.where(lane // 2 == spot // 2, turn(here, spot), left)
    zr[...] = right
    zl[...] = left


class Level:
    def __init__(
        self, own, low, high, rows, count, yu=None, yd=None, xu=None, xd=None,
        y2u=None, y2d=None, inner=slice(None),
    ):
        self.own, self.rows, self.inner = own, rows, inner
        self.low, self.high = low[rows], high[rows]
        self.yu, self.yd, self.xu, self.xd, self.y2u, self.y2d = yu, yd, xu, xd, y2u, y2d
        self.lane = lanes_of(count)
        self.kept = {}

    def once(self, key, make):
        if key not in self.kept:
            self.kept[key] = make()
        return self.kept[key]

    def own_rows(self, ref, k):
        if isinstance(ref, tuple):
            return stack([tile(part, k) for part in ref])
        return tile(ref, k, self.inner)

    def fine(self, x, y):
        if 0 <= x < LX and 0 <= y < LY:
            return self.own_rows(self.own[0], x * LY + y)
        if 0 <= x < LX:
            return tile(self.yu, 2 * x + y + 2, self.rows) if y < 0 else tile(self.yd, 2 * x + y - LY, self.rows)
        ref, near = (self.xu, x == -1) if x < 0 else (self.xd, x == LX)
        return tile(ref, y + 1 if near else 6 + y, self.rows)

    def fine_end(self, x, y):
        def make():
            if 0 <= x < LX and 0 <= y < LY:
                p = x * LY + y
                return jnp.where(
                    self.lane < HALF, turn(self.high, -2 * p), turn(self.low, 126 - 2 * p)
                )
            if 0 <= x < LX:
                return turn(tile(self.yu if y < 0 else self.yd, 16, self.rows), -(1 + 2 * x))
            return turn(tile(self.xu if x < 0 else self.xd, 10, self.rows), -(1 + 2 * y))

        return self.once(("end", x, y), make)

    def middle(self, x, y):
        def make():
            if 0 <= x < MX and 0 <= y < MY:
                k = x * MY + y
                beyond = jnp.where(
                    self.lane < 96, turn(self.high, -2 * k), turn(self.low, 62 - 2 * k)
                )
                return jnp.where(self.lane < 64, self.own_rows(self.own[1], k), beyond)
            if 0 <= x < MX:
                return tile(self.yu, 17 + MY * x + y + MY, self.rows) if y < 0 else tile(
                    self.yd, 17 + MY * x + y - MY, self.rows
                )
            ref, near = (self.xu, x == -1) if x < 0 else (self.xd, x == MX)
            return tile(ref, 12 + y if near else 15 + y, self.rows)

        return self.once(("middle", x, y), make)

    def coarse(self, x, y):
        def make():
            if 0 <= x < CX and y == 0:
                beyond = jnp.where(
                    self.lane < 64, turn(self.high, -48 - 2 * x), turn(self.low, 46 - 2 * x)
                )
                return jnp.where(self.lane < 32, self.own_rows(self.own[2], x), beyond)
            if 0 <= x < CX:
                if abs(y) == 2:
                    return tile(self.y2u if y < 0 else self.y2d, x, self.inner)
                return tile(self.yu if y < 0 else self.yd, 25 + x, self.rows)
            ref, near = (self.xu, x == -1) if x < 0 else (self.xd, x == CX)
            return tile(ref, 18 + y if near else 20, self.rows)

        return self.once(("coarse", x, y), make)


def put(ref, index, value):
    ref[:, index * LANES : (index + 1) * LANES] = value


def pack_ends(values):
    rows = values[0].shape[0]
    lane = lanes_of(rows)
    packed = jnp.zeros((rows, LANES), F32)
    for k, value in enumerate(values):
        packed = jnp.where(lane // 2 == k, turn(value, 1 + 2 * k), packed)
    return packed


def owns(refs, rows):
    ef, em, ec, cf, cm, cc = refs
    return ((ef, cf), (em, cm), (ec, cc)) if rows > ef.shape[0] else (ef, em, ec)


def pack_y_kernel(ef, em, ec, cf, cm, cc, zr, zl, yu, yd):
    rows = zr.shape[0]
    level = Level(owns((ef, em, ec, cf, cm, cc), rows), zr, zl, slice(0, rows), rows)
    for ref, first, edge in ((yu, LY - 2, LY - 1), (yd, 0, 0)):
        for x in range(LX):
            for j in range(2):
                put(ref, 2 * x + j, level.fine(x, first + j))
        put(ref, 16, pack_ends([level.fine_end(x, edge) for x in range(LX)]))
        for x in range(MX):
            for y in range(MY):
                put(ref, 17 + MY * x + y, level.middle(x, y))
        for x in range(CX):
            put(ref, 25 + x, level.coarse(x, 0))


def pack_x_kernel(ef, em, ec, cf, cm, cc, zr, zl, ryu, ryd, y2u, y2d, xu, xd):
    rows = zr.shape[0]
    level = Level(owns((ef, em, ec, cf, cm, cc), rows), zr, zl, slice(0, rows), rows, ryu, ryd)
    for ref, up in ((xu, True), (xd, False)):
        near, far = (LX - 1, LX - 2) if up else (0, 1)
        for y in range(-1, LY + 1):
            put(ref, y + 1, level.fine(near, y))
        for y in range(LY):
            put(ref, 6 + y, level.fine(far, y))
        put(ref, 10, pack_ends([level.fine_end(near, y) for y in range(LY)]))
        near, far = (MX - 1, MX - 2) if up else (0, 1)
        for y in range(-1, MY + 1):
            put(ref, 12 + y, level.middle(near, y))
        for y in range(MY):
            put(ref, 15 + y, level.middle(far, y))
        near, far = (CX - 1, CX - 2) if up else (0, 1)
        for y in range(-1, 2):
            put(ref, 18 + y, level.coarse(near, y))
        put(ref, 20, level.coarse(far, 0))


def faces(size_x, size_y):
    own = [(x, y) for x in range(size_x) for y in range(size_y)]
    beyond = [(x, y) for x in (-1, size_x) for y in range(size_y)]
    beyond += [(x, y) for x in range(size_x) for y in (-1, size_y)]
    return own, beyond


def neighbours(x, y):
    return ((x - 1, y), (x + 1, y), (x, y - 1), (x, y + 1))


def spread(weights, values):
    total = weights[0:1] * values[0]
    for side in range(1, 6):
        total = total + weights[side : side + 1] * values[side]
    return total


def smooth_tile(weights, here, values):
    return (2.0 * jacobi_weight) * here + weights[7:8] * spread(weights, values)


def gram_of(basis_ref, size):
    width = 4 * LANES

    def add(step, total):
        columns = pl.ds(pl.multiple_of(step * width, width), width)
        return total + dot(basis_ref[:size, columns], basis_ref[:, columns], (1, 1))

    return lax.fori_loop(0, FINE * LANES // width, add, jnp.zeros((size, LANES), F32))


def search_kernel(
    xp_ref, axp_ref, ef, em, ec, cf, cm, cc,
    zr, zl, yu, yd, xu, xd, y2u, y2d,
    wzr, wzl, wyu, wyd, wxu, wxd,
    wa_ref, gram, basis_ref,
):
    size = PAIR + ef.shape[0]
    basis_ref[:PAIR] = xp_ref[...]
    basis_ref[HALF : HALF + PAIR] = axp_ref[...]
    if size < HALF:
        blank = jnp.zeros((HALF - size, FINE * LANES), F32)
        basis_ref[size:HALF] = blank
        basis_ref[HALF + size :] = blank

    def rows_at(start, step):
        return pl.ds(pl.multiple_of(start + step * VECS, VECS), VECS)

    def block(step, carry):
        rows = rows_at(0, step)
        values = Level(
            (ef, em, ec), zr, zl, rows, VECS, yu, yd, xu, xd, y2u, y2d, rows
        )
        weights = Level(
            (cf, cm, cc), wzr, wzl, slice(PAIR, PAIR + 8), 8, wyu, wyd, wxu, wxd
        )
        targets = (
            (wa_ref, rows, rows_at(ef.shape[0], step)),
            (basis_ref, rows_at(PAIR, step), rows_at(HALF + PAIR, step)),
        )
        smooth_block(values, weights, cf, targets)
        return carry

    if size == 3 * VECS:
        block(0, 0)
    else:
        lax.fori_loop(0, (size - PAIR) // VECS, block, 0)
    gram[...] = gram_of(basis_ref, size)


def smooth_block(values, weights, cf, targets):
    lane = lanes_of(VECS)
    double = pair_matrix(True)

    own, beyond = faces(CX, CY)
    coarse_cells = own + beyond
    smoothed = []
    for cell in coarse_cells:
        here = values.coarse(*cell)
        around = [values.coarse(*other) for other in neighbours(*cell)]
        around += [turn(here, 1), turn(here, -1)]
        smoothed.append(smooth_tile(weights.coarse(*cell), here, around))
    doubled = dot(stack(smoothed), double)
    to_middle = {}
    for k, cell in enumerate(coarse_cells):
        ends = jnp.where(lane < 96, turn(smoothed[k], 32), smoothed[k])
        inner = doubled[VECS * k : VECS * (k + 1)]
        to_middle[cell] = jnp.where(lane < 64, inner, ends)

    own, beyond = faces(MX, MY)
    middle_cells = own + beyond
    smoothed = []
    for cell in middle_cells:
        here = values.middle(*cell)
        around = [values.middle(*other) for other in neighbours(*cell)]
        around += [turn(here, 1), turn(here, -1)]
        part = smooth_tile(weights.middle(*cell), here, around)
        smoothed.append(part + to_middle[cell[0] // 2, cell[1] // 2])
    doubled = dot(stack(smoothed), double)
    to_fine, to_end = {}, {}
    for k, cell in enumerate(middle_cells):
        to_fine[cell] = doubled[VECS * k : VECS * (k + 1)]
        to_end[cell] = jnp.where(lane < HALF, turn(smoothed[k], 64), smoothed[k])

    def zs(main, end):
        low = jnp.where(lane > 0, turn(main, 1), turn(end, 1))
        high = jnp.where(lane < LANES - 1, turn(main, -1), turn(end, -1))
        return [low, high]

    own, beyond = faces(LX, LY)
    found, found_end = {}, {}
    for cell in beyond + own:
        here, end = values.fine(*cell), values.fine_end(*cell)
        around = [values.fine(*other) for other in neighbours(*cell)] + zs(here, end)
        part = smooth_tile(weights.fine(*cell), here, around)
        found[cell] = part + to_fine[cell[0] // 2, cell[1] // 2]
    for cell in own:
        here, end = values.fine(*cell), values.fine_end(*cell)
        around = [values.fine_end(*other) for other in neighbours(*cell)] + zs(end, here)
        part = smooth_tile(weights.fine_end(*cell), end, around)
        found_end[cell] = part + to_end[cell[0] // 2, cell[1] // 2]
    for cell in own:
        k = cell[0] * LY + cell[1]
        here = found[cell]
        factors = tile(cf, k)
        around = [found[other] for other in neighbours(*cell)] + zs(here, found_end[cell])
        applied = factors[6:7] * here - spread(factors, around)
        columns = slice(k * LANES, (k + 1) * LANES)
        for ref, first, second in targets:
            ref[first, columns] = here
            ref[second, columns] = applied


def symmetric(summed):
    size = summed.shape[0]
    lane = lanes_of(size)
    flipped = lower_pad(summed).T
    sym_b = 0.5 * (summed + flipped[:size])
    sym_a = 0.5 * (turn(summed, HALF) + flipped[HALF : HALF + size])
    return jnp.where(lane < size, sym_b, 0.0), jnp.where(lane < size, sym_a, 0.0)


def judge_kernel(summed, gram, change, flag):
    size = 3 * VECS
    sym_b, sym_a = symmetric(summed[...])
    lane, row = lanes_of(VECS), rows_of(VECS)
    projected = solve_projected(
        jnp.where(lane < VECS, sym_b[:VECS], 0.0), jnp.where(lane < VECS, sym_a[:VECS], 0.0)
    )
    projected = jnp.where(lane < VECS, projected, 0.0)
    backward = turn(lower_pad(projected).T[:VECS], PAIR)
    direct = jnp.where(lanes_of(PAIR) == rows_of(PAIR), 1.0, 0.0).astype(F32)
    tail = jnp.where(lane == row + 3 * VECS, 1.0, 0.0).astype(F32) - backward
    mixing = stack([direct, tail])
    padded = lower_pad(mixing)
    small_b = dot(dot(mixing[:, :HALF], sym_b), padded, (1, 1))
    small_a = dot(dot(mixing[:, :HALF], sym_a), padded, (1, 1))
    gram[...] = jnp.where(lanes_of(size) < HALF, small_b, turn(small_a, HALF))
    change[...] = mixing
    lost = jnp.zeros((VECS, 1), F32)
    for small, full in ((small_b, sym_b), (small_a, sym_a)):
        after = jnp.where(lane == row + PAIR, small[PAIR:], 0.0)
        before = jnp.where(lane == row + 3 * VECS, full[3 * VECS :], 0.0)
        after = jnp.sum(after, axis=1, keepdims=True)
        before = jnp.sum(before, axis=1, keepdims=True)
        lost = jnp.maximum(lost, jnp.where(after > KEEP * before, 0.0, 1.0))
    flag[...] = jnp.broadcast_to(jnp.max(lost, axis=0, keepdims=True), (8, LANES))


def combine(coefficients, change, sources, targets):
    lane = lanes_of(VECS)
    both = stack([coefficients, jnp.where(lane >= VECS, coefficients, 0.0)])
    if change is not None:
        both = dot(both[:, : 3 * VECS], change)
    count = sources[0][1].stop - sources[0][1].start
    both = both[:, : PAIR + count]
    width = 8 * LANES

    def part(step, carry):
        columns = pl.ds(pl.multiple_of(step * width, width), width)
        for (old, rows, found), target in zip(sources, targets):
            target[:, columns] = dot(both, stack([old[:, columns], found[rows, columns]]))
        return carry

    lax.fori_loop(0, FINE * LANES // width, part, 0)


def mixed_kernel(
    gram, change, xp_ref, axp_ref, wa_ref, cf, cm, cc, nxp, naxp, ef, em, ec, zr, zl
):
    coefficients, projected = ritz(gram[...])
    own, applied = slice(0, PAIR), slice(PAIR, 2 * PAIR)
    sources = ((xp_ref, own, wa_ref), (axp_ref, applied, wa_ref))
    combine(coefficients, change[...], sources, (nxp, naxp))
    residual = naxp[:VECS] - dot(projected[:, :VECS], nxp[:VECS], (0, 0))
    level_parts(residual, cf, cm, cc, ef, em, ec)
    pack_z(ef, em, ec, cf, cm, cc, zr, zl)


def careful_kernel(change, xp_ref, axp_ref, wide_ref, gram, basis_ref):
    part = change[PAIR:, PAIR:HALF]
    blank = jnp.zeros((VECS, FINE * LANES), F32)
    for at, values, rows in ((0, xp_ref, slice(0, PAIR)), (HALF, axp_ref, slice(PAIR, 2 * PAIR))):
        basis_ref[at : at + PAIR] = values[...]
        basis_ref[at + PAIR : at + 3 * VECS] = dot(part, wide_ref[rows])
        basis_ref[at + 3 * VECS : at + HALF] = blank
    gram[...] = gram_of(basis_ref, 3 * VECS)


def last_kernel(summed, xp_ref, wa_ref, x_out, p_out, moved):
    coefficients, _ = ritz(summed[...])
    combine(coefficients, None, ((xp_ref, slice(0, VECS), wa_ref),), (moved,))
    for k in range(FINE):
        x_out[pl.ds(k, VECS, stride=FINE), :] = tile(moved, k, slice(0, VECS))
        p_out[pl.ds(k, VECS, stride=FINE), :] = tile(moved, k, slice(VECS, PAIR))


def shifted(values, axis, by):
    peers = lax.axis_size(axis)
    return lax.ppermute(values, axis, [(i, (i + by) % peers) for i in range(peers)])


def all_sum(values):
    bit = 1
    while bit < max(lax.axis_size(axis) for axis in ("gy", "gx", "gz")):
        for axis in ("gy", "gx", "gz"):
            peers = lax.axis_size(axis)
            if bit < peers:
                values = values + lax.ppermute(values, axis, [(i, i ^ bit) for i in range(peers)])
        bit *= 2
    return values


def exchange(parts, weights, zr, zl):
    rows = zr.shape[0]
    ec = parts[2]
    zr, zl = shifted(zr, "gz", 1), shifted(zl, "gz", -1)
    y2u, y2d = shifted(ec, "gy", 2), shifted(ec, "gy", -2)
    yu, yd = run(pack_y_kernel, [(rows, 27 * LANES)] * 2, (*parts, *weights, zr, zl))
    yu, yd = shifted(yu, "gy", 1), shifted(yd, "gy", -1)
    xu, xd = run(pack_x_kernel, [(rows, 21 * LANES)] * 2, (*parts, *weights, zr, zl, yu, yd, y2u, y2d))
    xu, xd = shifted(xu, "gx", 1), shifted(xd, "gx", -1)
    return (zr, zl, yu, yd, xu, xd), (y2u, y2d)


def on_device(x_block, p_block, voxel_class, conductance):
    sizes = [lax.axis_size(axis) for axis in ("gx", "gy", "gz")]
    all_cells = FINE * LANES * sizes[0] * sizes[1] * sizes[2]
    wide = FINE * LANES
    flags = []
    for axis, size in zip(("gx", "gy", "gz"), sizes):
        at = lax.axis_index(axis)
        flags += [at > 0, at < size - 1]
    flags = jnp.stack(flags).astype(F32)
    field, zr, zl, yu, yd, xu, xd = run(
        start_kernel,
        [(40, wide)] + [(40, LANES)] * 2 + [(40, LX * LANES)] * 2 + [(40, LY * LANES)] * 2,
        (
            x_block.reshape(VECS * FINE, LANES),
            p_block.reshape(VECS * FINE, LANES),
            voxel_class.reshape(FINE, LANES),
        ),
        (conductance,),
    )
    arrived = (
        shifted(zr, "gz", 1), shifted(zl, "gz", -1), shifted(yu, "gy", 1),
        shifted(yd, "gy", -1), shifted(xu, "gx", 1), shifted(xd, "gx", -1),
    )
    fields = [(PAIR, wide)] * 2
    weight_shapes = [(8, wide), (8, MIDDLE * LANES), (8, COARSE * LANES)]

    def part_shapes(rows):
        return [(rows, wide), (rows, MIDDLE * LANES), (rows, COARSE * LANES)]

    xp, axp, cf, cm, cc, *parts, zr, zl = run(
        first_kernel,
        fields + weight_shapes + part_shapes(PAIR) + [(PAIR + 8, LANES)] * 2,
        (field, *arrived),
        (flags,),
    )
    weights = (cf, cm, cc)
    basis = [(2 * HALF, wide)]

    def search(parts, sent, far, sent_weights):
        rows = parts[0].shape[0]
        inputs = (xp, axp, *parts, *weights, *sent, *far, *sent_weights)
        shapes = [(2 * rows, wide), (PAIR + rows, LANES)]
        return run(search_kernel, shapes, inputs, scratch=basis)

    sent_weights, far = exchange(parts, weights, zr, zl)
    wa, gram = search(parts, sent_weights, far, sent_weights)
    summed = all_sum(gram) * (1.0 / all_cells)
    small = (3 * VECS, LANES)
    gram, change, flag = run(judge_kernel, [small, small, (8, LANES)], (summed,))
    nexts = fields + part_shapes(VECS) + [(VECS, LANES)] * 2

    def careful(gram, change, wa):
        (gram,) = run(careful_kernel, [small], (change, xp, axp, wa), scratch=basis)
        return lax.psum(gram, ("gx", "gy", "gz")) * (1.0 / all_cells)

    def given(gram, change, wa):
        return gram

    gram = lax.cond(flag[0, 0] > 0.5, careful, given, gram, change, wa)
    xp, axp, *parts, zr, zl = run(mixed_kernel, nexts, (gram, change, xp, axp, wa, *weights))
    sent, far = exchange(parts, weights, zr, zl)
    wa, gram = search(parts, sent, far, sent_weights)
    gram = all_sum(gram) * (1.0 / all_cells)
    outs = [(VECS * FINE, LANES)] * 2
    x_out, p_out = run(last_kernel, outs, (gram, xp, wa), scratch=[(PAIR, wide)])
    return (x_out.reshape(x_block.shape), p_out.reshape(x_block.shape))


def solution(mesh):
    in_specs = (P(None, "gx", "gy", "gz"), P(None, "gx", "gy", "gz"), P("gx", "gy", "gz"), P())
    out_specs = (P(None, "gx", "gy", "gz"), P(None, "gx", "gy", "gz"))
    return jax.shard_map(
        on_device, mesh=mesh, in_specs=in_specs, out_specs=out_specs, check_vma=False
    )
```

```python
import jax
import jax.numpy as jnp
from jax import lax
from jax.experimental import pallas as pl
from jax.experimental.pallas import tpu as pltpu
from jax.sharding import PartitionSpec as P

VECS = 16
CLASSES = 8
ITERS = 2
INNER = 4
INTERPRET = False
GRANT = 24 * 1024 * 1024
PAIR = 2 * VECS
KEEP = 0.02

jacobi_weight = 2.0 / 3.0
mass_shift = 0.05

LX, LY, LANES = 8, 4, 128
MX, MY = LX // 2, LY // 2
CX, CY = LX // 4, LY // 4
FINE, MIDDLE, COARSE = LX * LY, MX * MY, CX * CY
SHAPE = jax.ShapeDtypeStruct
F32 = jnp.float32
HALF = LANES // 2


def tile(ref, index, rows=slice(None)):
    return ref[rows, index * LANES : (index + 1) * LANES]


def lanes_of(rows=8):
    return lax.broadcasted_iota(jnp.int32, (rows, LANES), 1)


def rows_of(rows):
    return lax.broadcasted_iota(jnp.int32, (rows, LANES), 0)


def turn(value, shift):
    shift = shift % LANES
    return value if shift == 0 else pltpu.roll(value, shift, 1)


def dot(left, right, contract=(1, 0)):
    return lax.dot_general(
        left,
        right,
        (((contract[0],), (contract[1],)), ((), ())),
        precision=lax.Precision.HIGHEST,
        preferred_element_type=F32,
    )


def pair_matrix(transposed):
    wide = lax.broadcasted_iota(jnp.int32, (LANES, LANES), 1 if transposed else 0)
    narrow = lax.broadcasted_iota(jnp.int32, (LANES, LANES), 0 if transposed else 1)
    return jnp.where(wide // 2 == narrow, 1.0, 0.0).astype(F32)


def stack(values):
    return jnp.concatenate(values, axis=0)


def run(body, outs, vmem, smem=(), scratch=()):
    in_specs = [pl.BlockSpec(memory_space=pltpu.SMEM)] * len(smem)
    in_specs += [pl.BlockSpec(memory_space=pltpu.VMEM)] * len(vmem)
    return pl.pallas_call(
        body,
        out_shape=[SHAPE(shape, F32) for shape in outs],
        in_specs=in_specs,
        out_specs=[pl.BlockSpec(memory_space=pltpu.VMEM)] * len(outs),
        scratch_shapes=[pltpu.VMEM(shape, F32) for shape in scratch],
        compiler_params=pltpu.CompilerParams(vmem_limit_bytes=GRANT),
        interpret=INTERPRET,
    )(*smem, *vmem)


def start_kernel(
    cond_ref, x_far, p_far, class_far, field_ref, zr, zl, yu, yd, xu, xd,
    x_ref, p_ref, class_ref, done,
):
    fetches = [
        pltpu.make_async_copy(far, near, done.at[k])
        for k, (far, near) in enumerate(
            ((class_far, class_ref), (x_far, x_ref), (p_far, p_ref))
        )
    ]
    for fetch in fetches:
        fetch.start()
    for fetch in fetches:
        fetch.wait()
    classes = class_ref[...]
    local = jnp.zeros(classes.shape, F32)
    for index in range(CLASSES):
        local = local + jnp.where(classes == index, cond_ref[index], 0.0)
    lane = lanes_of(40)
    right = jnp.zeros((40, LANES), F32)
    left = jnp.zeros((40, LANES), F32)
    for x in range(LX):
        for y in range(LY):
            p = x * LY + y
            cell = stack(
                [
                    x_ref[pl.ds(p, VECS, stride=FINE), :],
                    p_ref[pl.ds(p, VECS, stride=FINE), :],
                    jnp.broadcast_to(local[p : p + 1], (8, LANES)),
                ]
            )
            field_ref[:, p * LANES : (p + 1) * LANES] = cell
            right = jnp.where(lane == p, turn(cell, p + 1), right)
            left = jnp.where(lane == p, turn(cell, p), left)
            if y == LY - 1:
                yu[:, x * LANES : (x + 1) * LANES] = cell
            if y == 0:
                yd[:, x * LANES : (x + 1) * LANES] = cell
            if x == LX - 1:
                xu[:, y * LANES : (y + 1) * LANES] = cell
            if x == 0:
                xd[:, y * LANES : (y + 1) * LANES] = cell
    zr[...] = right
    zl[...] = left


def finish_weights(weights, shift_term):
    row = rows_of(8)
    weights = jnp.where(row < 6, weights, 0.0)
    diagonal = shift_term + jnp.sum(weights, axis=0, keepdims=True)
    return jnp.where(
        row < 6, weights, jnp.where(row == 6, diagonal, jacobi_weight / diagonal)
    )


def coarsen_weights(fine, size_x, size_y, shift_term, halve):
    row, lane = rows_of(8), lanes_of(8)
    sums = []
    for x in range(size_x):
        for y in range(size_y):
            total = jnp.zeros((8, LANES), F32)
            for i in range(2):
                for j in range(2):
                    keep = (row == i) | (row == 2 + j)
                    keep = keep | ((row == 4) & (lane % 2 == 0)) | ((row == 5) & (lane % 2 == 1))
                    total = total + jnp.where(keep, fine[2 * x + i, 2 * y + j], 0.0)
            sums.append(total)
    paired = dot(stack(sums), halve)
    return {
        (k // size_y, k % size_y): finish_weights(paired[8 * k : 8 * k + 8], shift_term)
        for k in range(size_x * size_y)
    }


def first_kernel(flag_ref, field_ref, zr, zl, yu, yd, xu, xd, xp_ref, axp_ref, cf, cm, cc, ef, em, ec, szr, szl):
    lane, row = lanes_of(8), rows_of(8)
    lane40 = lanes_of(40)
    from_low, from_high = zr[...], zl[...]
    flags = [flag_ref[k] for k in range(6)]
    ends = jnp.where((row == 4) & (lane == 0), flags[4], 1.0)
    ends = jnp.where((row == 5) & (lane == LANES - 1), flags[5], ends)
    fine = {}
    for x in range(LX):
        for y in range(LY):
            p = x * LY + y
            here = tile(field_ref, p)
            beside = [
                tile(field_ref, p - LY) if x > 0 else tile(xu, y),
                tile(field_ref, p + LY) if x < LX - 1 else tile(xd, y),
                tile(field_ref, p - 1) if y > 0 else tile(yu, x),
                tile(field_ref, p + 1) if y < LY - 1 else tile(yd, x),
                jnp.where(lane40 == 0, turn(from_low, -p), turn(here, 1)),
                jnp.where(lane40 == LANES - 1, turn(from_high, LANES - 1 - p), turn(here, -1)),
            ]
            around = stack([value[32:33] for value in beside] + [here[32:34]])
            own = here[32:40]
            keep = ends
            for side, at_end in enumerate((x == 0, x == LX - 1, y == 0, y == LY - 1)):
                if at_end:
                    keep = jnp.where(row == side, flags[side], keep)
            weights = finish_weights(2.0 * around * own / (around + own) * keep, mass_shift)
            fine[x, y] = weights
            cf[:, p * LANES : (p + 1) * LANES] = weights
            applied = weights[6:7] * here[:32]
            for side in range(6):
                applied = applied - weights[side : side + 1] * beside[side][:32]
            xp_ref[:, p * LANES : (p + 1) * LANES] = here[:32]
            axp_ref[:, p * LANES : (p + 1) * LANES] = applied
    halve = pair_matrix(False)
    middle = coarsen_weights(fine, MX, MY, 8.0 * mass_shift, halve)
    for (x, y), value in middle.items():
        k = x * MY + y
        cm[:, k * LANES : (k + 1) * LANES] = value
    coarse = coarsen_weights(middle, CX, CY, 64.0 * mass_shift, halve)
    for (x, y), value in coarse.items():
        cc[:, x * LANES : (x + 1) * LANES] = value
    level_parts(stack([xp_ref[:VECS], axp_ref[:VECS]]), cf, cm, cc, ef, em, ec)
    pack_z(ef, em, ec, cf, cm, cc, szr, szl)


def eliminate(rows, size, full):
    tiles = [rows[8 * i : 8 * i + 8] for i in range(rows.shape[0] // 8)]
    row = rows_of(8)
    kept = list(tiles)
    nothing = rows[:8] * 0.0
    for k in range(0, size, 2):
        at, sub = divmod(k, 8)
        spread_left = tiles[at][:, k : k + 1] + nothing
        spread_right = tiles[at][:, k + 1 : k + 2] + nothing

        def line(value, which):
            return jnp.broadcast_to(value[sub + which : sub + which + 1], (8, LANES))

        first, second = line(tiles[at], 0), line(tiles[at], 1)
        a, b = line(spread_left, 0), line(spread_right, 0)
        c, d = line(spread_left, 1), line(spread_right, 1)
        crossed = a * second - c * first
        inverse = 1.0 / (a * d - b * c)
        solved_first = (d * first - b * second) * inverse
        solved_second = crossed * inverse
        if not full:
            kept[at] = jnp.where(row == sub, first * (1.0 / jnp.sqrt(a)), kept[at])
            root = jnp.sqrt(inverse) * (1.0 / jnp.sqrt(a))
            kept[at] = jnp.where(row == sub + 1, crossed * root, kept[at])
        for i in range(len(tiles)):
            if i < at and not full:
                continue
            if i == at:
                left, right = spread_left, spread_right
            else:
                left, right = tiles[i][:, k : k + 1], tiles[i][:, k + 1 : k + 2]
            changed = tiles[i] - (left * solved_first + right * solved_second)
            if i == at:
                changed = jnp.where(row == sub, solved_first, changed)
                changed = jnp.where(row == sub + 1, solved_second, changed)
            tiles[i] = changed
    return stack(tiles if full else kept)


def lower_pad(matrix):
    missing = LANES - matrix.shape[0]
    return stack([matrix, jnp.zeros((missing, LANES), F32)])


def solve_projected(gram, cross):
    lane = lanes_of(VECS)
    on_diagonal = jnp.where((lane == rows_of(VECS)) & (lane < VECS), gram, 0.0)
    column = 1.0 / jnp.sqrt(jnp.sum(on_diagonal, axis=1, keepdims=True))
    across = jnp.sum(on_diagonal, axis=0, keepdims=True)
    across = jnp.where(lanes_of(1) < VECS, 1.0 / jnp.sqrt(across), 0.0)
    both = jnp.where(lane < HALF, gram * across, turn(cross, HALF)) * column
    return turn(eliminate(both, VECS, True), HALF) * column


def ritz(summed):
    size = 3 * VECS
    lane, row = lanes_of(size), rows_of(size)
    sym_b, sym_a = symmetric(summed)
    on_diagonal = jnp.where(lane == row, sym_b, 0.0)
    column = 1.0 / jnp.sqrt(jnp.sum(on_diagonal, axis=1, keepdims=True))
    across = jnp.sum(on_diagonal, axis=0, keepdims=True)
    across = jnp.where(lanes_of(1) < size, 1.0 / jnp.sqrt(across), 0.0)
    normed_b = sym_b * column * across
    normed_a = sym_a * column * across
    done = eliminate(jnp.where(lane < HALF, normed_a, turn(normed_b, HALF)), size, True)
    step = jnp.where(lane < size, turn(done, HALF), 0.0)
    weighed = dot(normed_b[:, :size], step)
    step_pad, weighed_pad = lower_pad(step), lower_pad(weighed)
    short_lane = lanes_of(VECS)

    def inner_step(_, basis):
        mapped = dot(basis, step_pad, (1, 1))
        product = dot(basis, weighed_pad, (1, 1))
        square = dot(product, lower_pad(mapped), (1, 1))
        done = eliminate(jnp.where(short_lane < HALF, square, turn(mapped, HALF)), VECS, False)
        return jnp.where(short_lane < size, turn(done, HALF), 0.0)

    basis = jnp.where(short_lane == rows_of(VECS), 1.0, 0.0).astype(F32)
    basis = lax.fori_loop(0, INNER, inner_step, basis)
    cross = dot(dot(basis, lower_pad(normed_a), (1, 1)), lower_pad(basis), (1, 1))
    return basis * across, cross


def level_parts(residual, cf, cm, cc, ef, em, ec):
    count = residual.shape[0]
    halve = pair_matrix(False)
    sums = []
    for mx in range(MX):
        for my in range(MY):
            total = jnp.zeros((count, LANES), F32)
            for i in range(2):
                for j in range(2):
                    p = (2 * mx + i) * LY + 2 * my + j
                    part = residual[:, p * LANES : (p + 1) * LANES]
                    total = total + part
                    ef[:, p * LANES : (p + 1) * LANES] = part * tile(cf, p, slice(7, 8))
            sums.append(total)
    paired = dot(stack(sums), halve)
    middle = [paired[count * k : count * (k + 1)] for k in range(MIDDLE)]
    for k in range(MIDDLE):
        em[:, k * LANES : (k + 1) * LANES] = middle[k] * tile(cm, k, slice(7, 8))
    sums = []
    for cx in range(CX):
        sums.append(sum(middle[(2 * cx + i) * MY + j] for i in range(2) for j in range(2)))
    paired = dot(stack(sums), halve)
    for k in range(COARSE):
        coarse = paired[count * k : count * (k + 1)]
        ec[:, k * LANES : (k + 1) * LANES] = coarse * tile(cc, k, slice(7, 8))


def pack_z(ef, em, ec, cf, cm, cc, zr, zl):
    rows = zr.shape[0]
    lane = lanes_of(rows)

    def cell(values, weights, k):
        here = tile(values, k)
        return stack([here, tile(weights, k)]) if rows > values.shape[0] else here

    right = jnp.zeros((rows, LANES), F32)
    left = jnp.zeros((rows, LANES), F32)
    levels = ((ef, cf, FINE, 0, 126), (em, cm, MIDDLE, 64, 62), (ec, cc, COARSE, 80, 30))
    for values, weights, count, base, last in levels:
        for k in range(count):
            here = cell(values, weights, k)
            spot = base + 2 * k
            right = jnp.where(lane // 2 == spot // 2, turn(here, spot - last), right)
            left = jnp.where(lane // 2 == spot // 2, turn(here, spot), left)
    zr[...] = right
    zl[...] = left


class Level:
    def __init__(
        self, own, low, high, rows, count, yu=None, yd=None, xu=None, xd=None,
        y2u=None, y2d=None, inner=slice(None),
    ):
        self.own, self.rows, self.inner = own, rows, inner
        self.low, self.high = low[rows], high[rows]
        self.yu, self.yd, self.xu, self.xd, self.y2u, self.y2d = yu, yd, xu, xd, y2u, y2d
        self.lane = lanes_of(count)
        self.kept = {}

    def once(self, key, make):
        if key not in self.kept:
            self.kept[key] = make()
        return self.kept[key]

    def own_rows(self, ref, k):
        if isinstance(ref, tuple):
            return stack([tile(part, k) for part in ref])
        return tile(ref, k, self.inner)

    def fine(self, x, y):
        if 0 <= x < LX and 0 <= y < LY:
            return self.own_rows(self.own[0], x * LY + y)
        if 0 <= x < LX:
            return tile(self.yu, 2 * x + y + 2, self.rows) if y < 0 else tile(self.yd, 2 * x + y - LY, self.rows)
        ref, near = (self.xu, x == -1) if x < 0 else (self.xd, x == LX)
        return tile(ref, y + 1 if near else 6 + y, self.rows)

    def fine_end(self, x, y):
        def make():
            if 0 <= x < LX and 0 <= y < LY:
                p = x * LY + y
                return jnp.where(
                    self.lane < HALF, turn(self.high, -2 * p), turn(self.low, 126 - 2 * p)
                )
            if 0 <= x < LX:
                return turn(tile(self.yu if y < 0 else self.yd, 16, self.rows), -(1 + 2 * x))
            return turn(tile(self.xu if x < 0 else self.xd, 10, self.rows), -(1 + 2 * y))

        return self.once(("end", x, y), make)

    def middle(self, x, y):
        def make():
            if 0 <= x < MX and 0 <= y < MY:
                k = x * MY + y
                beyond = jnp.where(
                    self.lane < 96, turn(self.high, -2 * k), turn(self.low, 62 - 2 * k)
                )
                return jnp.where(self.lane < 64, self.own_rows(self.own[1], k), beyond)
            if 0 <= x < MX:
                return tile(self.yu, 17 + MY * x + y + MY, self.rows) if y < 0 else tile(
                    self.yd, 17 + MY * x + y - MY, self.rows
                )
            ref, near = (self.xu, x == -1) if x < 0 else (self.xd, x == MX)
            return tile(ref, 12 + y if near else 15 + y, self.rows)

        return self.once(("middle", x, y), make)

    def coarse(self, x, y):
        def make():
            if 0 <= x < CX and y == 0:
                beyond = jnp.where(
                    self.lane < 64, turn(self.high, -48 - 2 * x), turn(self.low, 46 - 2 * x)
                )
                return jnp.where(self.lane < 32, self.own_rows(self.own[2], x), beyond)
            if 0 <= x < CX:
                if abs(y) == 2:
                    return tile(self.y2u if y < 0 else self.y2d, x, self.inner)
                return tile(self.yu if y < 0 else self.yd, 25 + x, self.rows)
            ref, near = (self.xu, x == -1) if x < 0 else (self.xd, x == CX)
            return tile(ref, 18 + y if near else 20, self.rows)

        return self.once(("coarse", x, y), make)


def put(ref, index, value):
    ref[:, index * LANES : (index + 1) * LANES] = value


def pack_ends(values):
    rows = values[0].shape[0]
    lane = lanes_of(rows)
    packed = jnp.zeros((rows, LANES), F32)
    for k, value in enumerate(values):
        packed = jnp.where(lane // 2 == k, turn(value, 1 + 2 * k), packed)
    return packed


def owns(refs, rows):
    ef, em, ec, cf, cm, cc = refs
    return ((ef, cf), (em, cm), (ec, cc)) if rows > ef.shape[0] else (ef, em, ec)


def pack_y_kernel(ef, em, ec, cf, cm, cc, zr, zl, yu, yd):
    rows = zr.shape[0]
    level = Level(owns((ef, em, ec, cf, cm, cc), rows), zr, zl, slice(0, rows), rows)
    for ref, first, edge in ((yu, LY - 2, LY - 1), (yd, 0, 0)):
        for x in range(LX):
            for j in range(2):
                put(ref, 2 * x + j, level.fine(x, first + j))
        put(ref, 16, pack_ends([level.fine_end(x, edge) for x in range(LX)]))
        for x in range(MX):
            for y in range(MY):
                put(ref, 17 + MY * x + y, level.middle(x, y))
        for x in range(CX):
            put(ref, 25 + x, level.coarse(x, 0))


def pack_x_kernel(ef, em, ec, cf, cm, cc, zr, zl, ryu, ryd, y2u, y2d, xu, xd):
    rows = zr.shape[0]
    level = Level(owns((ef, em, ec, cf, cm, cc), rows), zr, zl, slice(0, rows), rows, ryu, ryd)
    for ref, up in ((xu, True), (xd, False)):
        near, far = (LX - 1, LX - 2) if up else (0, 1)
        for y in range(-1, LY + 1):
            put(ref, y + 1, level.fine(near, y))
        for y in range(LY):
            put(ref, 6 + y, level.fine(far, y))
        put(ref, 10, pack_ends([level.fine_end(near, y) for y in range(LY)]))
        near, far = (MX - 1, MX - 2) if up else (0, 1)
        for y in range(-1, MY + 1):
            put(ref, 12 + y, level.middle(near, y))
        for y in range(MY):
            put(ref, 15 + y, level.middle(far, y))
        near, far = (CX - 1, CX - 2) if up else (0, 1)
        for y in range(-1, 2):
            put(ref, 18 + y, level.coarse(near, y))
        put(ref, 20, level.coarse(far, 0))


def faces(size_x, size_y):
    own = [(x, y) for x in range(size_x) for y in range(size_y)]
    beyond = [(x, y) for x in (-1, size_x) for y in range(size_y)]
    beyond += [(x, y) for x in range(size_x) for y in (-1, size_y)]
    return own, beyond


def neighbours(x, y):
    return ((x - 1, y), (x + 1, y), (x, y - 1), (x, y + 1))


def spread(weights, values):
    total = weights[0:1] * values[0]
    for side in range(1, 6):
        total = total + weights[side : side + 1] * values[side]
    return total


def smooth_tile(weights, here, values):
    return (2.0 * jacobi_weight) * here + weights[7:8] * spread(weights, values)


def gram_of(basis_ref, size):
    width = FINE * LANES // 2

    def add(step, total):
        columns = pl.ds(pl.multiple_of(step * width, width), width)
        return total + dot(basis_ref[:size, columns], basis_ref[:, columns], (1, 1))

    return lax.fori_loop(0, FINE * LANES // width, add, jnp.zeros((size, LANES), F32))


def search_kernel(
    xp_ref, axp_ref, ef, em, ec, cf, cm, cc,
    zr, zl, yu, yd, xu, xd, y2u, y2d,
    wzr, wzl, wyu, wyd, wxu, wxd,
    wa_ref, gram, basis_ref,
):
    size = PAIR + ef.shape[0]
    basis_ref[:PAIR] = xp_ref[...]
    basis_ref[HALF : HALF + PAIR] = axp_ref[...]
    if size < HALF:
        blank = jnp.zeros((HALF - size, FINE * LANES), F32)
        basis_ref[size:HALF] = blank
        basis_ref[HALF + size :] = blank

    def rows_at(start, step):
        return pl.ds(pl.multiple_of(start + step * VECS, VECS), VECS)

    def block(step, carry):
        rows = rows_at(0, step)
        values = Level(
            (ef, em, ec), zr, zl, rows, VECS, yu, yd, xu, xd, y2u, y2d, rows
        )
        weights = Level(
            (cf, cm, cc), wzr, wzl, slice(PAIR, PAIR + 8), 8, wyu, wyd, wxu, wxd
        )
        targets = (
            (wa_ref, rows, rows_at(ef.shape[0], step)),
            (basis_ref, rows_at(PAIR, step), rows_at(HALF + PAIR, step)),
        )
        smooth_block(values, weights, cf, targets)
        return carry

    if size == 3 * VECS:
        block(0, 0)
    else:
        lax.fori_loop(0, (size - PAIR) // VECS, block, 0)
    gram[...] = gram_of(basis_ref, size)


def smooth_block(values, weights, cf, targets):
    lane = lanes_of(VECS)
    double = pair_matrix(True)

    own, beyond = faces(CX, CY)
    coarse_cells = own + beyond
    smoothed = []
    for cell in coarse_cells:
        here = values.coarse(*cell)
        around = [values.coarse(*other) for other in neighbours(*cell)]
        around += [turn(here, 1), turn(here, -1)]
        smoothed.append(smooth_tile(weights.coarse(*cell), here, around))
    doubled = dot(stack(smoothed), double)
    to_middle = {}
    for k, cell in enumerate(coarse_cells):
        ends = jnp.where(lane < 96, turn(smoothed[k], 32), smoothed[k])
        inner = doubled[VECS * k : VECS * (k + 1)]
        to_middle[cell] = jnp.where(lane < 64, inner, ends)

    own, beyond = faces(MX, MY)
    middle_cells = own + beyond
    smoothed = []
    for cell in middle_cells:
        here = values.middle(*cell)
        around = [values.middle(*other) for other in neighbours(*cell)]
        around += [turn(here, 1), turn(here, -1)]
        part = smooth_tile(weights.middle(*cell), here, around)
        smoothed.append(part + to_middle[cell[0] // 2, cell[1] // 2])
    doubled = dot(stack(smoothed), double)
    to_fine, to_end = {}, {}
    for k, cell in enumerate(middle_cells):
        to_fine[cell] = doubled[VECS * k : VECS * (k + 1)]
        to_end[cell] = jnp.where(lane < HALF, turn(smoothed[k], 64), smoothed[k])

    def zs(main, end):
        low = jnp.where(lane > 0, turn(main, 1), turn(end, 1))
        high = jnp.where(lane < LANES - 1, turn(main, -1), turn(end, -1))
        return [low, high]

    own, beyond = faces(LX, LY)
    found, found_end = {}, {}
    for cell in beyond + own:
        here, end = values.fine(*cell), values.fine_end(*cell)
        around = [values.fine(*other) for other in neighbours(*cell)] + zs(here, end)
        part = smooth_tile(weights.fine(*cell), here, around)
        found[cell] = part + to_fine[cell[0] // 2, cell[1] // 2]
    for cell in own:
        here, end = values.fine(*cell), values.fine_end(*cell)
        around = [values.fine_end(*other) for other in neighbours(*cell)] + zs(end, here)
        part = smooth_tile(weights.fine_end(*cell), end, around)
        found_end[cell] = part + to_end[cell[0] // 2, cell[1] // 2]
    for cell in own:
        k = cell[0] * LY + cell[1]
        here = found[cell]
        factors = tile(cf, k)
        around = [found[other] for other in neighbours(*cell)] + zs(here, found_end[cell])
        applied = factors[6:7] * here - spread(factors, around)
        columns = slice(k * LANES, (k + 1) * LANES)
        for ref, first, second in targets:
            ref[first, columns] = here
            ref[second, columns] = applied


def symmetric(summed):
    size = summed.shape[0]
    lane = lanes_of(size)
    flipped = lower_pad(summed).T
    sym_b = 0.5 * (summed + flipped[:size])
    sym_a = 0.5 * (turn(summed, HALF) + flipped[HALF : HALF + size])
    return jnp.where(lane < size, sym_b, 0.0), jnp.where(lane < size, sym_a, 0.0)


def judge_kernel(summed, gram, change, flag):
    size = 3 * VECS
    sym_b, sym_a = symmetric(summed[...])
    lane, row = lanes_of(VECS), rows_of(VECS)
    projected = solve_projected(
        jnp.where(lane < VECS, sym_b[:VECS], 0.0), jnp.where(lane < VECS, sym_a[:VECS], 0.0)
    )
    projected = jnp.where(lane < VECS, projected, 0.0)
    backward = turn(lower_pad(projected).T[:VECS], PAIR)
    direct = jnp.where(lanes_of(PAIR) == rows_of(PAIR), 1.0, 0.0).astype(F32)
    tail = jnp.where(lane == row + 3 * VECS, 1.0, 0.0).astype(F32) - backward
    mixing = stack([direct, tail])
    padded = lower_pad(mixing)
    small_b = dot(dot(mixing[:, :HALF], sym_b), padded, (1, 1))
    small_a = dot(dot(mixing[:, :HALF], sym_a), padded, (1, 1))
    gram[...] = jnp.where(lanes_of(size) < HALF, small_b, turn(small_a, HALF))
    change[...] = mixing
    lost = jnp.zeros((VECS, 1), F32)
    for small, full in ((small_b, sym_b), (small_a, sym_a)):
        after = jnp.where(lane == row + PAIR, small[PAIR:], 0.0)
        before = jnp.where(lane == row + 3 * VECS, full[3 * VECS :], 0.0)
        after = jnp.sum(after, axis=1, keepdims=True)
        before = jnp.sum(before, axis=1, keepdims=True)
        lost = jnp.maximum(lost, jnp.where(after > KEEP * before, 0.0, 1.0))
    flag[...] = jnp.broadcast_to(jnp.max(lost, axis=0, keepdims=True), (8, LANES))


def combine(coefficients, change, sources, targets):
    lane = lanes_of(VECS)
    both = stack([coefficients, jnp.where(lane >= VECS, coefficients, 0.0)])
    if change is not None:
        both = dot(both[:, : 3 * VECS], change)
    count = sources[0][1].stop - sources[0][1].start
    both = both[:, : PAIR + count]
    width = 8 * LANES

    def part(step, carry):
        columns = pl.ds(pl.multiple_of(step * width, width), width)
        for (old, rows, found), target in zip(sources, targets):
            target[:, columns] = dot(both, stack([old[:, columns], found[rows, columns]]))
        return carry

    lax.fori_loop(0, FINE * LANES // width, part, 0)


def mixed_kernel(
    gram, change, xp_ref, axp_ref, wa_ref, cf, cm, cc, nxp, naxp, ef, em, ec, zr, zl
):
    coefficients, projected = ritz(gram[...])
    own, applied = slice(0, PAIR), slice(PAIR, 2 * PAIR)
    sources = ((xp_ref, own, wa_ref), (axp_ref, applied, wa_ref))
    combine(coefficients, change[...], sources, (nxp, naxp))
    residual = naxp[:VECS] - dot(projected[:, :VECS], nxp[:VECS], (0, 0))
    level_parts(residual, cf, cm, cc, ef, em, ec)
    pack_z(ef, em, ec, cf, cm, cc, zr, zl)


def careful_kernel(change, xp_ref, axp_ref, wide_ref, gram, basis_ref):
    part = change[PAIR:, PAIR:HALF]
    blank = jnp.zeros((VECS, FINE * LANES), F32)
    for at, values, rows in ((0, xp_ref, slice(0, PAIR)), (HALF, axp_ref, slice(PAIR, 2 * PAIR))):
        basis_ref[at : at + PAIR] = values[...]
        basis_ref[at + PAIR : at + 3 * VECS] = dot(part, wide_ref[rows])
        basis_ref[at + 3 * VECS : at + HALF] = blank
    gram[...] = gram_of(basis_ref, 3 * VECS)


def last_kernel(summed, xp_ref, wa_ref, x_out, p_out, moved):
    coefficients, _ = ritz(summed[...])
    combine(coefficients, None, ((xp_ref, slice(0, VECS), wa_ref),), (moved,))
    for k in range(FINE):
        x_out[pl.ds(k, VECS, stride=FINE), :] = tile(moved, k, slice(0, VECS))
        p_out[pl.ds(k, VECS, stride=FINE), :] = tile(moved, k, slice(VECS, PAIR))


def shifted(values, axis, by):
    peers = lax.axis_size(axis)
    return lax.ppermute(values, axis, [(i, (i + by) % peers) for i in range(peers)])


def masks_of(size):
    return {1: [], 2: [1], 4: [1, 3], 8: [1, 2, 6]}[size]


def all_sum(values):
    rounds = [(k, axis, m) for axis in ("gy", "gx", "gz") for k, m in enumerate(masks_of(lax.axis_size(axis)))]
    for _, axis, mask in sorted(rounds, key=lambda entry: entry[0]):
        pairs = [(i, i ^ mask) for i in range(lax.axis_size(axis))]
        values = values + lax.ppermute(values, axis, pairs)
    return values


def exchange(parts, weights, zr, zl):
    rows = zr.shape[0]
    ec = parts[2]
    zr, zl = shifted(zr, "gz", 1), shifted(zl, "gz", -1)
    y2u, y2d = shifted(ec, "gy", 2), shifted(ec, "gy", -2)
    yu, yd = run(pack_y_kernel, [(rows, 27 * LANES)] * 2, (*parts, *weights, zr, zl))
    yu, yd = shifted(yu, "gy", 1), shifted(yd, "gy", -1)
    xu, xd = run(pack_x_kernel, [(rows, 21 * LANES)] * 2, (*parts, *weights, zr, zl, yu, yd, y2u, y2d))
    xu, xd = shifted(xu, "gx", 1), shifted(xd, "gx", -1)
    return (zr, zl, yu, yd, xu, xd), (y2u, y2d)


def on_device(x_block, p_block, voxel_class, conductance):
    sizes = [lax.axis_size(axis) for axis in ("gx", "gy", "gz")]
    all_cells = FINE * LANES * sizes[0] * sizes[1] * sizes[2]
    wide = FINE * LANES
    flags = []
    for axis, size in zip(("gx", "gy", "gz"), sizes):
        at = lax.axis_index(axis)
        flags += [at > 0, at < size - 1]
    flags = jnp.stack(flags).astype(F32)
    far = (
        x_block.reshape(VECS * FINE, LANES),
        p_block.reshape(VECS * FINE, LANES),
        voxel_class.reshape(FINE, LANES),
    )
    if not INTERPRET:
        far = [pltpu.with_memory_space_constraint(array, pltpu.HBM) for array in far]
    sides = [(40, wide)] + [(40, LANES)] * 2 + [(40, LX * LANES)] * 2 + [(40, LY * LANES)] * 2
    field, zr, zl, yu, yd, xu, xd = pl.pallas_call(
        start_kernel,
        out_shape=[SHAPE(shape, F32) for shape in sides],
        in_specs=[pl.BlockSpec(memory_space=pltpu.SMEM)]
        + [pl.BlockSpec(memory_space=pltpu.HBM)] * 3,
        out_specs=[pl.BlockSpec(memory_space=pltpu.VMEM)] * len(sides),
        scratch_shapes=[pltpu.VMEM((VECS * FINE, LANES), F32)] * 2
        + [pltpu.VMEM((FINE, LANES), jnp.int32), pltpu.SemaphoreType.DMA((3,))],
        compiler_params=pltpu.CompilerParams(vmem_limit_bytes=GRANT),
        interpret=INTERPRET,
    )(
        conductance,
        *far,
    )
    arrived = (
        shifted(zr, "gz", 1), shifted(zl, "gz", -1), shifted(yu, "gy", 1),
        shifted(yd, "gy", -1), shifted(xu, "gx", 1), shifted(xd, "gx", -1),
    )
    fields = [(PAIR, wide)] * 2
    weight_shapes = [(8, wide), (8, MIDDLE * LANES), (8, COARSE * LANES)]

    def part_shapes(rows):
        return [(rows, wide), (rows, MIDDLE * LANES), (rows, COARSE * LANES)]

    xp, axp, cf, cm, cc, *parts, zr, zl = run(
        first_kernel,
        fields + weight_shapes + part_shapes(PAIR) + [(PAIR + 8, LANES)] * 2,
        (field, *arrived),
        (flags,),
    )
    weights = (cf, cm, cc)
    basis = [(2 * HALF, wide)]

    def search(parts, sent, far, sent_weights):
        rows = parts[0].shape[0]
        inputs = (xp, axp, *parts, *weights, *sent, *far, *sent_weights)
        shapes = [(2 * rows, wide), (PAIR + rows, LANES)]
        return run(search_kernel, shapes, inputs, scratch=basis)

    sent_weights, far = exchange(parts, weights, zr, zl)
    wa, gram = search(parts, sent_weights, far, sent_weights)
    summed = all_sum(gram) * (1.0 / all_cells)
    small = (3 * VECS, LANES)
    gram, change, flag = run(judge_kernel, [small, small, (8, LANES)], (summed,))
    nexts = fields + part_shapes(VECS) + [(VECS, LANES)] * 2

    def careful(gram, change, wa):
        (gram,) = run(careful_kernel, [small], (change, xp, axp, wa), scratch=basis)
        return lax.psum(gram, ("gx", "gy", "gz")) * (1.0 / all_cells)

    def given(gram, change, wa):
        return gram

    gram = lax.cond(flag[0, 0] > 0.5, careful, given, gram, change, wa)
    xp, axp, *parts, zr, zl = run(mixed_kernel, nexts, (gram, change, xp, axp, wa, *weights))
    sent, far = exchange(parts, weights, zr, zl)
    wa, gram = search(parts, sent, far, sent_weights)
    gram = all_sum(gram) * (1.0 / all_cells)
    outs = [(VECS * FINE, LANES)] * 2
    x_out, p_out = run(last_kernel, outs, (gram, xp, wa), scratch=[(PAIR, wide)])
    return (x_out.reshape(x_block.shape), p_out.reshape(x_block.shape))


def solution(mesh):
    in_specs = (P(None, "gx", "gy", "gz"), P(None, "gx", "gy", "gz"), P("gx", "gy", "gz"), P())
    out_specs = (P(None, "gx", "gy", "gz"), P(None, "gx", "gy", "gz"))
    return jax.shard_map(
        on_device, mesh=mesh, in_specs=in_specs, out_specs=out_specs, check_vma=False
    )
```

```python
import jax
import jax.numpy as jnp
from jax import lax
from jax.experimental import pallas as pl
from jax.experimental.pallas import tpu as pltpu
from jax.sharding import PartitionSpec as P

VECS = 16
CLASSES = 8
ITERS = 2
INNER = 4
INTERPRET = False
GRANT = 24 * 1024 * 1024
PAIR = 2 * VECS
KEEP = 0.02

jacobi_weight = 2.0 / 3.0
mass_shift = 0.05

LX, LY, LANES = 8, 4, 128
MX, MY = LX // 2, LY // 2
CX, CY = LX // 4, LY // 4
FINE, MIDDLE, COARSE = LX * LY, MX * MY, CX * CY
SHAPE = jax.ShapeDtypeStruct
F32 = jnp.float32
HALF = LANES // 2


def tile(ref, index, rows=slice(None)):
    return ref[rows, index * LANES : (index + 1) * LANES]


def lanes_of(rows=8):
    return lax.broadcasted_iota(jnp.int32, (rows, LANES), 1)


def rows_of(rows):
    return lax.broadcasted_iota(jnp.int32, (rows, LANES), 0)


def turn(value, shift):
    shift = shift % LANES
    return value if shift == 0 else pltpu.roll(value, shift, 1)


def dot(left, right, contract=(1, 0)):
    return lax.dot_general(
        left,
        right,
        (((contract[0],), (contract[1],)), ((), ())),
        precision=lax.Precision.HIGHEST,
        preferred_element_type=F32,
    )


def pair_matrix(transposed):
    wide = lax.broadcasted_iota(jnp.int32, (LANES, LANES), 1 if transposed else 0)
    narrow = lax.broadcasted_iota(jnp.int32, (LANES, LANES), 0 if transposed else 1)
    return jnp.where(wide // 2 == narrow, 1.0, 0.0).astype(F32)


def stack(values):
    return jnp.concatenate(values, axis=0)


def run(body, outs, vmem, smem=(), scratch=()):
    in_specs = [pl.BlockSpec(memory_space=pltpu.SMEM)] * len(smem)
    in_specs += [pl.BlockSpec(memory_space=pltpu.VMEM)] * len(vmem)
    return pl.pallas_call(
        body,
        out_shape=[SHAPE(shape, F32) for shape in outs],
        in_specs=in_specs,
        out_specs=[pl.BlockSpec(memory_space=pltpu.VMEM)] * len(outs),
        scratch_shapes=[pltpu.VMEM(shape, F32) for shape in scratch],
        compiler_params=pltpu.CompilerParams(vmem_limit_bytes=GRANT),
        interpret=INTERPRET,
    )(*smem, *vmem)


def start_kernel(
    cond_ref, x_far, p_far, class_far, field_ref, zr, zl, yu, yd, xu, xd,
    x_ref, p_ref, class_ref, done,
):
    fetches = [
        pltpu.make_async_copy(far, near, done.at[k])
        for k, (far, near) in enumerate(
            ((class_far, class_ref), (x_far, x_ref), (p_far, p_ref))
        )
    ]
    for fetch in fetches:
        fetch.start()
    for fetch in fetches:
        fetch.wait()
    classes = class_ref[...]
    local = jnp.zeros(classes.shape, F32)
    for index in range(CLASSES):
        local = local + jnp.where(classes == index, cond_ref[index], 0.0)
    lane = lanes_of(40)
    right = jnp.zeros((40, LANES), F32)
    left = jnp.zeros((40, LANES), F32)
    for x in range(LX):
        for y in range(LY):
            p = x * LY + y
            cell = stack(
                [
                    x_ref[pl.ds(p, VECS, stride=FINE), :],
                    p_ref[pl.ds(p, VECS, stride=FINE), :],
                    jnp.broadcast_to(local[p : p + 1], (8, LANES)),
                ]
            )
            field_ref[:, p * LANES : (p + 1) * LANES] = cell
            right = jnp.where(lane == p, turn(cell, p + 1), right)
            left = jnp.where(lane == p, turn(cell, p), left)
            if y == LY - 1:
                yu[:, x * LANES : (x + 1) * LANES] = cell
            if y == 0:
                yd[:, x * LANES : (x + 1) * LANES] = cell
            if x == LX - 1:
                xu[:, y * LANES : (y + 1) * LANES] = cell
            if x == 0:
                xd[:, y * LANES : (y + 1) * LANES] = cell
    zr[...] = right
    zl[...] = left


def finish_weights(weights, shift_term):
    row = rows_of(8)
    weights = jnp.where(row < 6, weights, 0.0)
    diagonal = shift_term + jnp.sum(weights, axis=0, keepdims=True)
    return jnp.where(
        row < 6, weights, jnp.where(row == 6, diagonal, jacobi_weight / diagonal)
    )


def coarsen_weights(fine, size_x, size_y, shift_term, halve):
    row, lane = rows_of(8), lanes_of(8)
    sums = []
    for x in range(size_x):
        for y in range(size_y):
            total = jnp.zeros((8, LANES), F32)
            for i in range(2):
                for j in range(2):
                    keep = (row == i) | (row == 2 + j)
                    keep = keep | ((row == 4) & (lane % 2 == 0)) | ((row == 5) & (lane % 2 == 1))
                    total = total + jnp.where(keep, fine[2 * x + i, 2 * y + j], 0.0)
            sums.append(total)
    paired = dot(stack(sums), halve)
    return {
        (k // size_y, k % size_y): finish_weights(paired[8 * k : 8 * k + 8], shift_term)
        for k in range(size_x * size_y)
    }


def first_kernel(flag_ref, field_ref, zr, zl, yu, yd, xu, xd, xp_ref, axp_ref, cf, cm, cc, ef, em, ec, szr, szl):
    lane, row = lanes_of(8), rows_of(8)
    lane40 = lanes_of(40)
    from_low, from_high = zr[...], zl[...]
    flags = [flag_ref[k] for k in range(6)]
    ends = jnp.where((row == 4) & (lane == 0), flags[4], 1.0)
    ends = jnp.where((row == 5) & (lane == LANES - 1), flags[5], ends)
    fine = {}
    for x in range(LX):
        for y in range(LY):
            p = x * LY + y
            here = tile(field_ref, p)
            beside = [
                tile(field_ref, p - LY) if x > 0 else tile(xu, y),
                tile(field_ref, p + LY) if x < LX - 1 else tile(xd, y),
                tile(field_ref, p - 1) if y > 0 else tile(yu, x),
                tile(field_ref, p + 1) if y < LY - 1 else tile(yd, x),
                jnp.where(lane40 == 0, turn(from_low, -p), turn(here, 1)),
                jnp.where(lane40 == LANES - 1, turn(from_high, LANES - 1 - p), turn(here, -1)),
            ]
            around = stack([value[32:33] for value in beside] + [here[32:34]])
            own = here[32:40]
            keep = ends
            for side, at_end in enumerate((x == 0, x == LX - 1, y == 0, y == LY - 1)):
                if at_end:
                    keep = jnp.where(row == side, flags[side], keep)
            weights = finish_weights(2.0 * around * own / (around + own) * keep, mass_shift)
            fine[x, y] = weights
            cf[:, p * LANES : (p + 1) * LANES] = weights
            applied = weights[6:7] * here[:32]
            for side in range(6):
                applied = applied - weights[side : side + 1] * beside[side][:32]
            xp_ref[:, p * LANES : (p + 1) * LANES] = here[:32]
            axp_ref[:, p * LANES : (p + 1) * LANES] = applied
    halve = pair_matrix(False)
    middle = coarsen_weights(fine, MX, MY, 8.0 * mass_shift, halve)
    for (x, y), value in middle.items():
        k = x * MY + y
        cm[:, k * LANES : (k + 1) * LANES] = value
    coarse = coarsen_weights(middle, CX, CY, 64.0 * mass_shift, halve)
    for (x, y), value in coarse.items():
        cc[:, x * LANES : (x + 1) * LANES] = value
    level_parts(stack([xp_ref[:VECS], axp_ref[:VECS]]), cf, cm, cc, ef, em, ec)
    pack_z(ef, em, ec, cf, cm, cc, szr, szl)


def eliminate(rows, size, full):
    tiles = [rows[8 * i : 8 * i + 8] for i in range(rows.shape[0] // 8)]
    row = rows_of(8)
    kept = list(tiles)
    nothing = rows[:8] * 0.0
    for k in range(0, size, 2):
        at, sub = divmod(k, 8)
        spread_left = tiles[at][:, k : k + 1] + nothing
        spread_right = tiles[at][:, k + 1 : k + 2] + nothing

        def line(value, which):
            return jnp.broadcast_to(value[sub + which : sub + which + 1], (8, LANES))

        first, second = line(tiles[at], 0), line(tiles[at], 1)
        a, b = line(spread_left, 0), line(spread_right, 0)
        c, d = line(spread_left, 1), line(spread_right, 1)
        crossed = a * second - c * first
        inverse = 1.0 / (a * d - b * c)
        solved_first = (d * first - b * second) * inverse
        solved_second = crossed * inverse
        if not full:
            kept[at] = jnp.where(row == sub, first * (1.0 / jnp.sqrt(a)), kept[at])
            root = jnp.sqrt(inverse) * (1.0 / jnp.sqrt(a))
            kept[at] = jnp.where(row == sub + 1, crossed * root, kept[at])
        for i in range(len(tiles)):
            if i < at and not full:
                continue
            if i == at:
                left, right = spread_left, spread_right
            else:
                left, right = tiles[i][:, k : k + 1], tiles[i][:, k + 1 : k + 2]
            changed = tiles[i] - (left * solved_first + right * solved_second)
            if i == at:
                changed = jnp.where(row == sub, solved_first, changed)
                changed = jnp.where(row == sub + 1, solved_second, changed)
            tiles[i] = changed
    return stack(tiles if full else kept)


def lower_pad(matrix):
    missing = LANES - matrix.shape[0]
    return stack([matrix, jnp.zeros((missing, LANES), F32)])


def solve_projected(gram, cross):
    lane = lanes_of(VECS)
    on_diagonal = jnp.where((lane == rows_of(VECS)) & (lane < VECS), gram, 0.0)
    column = 1.0 / jnp.sqrt(jnp.sum(on_diagonal, axis=1, keepdims=True))
    across = jnp.sum(on_diagonal, axis=0, keepdims=True)
    across = jnp.where(lanes_of(1) < VECS, 1.0 / jnp.sqrt(across), 0.0)
    both = jnp.where(lane < HALF, gram * across, turn(cross, HALF)) * column
    return turn(eliminate(both, VECS, True), HALF) * column


def ritz(summed):
    size = 3 * VECS
    lane, row = lanes_of(size), rows_of(size)
    sym_b, sym_a = symmetric(summed)
    on_diagonal = jnp.where(lane == row, sym_b, 0.0)
    column = 1.0 / jnp.sqrt(jnp.sum(on_diagonal, axis=1, keepdims=True))
    across = jnp.sum(on_diagonal, axis=0, keepdims=True)
    across = jnp.where(lanes_of(1) < size, 1.0 / jnp.sqrt(across), 0.0)
    normed_b = sym_b * column * across
    normed_a = sym_a * column * across
    done = eliminate(jnp.where(lane < HALF, normed_a, turn(normed_b, HALF)), size, True)
    step = jnp.where(lane < size, turn(done, HALF), 0.0)
    weighed = dot(normed_b[:, :size], step)
    step_pad, weighed_pad = lower_pad(step), lower_pad(weighed)
    short_lane = lanes_of(VECS)

    def inner_step(_, basis):
        mapped = dot(basis, step_pad, (1, 1))
        product = dot(basis, weighed_pad, (1, 1))
        square = dot(product, lower_pad(mapped), (1, 1))
        done = eliminate(jnp.where(short_lane < HALF, square, turn(mapped, HALF)), VECS, False)
        return jnp.where(short_lane < size, turn(done, HALF), 0.0)

    basis = jnp.where(short_lane == rows_of(VECS), 1.0, 0.0).astype(F32)
    basis = lax.fori_loop(0, INNER, inner_step, basis)
    cross = dot(dot(basis, lower_pad(normed_a), (1, 1)), lower_pad(basis), (1, 1))
    return basis * across, cross


def level_parts(residual, cf, cm, cc, ef, em, ec):
    count = residual.shape[0]
    halve = pair_matrix(False)
    sums = []
    for mx in range(MX):
        for my in range(MY):
            total = jnp.zeros((count, LANES), F32)
            for i in range(2):
                for j in range(2):
                    p = (2 * mx + i) * LY + 2 * my + j
                    part = residual[:, p * LANES : (p + 1) * LANES]
                    total = total + part
                    ef[:, p * LANES : (p + 1) * LANES] = part * tile(cf, p, slice(7, 8))
            sums.append(total)
    paired = dot(stack(sums), halve)
    middle = [paired[count * k : count * (k + 1)] for k in range(MIDDLE)]
    for k in range(MIDDLE):
        em[:, k * LANES : (k + 1) * LANES] = middle[k] * tile(cm, k, slice(7, 8))
    sums = []
    for cx in range(CX):
        sums.append(sum(middle[(2 * cx + i) * MY + j] for i in range(2) for j in range(2)))
    paired = dot(stack(sums), halve)
    for k in range(COARSE):
        coarse = paired[count * k : count * (k + 1)]
        ec[:, k * LANES : (k + 1) * LANES] = coarse * tile(cc, k, slice(7, 8))


def pack_z(ef, em, ec, cf, cm, cc, zr, zl):
    rows = zr.shape[0]
    lane = lanes_of(rows)

    def cell(values, weights, k):
        here = tile(values, k)
        return stack([here, tile(weights, k)]) if rows > values.shape[0] else here

    right = jnp.zeros((rows, LANES), F32)
    left = jnp.zeros((rows, LANES), F32)
    levels = ((ef, cf, FINE, 0, 126), (em, cm, MIDDLE, 64, 62), (ec, cc, COARSE, 80, 30))
    for values, weights, count, base, last in levels:
        for k in range(count):
            here = cell(values, weights, k)
            spot = base + 2 * k
            right = jnp.where(lane // 2 == spot // 2, turn(here, spot - last), right)
            left = jnp.where(lane // 2 == spot // 2, turn(here, spot), left)
    zr[...] = right
    zl[...] = left


Y_TILES, X_TILES = 25, 17


def apart_tile(ref, base, k):
    return tile(ref, base + k // 4, slice(8 * (k % 4), 8 * (k % 4) + 8))


class Level:
    def __init__(
        self, own, low, high, rows, count, yu=None, yd=None, xu=None, xd=None,
        y2u=None, y2d=None, inner=slice(None), apart=False,
    ):
        self.own, self.inner, self.apart = own, inner, apart
        self.low, self.high = low[rows], high[rows]
        self.yu, self.yd, self.xu, self.xd, self.y2u, self.y2d = yu, yd, xu, xd, y2u, y2d
        self.lane = lanes_of(count)
        self.kept = {}

    def once(self, key, make):
        if key not in self.kept:
            self.kept[key] = make()
        return self.kept[key]

    def own_rows(self, ref, k):
        return tile(ref, k, self.inner)

    def fine(self, x, y):
        if 0 <= x < LX and 0 <= y < LY:
            return self.own_rows(self.own[0], x * LY + y)
        if 0 <= x < LX:
            ref, layer = (self.yu, y + 2) if y < 0 else (self.yd, y - LY)
            if self.apart:
                return apart_tile(ref, Y_TILES, x)
            return tile(ref, 2 * x + layer, self.inner)
        ref, near = (self.xu, x == -1) if x < 0 else (self.xd, x == LX)
        if self.apart:
            return apart_tile(ref, X_TILES, y)
        return tile(ref, y + 1 if near else 6 + y, self.inner)

    def fine_end(self, x, y):
        def make():
            if 0 <= x < LX and 0 <= y < LY:
                p = x * LY + y
                return jnp.where(
                    self.lane < HALF, turn(self.high, -2 * p), turn(self.low, 126 - 2 * p)
                )
            if 0 <= x < LX:
                return turn(tile(self.yu if y < 0 else self.yd, 16, self.inner), -(1 + 2 * x))
            return turn(tile(self.xu if x < 0 else self.xd, 10, self.inner), -(1 + 2 * y))

        return self.once(("end", x, y), make)

    def middle(self, x, y):
        def make():
            if 0 <= x < MX and 0 <= y < MY:
                k = x * MY + y
                beyond = jnp.where(
                    self.lane < 96, turn(self.high, -2 * k), turn(self.low, 62 - 2 * k)
                )
                return jnp.where(self.lane < 64, self.own_rows(self.own[1], k), beyond)
            if 0 <= x < MX:
                ref = self.yu if y < 0 else self.yd
                if self.apart:
                    return apart_tile(ref, Y_TILES, LX + x)
                if y in (-1, MY):
                    return tile(ref, 17 + x, self.inner)
                return turn(tile(ref, 21 + x // 2, self.inner), -64 * (x % 2))
            ref, near = (self.xu, x == -1) if x < 0 else (self.xd, x == MX)
            if self.apart:
                return apart_tile(ref, X_TILES, LY + y)
            if not near:
                return turn(tile(ref, 14, self.inner), -64 * y)
            if 0 <= y < MY:
                return tile(ref, 11 + y, self.inner)
            return turn(tile(ref, 13, self.inner), 0 if y < 0 else -64)

        return self.once(("middle", x, y), make)

    def coarse(self, x, y):
        def make():
            if 0 <= x < CX and y == 0:
                beyond = jnp.where(
                    self.lane < 64, turn(self.high, -48 - 2 * x), turn(self.low, 46 - 2 * x)
                )
                return jnp.where(self.lane < 32, self.own_rows(self.own[2], x), beyond)
            if 0 <= x < CX:
                if abs(y) == 2:
                    return tile(self.y2u if y < 0 else self.y2d, x, self.inner)
                ref = self.yu if y < 0 else self.yd
                if self.apart:
                    return apart_tile(ref, Y_TILES, LX + MX + x)
                return tile(ref, 23 + x, self.inner)
            ref, near = (self.xu, x == -1) if x < 0 else (self.xd, x == CX)
            if self.apart:
                return apart_tile(ref, X_TILES, LY + MY)
            if near and y == 0:
                return tile(ref, 15, self.inner)
            return turn(tile(ref, 16, self.inner), -64 if not near else 0 if y < 0 else -32)

        return self.once(("coarse", x, y), make)


def put(ref, index, value):
    ref[:, index * LANES : (index + 1) * LANES] = value


def pack_ends(values):
    rows = values[0].shape[0]
    lane = lanes_of(rows)
    packed = jnp.zeros((rows, LANES), F32)
    for k, value in enumerate(values):
        packed = jnp.where(lane // 2 == k, turn(value, 1 + 2 * k), packed)
    return packed


def halves(left, right):
    return jnp.where(lanes_of(left.shape[0]) < HALF, left, turn(right, HALF))


def put_apart(ref, base, weights):
    if ref.shape[1] == base * LANES:
        return
    for k in range(0, len(weights), 4):
        group = weights[k : k + 4]
        put(ref, base + k // 4, stack(group + group[:1] * (4 - len(group))))


def pack_y_kernel(ef, em, ec, cf, cm, cc, zr, zl, yu, yd):
    count = ef.shape[0]
    level = Level((ef, em, ec), zr, zl, slice(0, count), count)
    for ref, first, edge, near, far in ((yu, LY - 2, LY - 1, MY - 1, 0), (yd, 0, 0, 0, MY - 1)):
        for x in range(LX):
            for j in range(2):
                put(ref, 2 * x + j, level.fine(x, first + j))
        put(ref, 16, pack_ends([level.fine_end(x, edge) for x in range(LX)]))
        for x in range(MX):
            put(ref, 17 + x, level.middle(x, near))
        for k in range(MX // 2):
            put(ref, 21 + k, halves(level.middle(2 * k, far), level.middle(2 * k + 1, far)))
        for x in range(CX):
            put(ref, 23 + x, level.coarse(x, 0))
        weights = [tile(cf, x * LY + edge) for x in range(LX)]
        weights += [tile(cm, x * MY + near) for x in range(MX)]
        put_apart(ref, Y_TILES, weights + [tile(cc, x) for x in range(CX)])


def pack_x_kernel(ef, em, ec, cf, cm, cc, zr, zl, ryu, ryd, y2u, y2d, xu, xd):
    count = ef.shape[0]
    lane = lanes_of(count)
    level = Level((ef, em, ec), zr, zl, slice(0, count), count, ryu, ryd)
    for ref, up in ((xu, True), (xd, False)):
        near, far = (LX - 1, LX - 2) if up else (0, 1)
        for y in range(-1, LY + 1):
            put(ref, y + 1, level.fine(near, y))
        for y in range(LY):
            put(ref, 6 + y, level.fine(far, y))
        put(ref, 10, pack_ends([level.fine_end(near, y) for y in range(LY)]))
        weights = [tile(cf, near * LY + y) for y in range(LY)]
        near, far = (MX - 1, MX - 2) if up else (0, 1)
        for y in range(MY):
            put(ref, 11 + y, level.middle(near, y))
        put(ref, 13, halves(level.middle(near, -1), level.middle(near, MY)))
        put(ref, 14, halves(level.middle(far, 0), level.middle(far, 1)))
        weights += [tile(cm, near * MY + y) for y in range(MY)]
        near, far = (CX - 1, CX - 2) if up else (0, 1)
        put(ref, 15, level.coarse(near, 0))
        ends = jnp.where(lane < 32, level.coarse(near, -1), turn(level.coarse(near, 1), 32))
        put(ref, 16, halves(ends, level.coarse(far, 0)))
        put_apart(ref, X_TILES, weights + [tile(cc, near)])


def faces(size_x, size_y):
    own = [(x, y) for x in range(size_x) for y in range(size_y)]
    beyond = [(x, y) for x in (-1, size_x) for y in range(size_y)]
    beyond += [(x, y) for x in range(size_x) for y in (-1, size_y)]
    return own, beyond


def neighbours(x, y):
    return ((x - 1, y), (x + 1, y), (x, y - 1), (x, y + 1))


def spread(weights, values):
    total = weights[0:1] * values[0]
    for side in range(1, 6):
        total = total + weights[side : side + 1] * values[side]
    return total


def smooth_tile(weights, here, values):
    return (2.0 * jacobi_weight) * here + weights[7:8] * spread(weights, values)


def gram_of(basis_ref, size, chunks=4):
    width = FINE * LANES // chunks

    def add(step, total):
        columns = pl.ds(pl.multiple_of(step * width, width), width)
        return total + dot(basis_ref[:size, columns], basis_ref[:, columns], (1, 1))

    return lax.fori_loop(0, FINE * LANES // width, add, jnp.zeros((size, LANES), F32))


def search_kernel(
    xp_ref, axp_ref, ef, em, ec, cf, cm, cc,
    zr, zl, yu, yd, xu, xd, y2u, y2d,
    wzr, wzl, wyu, wyd, wxu, wxd,
    wa_ref, gram, basis_ref,
):
    size = PAIR + ef.shape[0]
    basis_ref[:PAIR] = xp_ref[...]
    basis_ref[HALF : HALF + PAIR] = axp_ref[...]
    if size < HALF:
        blank = jnp.zeros((HALF - size, FINE * LANES), F32)
        basis_ref[size:HALF] = blank
        basis_ref[HALF + size :] = blank

    def rows_at(start, step):
        return slice(start + step * VECS, start + (step + 1) * VECS)

    for step in range((size - PAIR) // VECS):
        rows = rows_at(0, step)
        values = Level(
            (ef, em, ec), zr, zl, rows, VECS, yu, yd, xu, xd, y2u, y2d, rows
        )
        weights = Level(
            (cf, cm, cc), wzr, wzl, slice(PAIR, PAIR + 8), 8, wyu, wyd, wxu, wxd, apart=True
        )
        targets = (
            (wa_ref, rows, rows_at(ef.shape[0], step)),
            (basis_ref, rows_at(PAIR, step), rows_at(HALF + PAIR, step)),
        )
        smooth_block(values, weights, cf, targets)
    gram[...] = gram_of(basis_ref, size)


def smooth_block(values, weights, cf, targets):
    lane = lanes_of(VECS)
    double = pair_matrix(True)

    own, beyond = faces(CX, CY)
    coarse_cells = own + beyond
    smoothed = []
    for cell in coarse_cells:
        here = values.coarse(*cell)
        around = [values.coarse(*other) for other in neighbours(*cell)]
        around += [turn(here, 1), turn(here, -1)]
        smoothed.append(smooth_tile(weights.coarse(*cell), here, around))
    doubled = dot(stack(smoothed), double)
    to_middle = {}
    for k, cell in enumerate(coarse_cells):
        ends = jnp.where(lane < 96, turn(smoothed[k], 32), smoothed[k])
        inner = doubled[VECS * k : VECS * (k + 1)]
        to_middle[cell] = jnp.where(lane < 64, inner, ends)

    own, beyond = faces(MX, MY)
    middle_cells = own + beyond
    smoothed = []
    for cell in middle_cells:
        here = values.middle(*cell)
        around = [values.middle(*other) for other in neighbours(*cell)]
        around += [turn(here, 1), turn(here, -1)]
        part = smooth_tile(weights.middle(*cell), here, around)
        smoothed.append(part + to_middle[cell[0] // 2, cell[1] // 2])
    doubled = dot(stack(smoothed), double)
    to_fine, to_end = {}, {}
    for k, cell in enumerate(middle_cells):
        to_fine[cell] = doubled[VECS * k : VECS * (k + 1)]
        to_end[cell] = jnp.where(lane < HALF, turn(smoothed[k], 64), smoothed[k])

    def zs(main, end):
        low = jnp.where(lane > 0, turn(main, 1), turn(end, 1))
        high = jnp.where(lane < LANES - 1, turn(main, -1), turn(end, -1))
        return [low, high]

    own, beyond = faces(LX, LY)
    found, found_end = {}, {}
    for cell in beyond + own:
        here, end = values.fine(*cell), values.fine_end(*cell)
        around = [values.fine(*other) for other in neighbours(*cell)] + zs(here, end)
        part = smooth_tile(weights.fine(*cell), here, around)
        found[cell] = part + to_fine[cell[0] // 2, cell[1] // 2]
    for cell in own:
        here, end = values.fine(*cell), values.fine_end(*cell)
        around = [values.fine_end(*other) for other in neighbours(*cell)] + zs(end, here)
        part = smooth_tile(weights.fine_end(*cell), end, around)
        found_end[cell] = part + to_end[cell[0] // 2, cell[1] // 2]
    for cell in own:
        k = cell[0] * LY + cell[1]
        here = found[cell]
        factors = tile(cf, k)
        around = [found[other] for other in neighbours(*cell)] + zs(here, found_end[cell])
        applied = factors[6:7] * here - spread(factors, around)
        columns = slice(k * LANES, (k + 1) * LANES)
        for ref, first, second in targets:
            ref[first, columns] = here
            ref[second, columns] = applied


def symmetric(summed):
    size = summed.shape[0]
    lane = lanes_of(size)
    flipped = lower_pad(summed).T
    sym_b = 0.5 * (summed + flipped[:size])
    sym_a = 0.5 * (turn(summed, HALF) + flipped[HALF : HALF + size])
    return jnp.where(lane < size, sym_b, 0.0), jnp.where(lane < size, sym_a, 0.0)


def judge_kernel(summed, gram, change, flag):
    size = 3 * VECS
    sym_b, sym_a = symmetric(summed[...])
    lane, row = lanes_of(VECS), rows_of(VECS)
    projected = solve_projected(
        jnp.where(lane < VECS, sym_b[:VECS], 0.0), jnp.where(lane < VECS, sym_a[:VECS], 0.0)
    )
    projected = jnp.where(lane < VECS, projected, 0.0)
    backward = turn(lower_pad(projected).T[:VECS], PAIR)
    direct = jnp.where(lanes_of(PAIR) == rows_of(PAIR), 1.0, 0.0).astype(F32)
    tail = jnp.where(lane == row + 3 * VECS, 1.0, 0.0).astype(F32) - backward
    mixing = stack([direct, tail])
    padded = lower_pad(mixing)
    small_b = dot(dot(mixing[:, :HALF], sym_b), padded, (1, 1))
    small_a = dot(dot(mixing[:, :HALF], sym_a), padded, (1, 1))
    gram[...] = jnp.where(lanes_of(size) < HALF, small_b, turn(small_a, HALF))
    change[...] = mixing
    lost = jnp.zeros((VECS, 1), F32)
    for small, full in ((small_b, sym_b), (small_a, sym_a)):
        after = jnp.where(lane == row + PAIR, small[PAIR:], 0.0)
        before = jnp.where(lane == row + 3 * VECS, full[3 * VECS :], 0.0)
        after = jnp.sum(after, axis=1, keepdims=True)
        before = jnp.sum(before, axis=1, keepdims=True)
        lost = jnp.maximum(lost, jnp.where(after > KEEP * before, 0.0, 1.0))
    flag[...] = jnp.broadcast_to(jnp.max(lost, axis=0, keepdims=True), (8, LANES))


def combine(coefficients, change, sources, targets):
    lane = lanes_of(VECS)
    both = stack([coefficients, jnp.where(lane >= VECS, coefficients, 0.0)])
    if change is not None:
        both = dot(both[:, : 3 * VECS], change)
    count = sources[0][1].stop - sources[0][1].start
    both = both[:, : PAIR + count]
    width = 8 * LANES

    def part(step, carry):
        columns = pl.ds(pl.multiple_of(step * width, width), width)
        for (old, rows, found), target in zip(sources, targets):
            target[:, columns] = dot(both, stack([old[:, columns], found[rows, columns]]))
        return carry

    lax.fori_loop(0, FINE * LANES // width, part, 0)


def mixed_kernel(
    gram, change, xp_ref, axp_ref, wa_ref, cf, cm, cc, nxp, naxp, ef, em, ec, zr, zl
):
    coefficients, projected = ritz(gram[...])
    own, applied = slice(0, PAIR), slice(PAIR, 2 * PAIR)
    sources = ((xp_ref, own, wa_ref), (axp_ref, applied, wa_ref))
    combine(coefficients, change[...], sources, (nxp, naxp))
    residual = naxp[:VECS] - dot(projected[:, :VECS], nxp[:VECS], (0, 0))
    level_parts(residual, cf, cm, cc, ef, em, ec)
    pack_z(ef, em, ec, cf, cm, cc, zr, zl)


def careful_kernel(change, xp_ref, axp_ref, wide_ref, gram, basis_ref):
    part = change[PAIR:, PAIR:HALF]
    blank = jnp.zeros((VECS, FINE * LANES), F32)
    for at, values, rows in ((0, xp_ref, slice(0, PAIR)), (HALF, axp_ref, slice(PAIR, 2 * PAIR))):
        basis_ref[at : at + PAIR] = values[...]
        basis_ref[at + PAIR : at + 3 * VECS] = dot(part, wide_ref[rows])
        basis_ref[at + 3 * VECS : at + HALF] = blank
    gram[...] = gram_of(basis_ref, 3 * VECS, 16)


def last_kernel(summed, xp_ref, wa_ref, x_out, p_out, moved):
    coefficients, _ = ritz(summed[...])
    combine(coefficients, None, ((xp_ref, slice(0, VECS), wa_ref),), (moved,))
    for k in range(FINE):
        x_out[pl.ds(k, VECS, stride=FINE), :] = tile(moved, k, slice(0, VECS))
        p_out[pl.ds(k, VECS, stride=FINE), :] = tile(moved, k, slice(VECS, PAIR))


def shifted(values, axis, by):
    peers = lax.axis_size(axis)
    return lax.ppermute(values, axis, [(i, (i + by) % peers) for i in range(peers)])


def masks_of(size):
    return {1: [], 2: [1], 4: [1, 3], 8: [1, 2, 6]}[size]


def all_sum(values):
    rounds = [(k, axis, m) for axis in ("gy", "gx", "gz") for k, m in enumerate(masks_of(lax.axis_size(axis)))]
    for _, axis, mask in sorted(rounds, key=lambda entry: entry[0]):
        pairs = [(i, i ^ mask) for i in range(lax.axis_size(axis))]
        values = values + lax.ppermute(values, axis, pairs)
    return values


def exchange(parts, weights, zr, zl):
    ec = parts[2]
    count = ec.shape[0]
    extra = (4, 2) if zr.shape[0] > count else (0, 0)
    zr, zl = shifted(zr, "gz", 1), shifted(zl, "gz", -1)
    y2u, y2d = shifted(ec, "gy", 2), shifted(ec, "gy", -2)
    shape = (count, (Y_TILES + extra[0]) * LANES)
    yu, yd = run(pack_y_kernel, [shape] * 2, (*parts, *weights, zr, zl))
    yu, yd = shifted(yu, "gy", 1), shifted(yd, "gy", -1)
    shape = (count, (X_TILES + extra[1]) * LANES)
    xu, xd = run(pack_x_kernel, [shape] * 2, (*parts, *weights, zr, zl, yu, yd, y2u, y2d))
    xu, xd = shifted(xu, "gx", 1), shifted(xd, "gx", -1)
    return (zr, zl, yu, yd, xu, xd), (y2u, y2d)


def on_device(x_block, p_block, voxel_class, conductance):
    sizes = [lax.axis_size(axis) for axis in ("gx", "gy", "gz")]
    all_cells = FINE * LANES * sizes[0] * sizes[1] * sizes[2]
    wide = FINE * LANES
    flags = []
    for axis, size in zip(("gx", "gy", "gz"), sizes):
        at = lax.axis_index(axis)
        flags += [at > 0, at < size - 1]
    flags = jnp.stack(flags).astype(F32)
    far = (
        x_block.reshape(VECS * FINE, LANES),
        p_block.reshape(VECS * FINE, LANES),
        voxel_class.reshape(FINE, LANES),
    )
    if not INTERPRET:
        far = [pltpu.with_memory_space_constraint(array, pltpu.HBM) for array in far]
    sides = [(40, wide)] + [(40, LANES)] * 2 + [(40, LX * LANES)] * 2 + [(40, LY * LANES)] * 2
    field, zr, zl, yu, yd, xu, xd = pl.pallas_call(
        start_kernel,
        out_shape=[SHAPE(shape, F32) for shape in sides],
        in_specs=[pl.BlockSpec(memory_space=pltpu.SMEM)]
        + [pl.BlockSpec(memory_space=pltpu.HBM)] * 3,
        out_specs=[pl.BlockSpec(memory_space=pltpu.VMEM)] * len(sides),
        scratch_shapes=[pltpu.VMEM((VECS * FINE, LANES), F32)] * 2
        + [pltpu.VMEM((FINE, LANES), jnp.int32), pltpu.SemaphoreType.DMA((3,))],
        compiler_params=pltpu.CompilerParams(vmem_limit_bytes=GRANT),
        interpret=INTERPRET,
    )(
        conductance,
        *far,
    )
    arrived = (
        shifted(zr, "gz", 1), shifted(zl, "gz", -1), shifted(yu, "gy", 1),
        shifted(yd, "gy", -1), shifted(xu, "gx", 1), shifted(xd, "gx", -1),
    )
    fields = [(PAIR, wide)] * 2
    weight_shapes = [(8, wide), (8, MIDDLE * LANES), (8, COARSE * LANES)]

    def part_shapes(rows):
        return [(rows, wide), (rows, MIDDLE * LANES), (rows, COARSE * LANES)]

    xp, axp, cf, cm, cc, *parts, zr, zl = run(
        first_kernel,
        fields + weight_shapes + part_shapes(PAIR) + [(PAIR + 8, LANES)] * 2,
        (field, *arrived),
        (flags,),
    )
    weights = (cf, cm, cc)
    basis = [(2 * HALF, wide)]

    def search(parts, sent, far, sent_weights):
        rows = parts[0].shape[0]
        inputs = (xp, axp, *parts, *weights, *sent, *far, *sent_weights)
        shapes = [(2 * rows, wide), (PAIR + rows, LANES)]
        return run(search_kernel, shapes, inputs, scratch=basis)

    sent_weights, far = exchange(parts, weights, zr, zl)
    wa, gram = search(parts, sent_weights, far, sent_weights)
    summed = all_sum(gram) * (1.0 / all_cells)
    small = (3 * VECS, LANES)
    gram, change, flag = run(judge_kernel, [small, small, (8, LANES)], (summed,))
    nexts = fields + part_shapes(VECS) + [(VECS, LANES)] * 2

    def careful(gram, change, wa):
        (gram,) = run(careful_kernel, [small], (change, xp, axp, wa), scratch=basis)
        return lax.psum(gram, ("gx", "gy", "gz")) * (1.0 / all_cells)

    def given(gram, change, wa):
        return gram

    gram = lax.cond(flag[0, 0] > 0.5, careful, given, gram, change, wa)
    xp, axp, *parts, zr, zl = run(mixed_kernel, nexts, (gram, change, xp, axp, wa, *weights))
    sent, far = exchange(parts, weights, zr, zl)
    wa, gram = search(parts, sent, far, sent_weights)
    gram = all_sum(gram) * (1.0 / all_cells)
    outs = [(VECS * FINE, LANES)] * 2
    x_out, p_out = run(last_kernel, outs, (gram, xp, wa), scratch=[(PAIR, wide)])
    return (x_out.reshape(x_block.shape), p_out.reshape(x_block.shape))


def solution(mesh):
    in_specs = (P(None, "gx", "gy", "gz"), P(None, "gx", "gy", "gz"), P("gx", "gy", "gz"), P())
    out_specs = (P(None, "gx", "gy", "gz"), P(None, "gx", "gy", "gz"))
    return jax.shard_map(
        on_device, mesh=mesh, in_specs=in_specs, out_specs=out_specs, check_vma=False
    )
```

```python
import jax
import jax.numpy as jnp
from jax import lax
from jax.experimental import pallas as pl
from jax.experimental.pallas import tpu as pltpu
from jax.sharding import PartitionSpec as P

VECS = 16
CLASSES = 8
ITERS = 2
INNER = 4
INTERPRET = False
GRANT = 24 * 1024 * 1024
PAIR = 2 * VECS
KEEP = 0.02

jacobi_weight = 2.0 / 3.0
mass_shift = 0.05

LX, LY, LANES = 8, 4, 128
MX, MY = LX // 2, LY // 2
CX, CY = LX // 4, LY // 4
FINE, MIDDLE, COARSE = LX * LY, MX * MY, CX * CY
SHAPE = jax.ShapeDtypeStruct
F32 = jnp.float32
HALF = LANES // 2


def tile(ref, index, rows=slice(None)):
    return ref[rows, index * LANES : (index + 1) * LANES]


def lanes_of(rows=8):
    return lax.broadcasted_iota(jnp.int32, (rows, LANES), 1)


def rows_of(rows):
    return lax.broadcasted_iota(jnp.int32, (rows, LANES), 0)


def turn(value, shift):
    shift = shift % LANES
    return value if shift == 0 else pltpu.roll(value, shift, 1)


def dot(left, right, contract=(1, 0)):
    return lax.dot_general(
        left,
        right,
        (((contract[0],), (contract[1],)), ((), ())),
        precision=lax.Precision.HIGHEST,
        preferred_element_type=F32,
    )


def pair_matrix(transposed):
    wide = lax.broadcasted_iota(jnp.int32, (LANES, LANES), 1 if transposed else 0)
    narrow = lax.broadcasted_iota(jnp.int32, (LANES, LANES), 0 if transposed else 1)
    return jnp.where(wide // 2 == narrow, 1.0, 0.0).astype(F32)


def stack(values):
    return jnp.concatenate(values, axis=0)


def run(body, outs, vmem, smem=(), scratch=()):
    in_specs = [pl.BlockSpec(memory_space=pltpu.SMEM)] * len(smem)
    in_specs += [pl.BlockSpec(memory_space=pltpu.VMEM)] * len(vmem)
    return pl.pallas_call(
        body,
        out_shape=[SHAPE(shape, F32) for shape in outs],
        in_specs=in_specs,
        out_specs=[pl.BlockSpec(memory_space=pltpu.VMEM)] * len(outs),
        scratch_shapes=[pltpu.VMEM(shape, F32) for shape in scratch],
        compiler_params=pltpu.CompilerParams(vmem_limit_bytes=GRANT),
        interpret=INTERPRET,
    )(*smem, *vmem)


def start_kernel(
    cond_ref, x_far, p_far, class_far, field_ref, zr, zl, yu, yd, xu, xd,
    x_ref, p_ref, class_ref, done,
):
    fetches = [
        pltpu.make_async_copy(far, near, done.at[k])
        for k, (far, near) in enumerate(
            ((class_far, class_ref), (x_far, x_ref), (p_far, p_ref))
        )
    ]
    for fetch in fetches:
        fetch.start()
    for fetch in fetches:
        fetch.wait()
    classes = class_ref[...]
    local = jnp.zeros(classes.shape, F32)
    for index in range(CLASSES):
        local = local + jnp.where(classes == index, cond_ref[index], 0.0)
    lane = lanes_of(40)
    right = jnp.zeros((40, LANES), F32)
    left = jnp.zeros((40, LANES), F32)
    for x in range(LX):
        for y in range(LY):
            p = x * LY + y
            cell = stack(
                [
                    x_ref[pl.ds(p, VECS, stride=FINE), :],
                    p_ref[pl.ds(p, VECS, stride=FINE), :],
                    jnp.broadcast_to(local[p : p + 1], (8, LANES)),
                ]
            )
            field_ref[:, p * LANES : (p + 1) * LANES] = cell
            right = jnp.where(lane == p, turn(cell, p + 1), right)
            left = jnp.where(lane == p, turn(cell, p), left)
            if y == LY - 1:
                yu[:, x * LANES : (x + 1) * LANES] = cell
            if y == 0:
                yd[:, x * LANES : (x + 1) * LANES] = cell
            if x == LX - 1:
                xu[:, y * LANES : (y + 1) * LANES] = cell
            if x == 0:
                xd[:, y * LANES : (y + 1) * LANES] = cell
    zr[...] = right
    zl[...] = left


def finish_weights(weights, shift_term):
    row = rows_of(8)
    weights = jnp.where(row < 6, weights, 0.0)
    diagonal = shift_term + jnp.sum(weights, axis=0, keepdims=True)
    return jnp.where(
        row < 6, weights, jnp.where(row == 6, diagonal, jacobi_weight / diagonal)
    )


def coarsen_weights(fine, size_x, size_y, shift_term, halve):
    row, lane = rows_of(8), lanes_of(8)
    sums = []
    for x in range(size_x):
        for y in range(size_y):
            total = jnp.zeros((8, LANES), F32)
            for i in range(2):
                for j in range(2):
                    keep = (row == i) | (row == 2 + j)
                    keep = keep | ((row == 4) & (lane % 2 == 0)) | ((row == 5) & (lane % 2 == 1))
                    total = total + jnp.where(keep, fine[2 * x + i, 2 * y + j], 0.0)
            sums.append(total)
    paired = dot(stack(sums), halve)
    return {
        (k // size_y, k % size_y): finish_weights(paired[8 * k : 8 * k + 8], shift_term)
        for k in range(size_x * size_y)
    }


def first_kernel(flag_ref, field_ref, zr, zl, yu, yd, xu, xd, xp_ref, axp_ref, cf, cm, cc, ef, em, ec, szr, szl):
    lane, row = lanes_of(8), rows_of(8)
    lane40 = lanes_of(40)
    from_low, from_high = zr[...], zl[...]
    flags = [flag_ref[k] for k in range(6)]
    ends = jnp.where((row == 4) & (lane == 0), flags[4], 1.0)
    ends = jnp.where((row == 5) & (lane == LANES - 1), flags[5], ends)
    fine = {}
    for x in range(LX):
        for y in range(LY):
            p = x * LY + y
            here = tile(field_ref, p)
            beside = [
                tile(field_ref, p - LY) if x > 0 else tile(xu, y),
                tile(field_ref, p + LY) if x < LX - 1 else tile(xd, y),
                tile(field_ref, p - 1) if y > 0 else tile(yu, x),
                tile(field_ref, p + 1) if y < LY - 1 else tile(yd, x),
                jnp.where(lane40 == 0, turn(from_low, -p), turn(here, 1)),
                jnp.where(lane40 == LANES - 1, turn(from_high, LANES - 1 - p), turn(here, -1)),
            ]
            around = stack([value[32:33] for value in beside] + [here[32:34]])
            own = here[32:40]
            keep = ends
            for side, at_end in enumerate((x == 0, x == LX - 1, y == 0, y == LY - 1)):
                if at_end:
                    keep = jnp.where(row == side, flags[side], keep)
            weights = finish_weights(2.0 * around * own / (around + own) * keep, mass_shift)
            fine[x, y] = weights
            cf[:, p * LANES : (p + 1) * LANES] = weights
            applied = weights[6:7] * here[:32]
            for side in range(6):
                applied = applied - weights[side : side + 1] * beside[side][:32]
            xp_ref[:, p * LANES : (p + 1) * LANES] = here[:32]
            axp_ref[:, p * LANES : (p + 1) * LANES] = applied
    halve = pair_matrix(False)
    middle = coarsen_weights(fine, MX, MY, 8.0 * mass_shift, halve)
    for (x, y), value in middle.items():
        k = x * MY + y
        cm[:, k * LANES : (k + 1) * LANES] = value
    coarse = coarsen_weights(middle, CX, CY, 64.0 * mass_shift, halve)
    for (x, y), value in coarse.items():
        cc[:, x * LANES : (x + 1) * LANES] = value
    level_parts(stack([xp_ref[:VECS], axp_ref[:VECS]]), cf, cm, cc, ef, em, ec)
    pack_z(ef, em, ec, cf, cm, cc, szr, szl)


def eliminate(rows, size, full):
    tiles = [rows[8 * i : 8 * i + 8] for i in range(rows.shape[0] // 8)]
    row = rows_of(8)
    kept = list(tiles)
    nothing = rows[:8] * 0.0
    for k in range(0, size, 2):
        at, sub = divmod(k, 8)
        spread_left = tiles[at][:, k : k + 1] + nothing
        spread_right = tiles[at][:, k + 1 : k + 2] + nothing

        def line(value, which):
            return jnp.broadcast_to(value[sub + which : sub + which + 1], (8, LANES))

        first, second = line(tiles[at], 0), line(tiles[at], 1)
        a, b = line(spread_left, 0), line(spread_right, 0)
        c, d = line(spread_left, 1), line(spread_right, 1)
        crossed = a * second - c * first
        inverse = 1.0 / (a * d - b * c)
        solved_first = (d * first - b * second) * inverse
        solved_second = crossed * inverse
        if not full:
            kept[at] = jnp.where(row == sub, first * (1.0 / jnp.sqrt(a)), kept[at])
            root = jnp.sqrt(inverse) * (1.0 / jnp.sqrt(a))
            kept[at] = jnp.where(row == sub + 1, crossed * root, kept[at])
        for i in range(len(tiles)):
            if i < at and not full:
                continue
            if i == at:
                left, right = spread_left, spread_right
            else:
                left, right = tiles[i][:, k : k + 1], tiles[i][:, k + 1 : k + 2]
            changed = tiles[i] - (left * solved_first + right * solved_second)
            if i == at:
                changed = jnp.where(row == sub, solved_first, changed)
                changed = jnp.where(row == sub + 1, solved_second, changed)
            tiles[i] = changed
    return stack(tiles if full else kept)


def lower_pad(matrix):
    missing = LANES - matrix.shape[0]
    return stack([matrix, jnp.zeros((missing, LANES), F32)])


def solve_projected(gram, cross):
    lane = lanes_of(VECS)
    on_diagonal = jnp.where((lane == rows_of(VECS)) & (lane < VECS), gram, 0.0)
    column = 1.0 / jnp.sqrt(jnp.sum(on_diagonal, axis=1, keepdims=True))
    across = jnp.sum(on_diagonal, axis=0, keepdims=True)
    across = jnp.where(lanes_of(1) < VECS, 1.0 / jnp.sqrt(across), 0.0)
    both = jnp.where(lane < HALF, gram * across, turn(cross, HALF)) * column
    return turn(eliminate(both, VECS, True), HALF) * column


def ritz(summed):
    size = 3 * VECS
    lane, row = lanes_of(size), rows_of(size)
    sym_b, sym_a = symmetric(summed)
    on_diagonal = jnp.where(lane == row, sym_b, 0.0)
    column = 1.0 / jnp.sqrt(jnp.sum(on_diagonal, axis=1, keepdims=True))
    across = jnp.sum(on_diagonal, axis=0, keepdims=True)
    across = jnp.where(lanes_of(1) < size, 1.0 / jnp.sqrt(across), 0.0)
    normed_b = sym_b * column * across
    normed_a = sym_a * column * across
    done = eliminate(jnp.where(lane < HALF, normed_a, turn(normed_b, HALF)), size, True)
    step = jnp.where(lane < size, turn(done, HALF), 0.0)
    weighed = dot(normed_b[:, :size], step)
    step_pad, weighed_pad = lower_pad(step), lower_pad(weighed)
    short_lane = lanes_of(VECS)

    def inner_step(_, basis):
        mapped = dot(basis, step_pad, (1, 1))
        product = dot(basis, weighed_pad, (1, 1))
        square = dot(product, lower_pad(mapped), (1, 1))
        done = eliminate(jnp.where(short_lane < HALF, square, turn(mapped, HALF)), VECS, False)
        return jnp.where(short_lane < size, turn(done, HALF), 0.0)

    basis = jnp.where(short_lane == rows_of(VECS), 1.0, 0.0).astype(F32)
    basis = lax.fori_loop(0, INNER, inner_step, basis)
    cross = dot(dot(basis, lower_pad(normed_a), (1, 1)), lower_pad(basis), (1, 1))
    return basis * across, cross


def level_parts(residual, cf, cm, cc, ef, em, ec):
    count = residual.shape[0]
    halve = pair_matrix(False)
    sums = []
    for mx in range(MX):
        for my in range(MY):
            total = jnp.zeros((count, LANES), F32)
            for i in range(2):
                for j in range(2):
                    p = (2 * mx + i) * LY + 2 * my + j
                    part = residual[:, p * LANES : (p + 1) * LANES]
                    total = total + part
                    ef[:, p * LANES : (p + 1) * LANES] = part * tile(cf, p, slice(7, 8))
            sums.append(total)
    paired = dot(stack(sums), halve)
    middle = [paired[count * k : count * (k + 1)] for k in range(MIDDLE)]
    for k in range(MIDDLE):
        em[:, k * LANES : (k + 1) * LANES] = middle[k] * tile(cm, k, slice(7, 8))
    sums = []
    for cx in range(CX):
        sums.append(sum(middle[(2 * cx + i) * MY + j] for i in range(2) for j in range(2)))
    paired = dot(stack(sums), halve)
    for k in range(COARSE):
        coarse = paired[count * k : count * (k + 1)]
        ec[:, k * LANES : (k + 1) * LANES] = coarse * tile(cc, k, slice(7, 8))


def pack_z(ef, em, ec, cf, cm, cc, zr, zl):
    rows = zr.shape[0]
    lane = lanes_of(rows)

    def cell(values, weights, k):
        here = tile(values, k)
        return stack([here, tile(weights, k)]) if rows > values.shape[0] else here

    right = jnp.zeros((rows, LANES), F32)
    left = jnp.zeros((rows, LANES), F32)
    levels = ((ef, cf, FINE, 0, 126), (em, cm, MIDDLE, 64, 62), (ec, cc, COARSE, 80, 30))
    for values, weights, count, base, last in levels:
        for k in range(count):
            here = cell(values, weights, k)
            spot = base + 2 * k
            right = jnp.where(lane // 2 == spot // 2, turn(here, spot - last), right)
            left = jnp.where(lane // 2 == spot // 2, turn(here, spot), left)
    zr[...] = right
    zl[...] = left


Y_TILES, X_TILES = 25, 17


def apart_tile(ref, base, k):
    return tile(ref, base + k // 4, slice(8 * (k % 4), 8 * (k % 4) + 8))


class Level:
    def __init__(
        self, own, low, high, rows, count, yu=None, yd=None, xu=None, xd=None,
        y2u=None, y2d=None, inner=slice(None), apart=False,
    ):
        self.own, self.inner, self.apart = own, inner, apart
        self.low, self.high = low[rows], high[rows]
        self.yu, self.yd, self.xu, self.xd, self.y2u, self.y2d = yu, yd, xu, xd, y2u, y2d
        self.lane = lanes_of(count)
        self.kept = {}

    def once(self, key, make):
        if key not in self.kept:
            self.kept[key] = make()
        return self.kept[key]

    def own_rows(self, ref, k):
        return tile(ref, k, self.inner)

    def fine(self, x, y):
        if 0 <= x < LX and 0 <= y < LY:
            return self.own_rows(self.own[0], x * LY + y)
        if 0 <= x < LX:
            ref, layer = (self.yu, y + 2) if y < 0 else (self.yd, y - LY)
            if self.apart:
                return apart_tile(ref, Y_TILES, x)
            return tile(ref, 2 * x + layer, self.inner)
        ref, near = (self.xu, x == -1) if x < 0 else (self.xd, x == LX)
        if self.apart:
            return apart_tile(ref, X_TILES, y)
        return tile(ref, y + 1 if near else 6 + y, self.inner)

    def fine_end(self, x, y):
        def make():
            if 0 <= x < LX and 0 <= y < LY:
                p = x * LY + y
                return jnp.where(
                    self.lane < HALF, turn(self.high, -2 * p), turn(self.low, 126 - 2 * p)
                )
            if 0 <= x < LX:
                return turn(tile(self.yu if y < 0 else self.yd, 16, self.inner), -(1 + 2 * x))
            return turn(tile(self.xu if x < 0 else self.xd, 10, self.inner), -(1 + 2 * y))

        return self.once(("end", x, y), make)

    def middle(self, x, y):
        def make():
            if 0 <= x < MX and 0 <= y < MY:
                k = x * MY + y
                beyond = jnp.where(
                    self.lane < 96, turn(self.high, -2 * k), turn(self.low, 62 - 2 * k)
                )
                return jnp.where(self.lane < 64, self.own_rows(self.own[1], k), beyond)
            if 0 <= x < MX:
                ref = self.yu if y < 0 else self.yd
                if self.apart:
                    return apart_tile(ref, Y_TILES, LX + x)
                if y in (-1, MY):
                    return tile(ref, 17 + x, self.inner)
                return turn(tile(ref, 21 + x // 2, self.inner), -64 * (x % 2))
            ref, near = (self.xu, x == -1) if x < 0 else (self.xd, x == MX)
            if self.apart:
                return apart_tile(ref, X_TILES, LY + y)
            if not near:
                return turn(tile(ref, 14, self.inner), -64 * y)
            if 0 <= y < MY:
                return tile(ref, 11 + y, self.inner)
            return turn(tile(ref, 13, self.inner), 0 if y < 0 else -64)

        return self.once(("middle", x, y), make)

    def coarse(self, x, y):
        def make():
            if 0 <= x < CX and y == 0:
                beyond = jnp.where(
                    self.lane < 64, turn(self.high, -48 - 2 * x), turn(self.low, 46 - 2 * x)
                )
                return jnp.where(self.lane < 32, self.own_rows(self.own[2], x), beyond)
            if 0 <= x < CX:
                if abs(y) == 2:
                    return tile(self.y2u if y < 0 else self.y2d, x, self.inner)
                ref = self.yu if y < 0 else self.yd
                if self.apart:
                    return apart_tile(ref, Y_TILES, LX + MX + x)
                return tile(ref, 23 + x, self.inner)
            ref, near = (self.xu, x == -1) if x < 0 else (self.xd, x == CX)
            if self.apart:
                return apart_tile(ref, X_TILES, LY + MY)
            if near and y == 0:
                return tile(ref, 15, self.inner)
            return turn(tile(ref, 16, self.inner), -64 if not near else 0 if y < 0 else -32)

        return self.once(("coarse", x, y), make)


def put(ref, index, value):
    ref[:, index * LANES : (index + 1) * LANES] = value


def pack_ends(values):
    rows = values[0].shape[0]
    lane = lanes_of(rows)
    packed = jnp.zeros((rows, LANES), F32)
    for k, value in enumerate(values):
        packed = jnp.where(lane // 2 == k, turn(value, 1 + 2 * k), packed)
    return packed


def halves(left, right):
    return jnp.where(lanes_of(left.shape[0]) < HALF, left, turn(right, HALF))


def put_apart(ref, base, weights):
    if ref.shape[1] == base * LANES:
        return
    for k in range(0, len(weights), 4):
        group = weights[k : k + 4]
        put(ref, base + k // 4, stack(group + group[:1] * (4 - len(group))))


def pack_y_kernel(ef, em, ec, cf, cm, cc, zr, zl, yu, yd):
    count = ef.shape[0]
    level = Level((ef, em, ec), zr, zl, slice(0, count), count)
    for ref, first, edge, near, far in ((yu, LY - 2, LY - 1, MY - 1, 0), (yd, 0, 0, 0, MY - 1)):
        for x in range(LX):
            for j in range(2):
                put(ref, 2 * x + j, level.fine(x, first + j))
        put(ref, 16, pack_ends([level.fine_end(x, edge) for x in range(LX)]))
        for x in range(MX):
            put(ref, 17 + x, level.middle(x, near))
        for k in range(MX // 2):
            put(ref, 21 + k, halves(level.middle(2 * k, far), level.middle(2 * k + 1, far)))
        for x in range(CX):
            put(ref, 23 + x, level.coarse(x, 0))
        weights = [tile(cf, x * LY + edge) for x in range(LX)]
        weights += [tile(cm, x * MY + near) for x in range(MX)]
        put_apart(ref, Y_TILES, weights + [tile(cc, x) for x in range(CX)])


def pack_x_kernel(ef, em, ec, cf, cm, cc, zr, zl, ryu, ryd, y2u, y2d, xu, xd):
    count = ef.shape[0]
    lane = lanes_of(count)
    level = Level((ef, em, ec), zr, zl, slice(0, count), count, ryu, ryd)
    for ref, up in ((xu, True), (xd, False)):
        near, far = (LX - 1, LX - 2) if up else (0, 1)
        for y in range(-1, LY + 1):
            put(ref, y + 1, level.fine(near, y))
        for y in range(LY):
            put(ref, 6 + y, level.fine(far, y))
        put(ref, 10, pack_ends([level.fine_end(near, y) for y in range(LY)]))
        weights = [tile(cf, near * LY + y) for y in range(LY)]
        near, far = (MX - 1, MX - 2) if up else (0, 1)
        for y in range(MY):
            put(ref, 11 + y, level.middle(near, y))
        put(ref, 13, halves(level.middle(near, -1), level.middle(near, MY)))
        put(ref, 14, halves(level.middle(far, 0), level.middle(far, 1)))
        weights += [tile(cm, near * MY + y) for y in range(MY)]
        near, far = (CX - 1, CX - 2) if up else (0, 1)
        put(ref, 15, level.coarse(near, 0))
        ends = jnp.where(lane < 32, level.coarse(near, -1), turn(level.coarse(near, 1), 32))
        put(ref, 16, halves(ends, level.coarse(far, 0)))
        put_apart(ref, X_TILES, weights + [tile(cc, near)])


def faces(size_x, size_y):
    own = [(x, y) for x in range(size_x) for y in range(size_y)]
    beyond = [(x, y) for x in (-1, size_x) for y in range(size_y)]
    beyond += [(x, y) for x in range(size_x) for y in (-1, size_y)]
    return own, beyond


def neighbours(x, y):
    return ((x - 1, y), (x + 1, y), (x, y - 1), (x, y + 1))


def spread(weights, values):
    total = weights[0:1] * values[0]
    for side in range(1, 6):
        total = total + weights[side : side + 1] * values[side]
    return total


def smooth_tile(weights, here, values):
    return (2.0 * jacobi_weight) * here + weights[7:8] * spread(weights, values)


def search_kernel(
    xp_ref, axp_ref, ef, em, ec, cf, cm, cc,
    zr, zl, yu, yd, xu, xd, y2u, y2d,
    wzr, wzl, wyu, wyd, wxu, wxd,
    wa_ref, gram, basis_ref,
):
    size = PAIR + ef.shape[0]
    basis_ref[:PAIR] = xp_ref[...]
    basis_ref[HALF : HALF + PAIR] = axp_ref[...]
    if size < HALF:
        blank = jnp.zeros((HALF - size, FINE * LANES), F32)
        basis_ref[size:HALF] = blank
        basis_ref[HALF + size :] = blank

    def rows_at(start, step):
        return slice(start + step * VECS, start + (step + 1) * VECS)

    for step in range((size - PAIR) // VECS):
        rows = rows_at(0, step)
        values = Level(
            (ef, em, ec), zr, zl, rows, VECS, yu, yd, xu, xd, y2u, y2d, rows
        )
        weights = Level(
            (cf, cm, cc), wzr, wzl, slice(PAIR, PAIR + 8), 8, wyu, wyd, wxu, wxd, apart=True
        )
        targets = (
            (wa_ref, rows, rows_at(ef.shape[0], step)),
            (basis_ref, rows_at(PAIR, step), rows_at(HALF + PAIR, step)),
        )
        smooth_block(values, weights, cf, targets)
    gram[...] = dot(basis_ref[:size], basis_ref[...], (1, 1))


def smooth_block(values, weights, cf, targets):
    lane = lanes_of(VECS)
    double = pair_matrix(True)

    own, beyond = faces(CX, CY)
    coarse_cells = own + beyond
    smoothed = []
    for cell in coarse_cells:
        here = values.coarse(*cell)
        around = [values.coarse(*other) for other in neighbours(*cell)]
        around += [turn(here, 1), turn(here, -1)]
        smoothed.append(smooth_tile(weights.coarse(*cell), here, around))
    doubled = dot(stack(smoothed), double)
    to_middle = {}
    for k, cell in enumerate(coarse_cells):
        ends = jnp.where(lane < 96, turn(smoothed[k], 32), smoothed[k])
        inner = doubled[VECS * k : VECS * (k + 1)]
        to_middle[cell] = jnp.where(lane < 64, inner, ends)

    own, beyond = faces(MX, MY)
    middle_cells = own + beyond
    smoothed = []
    for cell in middle_cells:
        here = values.middle(*cell)
        around = [values.middle(*other) for other in neighbours(*cell)]
        around += [turn(here, 1), turn(here, -1)]
        part = smooth_tile(weights.middle(*cell), here, around)
        smoothed.append(part + to_middle[cell[0] // 2, cell[1] // 2])
    doubled = dot(stack(smoothed), double)
    to_fine, to_end = {}, {}
    for k, cell in enumerate(middle_cells):
        to_fine[cell] = doubled[VECS * k : VECS * (k + 1)]
        to_end[cell] = jnp.where(lane < HALF, turn(smoothed[k], 64), smoothed[k])

    def zs(main, end):
        low = jnp.where(lane > 0, turn(main, 1), turn(end, 1))
        high = jnp.where(lane < LANES - 1, turn(main, -1), turn(end, -1))
        return [low, high]

    own, beyond = faces(LX, LY)
    found, found_end = {}, {}
    for cell in beyond + own:
        here, end = values.fine(*cell), values.fine_end(*cell)
        around = [values.fine(*other) for other in neighbours(*cell)] + zs(here, end)
        part = smooth_tile(weights.fine(*cell), here, around)
        found[cell] = part + to_fine[cell[0] // 2, cell[1] // 2]
    for cell in own:
        here, end = values.fine(*cell), values.fine_end(*cell)
        around = [values.fine_end(*other) for other in neighbours(*cell)] + zs(end, here)
        part = smooth_tile(weights.fine_end(*cell), end, around)
        found_end[cell] = part + to_end[cell[0] // 2, cell[1] // 2]
    for cell in own:
        k = cell[0] * LY + cell[1]
        here = found[cell]
        factors = tile(cf, k)
        around = [found[other] for other in neighbours(*cell)] + zs(here, found_end[cell])
        applied = factors[6:7] * here - spread(factors, around)
        columns = slice(k * LANES, (k + 1) * LANES)
        for ref, first, second in targets:
            ref[first, columns] = here
            ref[second, columns] = applied


def symmetric(summed):
    size = summed.shape[0]
    lane = lanes_of(size)
    flipped = lower_pad(summed).T
    sym_b = 0.5 * (summed + flipped[:size])
    sym_a = 0.5 * (turn(summed, HALF) + flipped[HALF : HALF + size])
    return jnp.where(lane < size, sym_b, 0.0), jnp.where(lane < size, sym_a, 0.0)


def judge_kernel(summed, gram, change, flag):
    size = 3 * VECS
    sym_b, sym_a = symmetric(summed[...])
    lane, row = lanes_of(VECS), rows_of(VECS)
    projected = solve_projected(
        jnp.where(lane < VECS, sym_b[:VECS], 0.0), jnp.where(lane < VECS, sym_a[:VECS], 0.0)
    )
    projected = jnp.where(lane < VECS, projected, 0.0)
    backward = turn(lower_pad(projected).T[:VECS], PAIR)
    direct = jnp.where(lanes_of(PAIR) == rows_of(PAIR), 1.0, 0.0).astype(F32)
    tail = jnp.where(lane == row + 3 * VECS, 1.0, 0.0).astype(F32) - backward
    mixing = stack([direct, tail])
    padded = lower_pad(mixing)
    small_b = dot(dot(mixing[:, :HALF], sym_b), padded, (1, 1))
    small_a = dot(dot(mixing[:, :HALF], sym_a), padded, (1, 1))
    gram[...] = jnp.where(lanes_of(size) < HALF, small_b, turn(small_a, HALF))
    change[...] = mixing
    lost = jnp.zeros((VECS, 1), F32)
    for small, full in ((small_b, sym_b), (small_a, sym_a)):
        after = jnp.where(lane == row + PAIR, small[PAIR:], 0.0)
        before = jnp.where(lane == row + 3 * VECS, full[3 * VECS :], 0.0)
        after = jnp.sum(after, axis=1, keepdims=True)
        before = jnp.sum(before, axis=1, keepdims=True)
        lost = jnp.maximum(lost, jnp.where(after > KEEP * before, 0.0, 1.0))
    flag[...] = jnp.broadcast_to(jnp.max(lost, axis=0, keepdims=True), (8, LANES))


def combine(coefficients, change, sources, targets):
    lane = lanes_of(VECS)
    both = stack([coefficients, jnp.where(lane >= VECS, coefficients, 0.0)])
    if change is not None:
        both = dot(both[:, : 3 * VECS], change)
    count = sources[0][1].stop - sources[0][1].start
    both = both[:, : PAIR + count]
    width = 8 * LANES

    def part(step, carry):
        columns = pl.ds(pl.multiple_of(step * width, width), width)
        for (old, rows, found), target in zip(sources, targets):
            target[:, columns] = dot(both, stack([old[:, columns], found[rows, columns]]))
        return carry

    lax.fori_loop(0, FINE * LANES // width, part, 0)


def mixed_kernel(
    gram, change, xp_ref, axp_ref, wa_ref, cf, cm, cc, nxp, naxp, ef, em, ec, zr, zl
):
    coefficients, projected = ritz(gram[...])
    own, applied = slice(0, PAIR), slice(PAIR, 2 * PAIR)
    sources = ((xp_ref, own, wa_ref), (axp_ref, applied, wa_ref))
    combine(coefficients, change[...], sources, (nxp, naxp))
    residual = naxp[:VECS] - dot(projected[:, :VECS], nxp[:VECS], (0, 0))
    level_parts(residual, cf, cm, cc, ef, em, ec)
    pack_z(ef, em, ec, cf, cm, cc, zr, zl)


def careful_kernel(change, xp_ref, axp_ref, wide_ref, gram, basis_ref):
    part = change[PAIR:, PAIR:HALF]
    blank = jnp.zeros((VECS, FINE * LANES), F32)
    for at, values, rows in ((0, xp_ref, slice(0, PAIR)), (HALF, axp_ref, slice(PAIR, 2 * PAIR))):
        basis_ref[at : at + PAIR] = values[...]
        basis_ref[at + PAIR : at + 3 * VECS] = dot(part, wide_ref[rows])
        basis_ref[at + 3 * VECS : at + HALF] = blank
    width = 2 * LANES

    def add(step, total):
        columns = pl.ds(pl.multiple_of(step * width, width), width)
        return total + dot(basis_ref[: 3 * VECS, columns], basis_ref[:, columns], (1, 1))

    total = jnp.zeros((3 * VECS, LANES), F32)
    gram[...] = lax.fori_loop(0, FINE * LANES // width, add, total)


def last_kernel(summed, xp_ref, wa_ref, x_out, p_out, moved):
    coefficients, _ = ritz(summed[...])
    combine(coefficients, None, ((xp_ref, slice(0, VECS), wa_ref),), (moved,))
    for k in range(FINE):
        x_out[pl.ds(k, VECS, stride=FINE), :] = tile(moved, k, slice(0, VECS))
        p_out[pl.ds(k, VECS, stride=FINE), :] = tile(moved, k, slice(VECS, PAIR))


def shifted(values, axis, by):
    peers = lax.axis_size(axis)
    return lax.ppermute(values, axis, [(i, (i + by) % peers) for i in range(peers)])


def masks_of(size):
    return {1: [], 2: [1], 4: [1, 3], 8: [1, 2, 6]}[size]


def all_sum(values):
    rounds = [(k, axis, m) for axis in ("gy", "gx", "gz") for k, m in enumerate(masks_of(lax.axis_size(axis)))]
    for _, axis, mask in sorted(rounds, key=lambda entry: entry[0]):
        pairs = [(i, i ^ mask) for i in range(lax.axis_size(axis))]
        values = values + lax.ppermute(values, axis, pairs)
    return values


def exchange(parts, weights, zr, zl):
    ec = parts[2]
    count = ec.shape[0]
    extra = (4, 2) if zr.shape[0] > count else (0, 0)
    zr, zl = shifted(zr, "gz", 1), shifted(zl, "gz", -1)
    y2u, y2d = shifted(ec, "gy", 2), shifted(ec, "gy", -2)
    shape = (count, (Y_TILES + extra[0]) * LANES)
    yu, yd = run(pack_y_kernel, [shape] * 2, (*parts, *weights, zr, zl))
    yu, yd = shifted(yu, "gy", 1), shifted(yd, "gy", -1)
    shape = (count, (X_TILES + extra[1]) * LANES)
    xu, xd = run(pack_x_kernel, [shape] * 2, (*parts, *weights, zr, zl, yu, yd, y2u, y2d))
    xu, xd = shifted(xu, "gx", 1), shifted(xd, "gx", -1)
    return (zr, zl, yu, yd, xu, xd), (y2u, y2d)


def on_device(x_block, p_block, voxel_class, conductance):
    sizes = [lax.axis_size(axis) for axis in ("gx", "gy", "gz")]
    all_cells = FINE * LANES * sizes[0] * sizes[1] * sizes[2]
    wide = FINE * LANES
    flags = []
    for axis, size in zip(("gx", "gy", "gz"), sizes):
        at = lax.axis_index(axis)
        flags += [at > 0, at < size - 1]
    flags = jnp.stack(flags).astype(F32)
    far = (
        x_block.reshape(VECS * FINE, LANES),
        p_block.reshape(VECS * FINE, LANES),
        voxel_class.reshape(FINE, LANES),
    )
    if not INTERPRET:
        far = [pltpu.with_memory_space_constraint(array, pltpu.HBM) for array in far]
    sides = [(40, wide)] + [(40, LANES)] * 2 + [(40, LX * LANES)] * 2 + [(40, LY * LANES)] * 2
    field, zr, zl, yu, yd, xu, xd = pl.pallas_call(
        start_kernel,
        out_shape=[SHAPE(shape, F32) for shape in sides],
        in_specs=[pl.BlockSpec(memory_space=pltpu.SMEM)]
        + [pl.BlockSpec(memory_space=pltpu.HBM)] * 3,
        out_specs=[pl.BlockSpec(memory_space=pltpu.VMEM)] * len(sides),
        scratch_shapes=[pltpu.VMEM((VECS * FINE, LANES), F32)] * 2
        + [pltpu.VMEM((FINE, LANES), jnp.int32), pltpu.SemaphoreType.DMA((3,))],
        compiler_params=pltpu.CompilerParams(vmem_limit_bytes=GRANT),
        interpret=INTERPRET,
    )(
        conductance,
        *far,
    )
    arrived = (
        shifted(zr, "gz", 1), shifted(zl, "gz", -1), shifted(yu, "gy", 1),
        shifted(yd, "gy", -1), shifted(xu, "gx", 1), shifted(xd, "gx", -1),
    )
    fields = [(PAIR, wide)] * 2
    weight_shapes = [(8, wide), (8, MIDDLE * LANES), (8, COARSE * LANES)]

    def part_shapes(rows):
        return [(rows, wide), (rows, MIDDLE * LANES), (rows, COARSE * LANES)]

    xp, axp, cf, cm, cc, *parts, zr, zl = run(
        first_kernel,
        fields + weight_shapes + part_shapes(PAIR) + [(PAIR + 8, LANES)] * 2,
        (field, *arrived),
        (flags,),
    )
    weights = (cf, cm, cc)
    basis = [(2 * HALF, wide)]

    def search(parts, sent, far, sent_weights):
        rows = parts[0].shape[0]
        inputs = (xp, axp, *parts, *weights, *sent, *far, *sent_weights)
        shapes = [(2 * rows, wide), (PAIR + rows, LANES)]
        return run(search_kernel, shapes, inputs, scratch=basis)

    sent_weights, far = exchange(parts, weights, zr, zl)
    wa, gram = search(parts, sent_weights, far, sent_weights)
    summed = all_sum(gram) * (1.0 / all_cells)
    small = (3 * VECS, LANES)
    gram, change, flag = run(judge_kernel, [small, small, (8, LANES)], (summed,))
    nexts = fields + part_shapes(VECS) + [(VECS, LANES)] * 2

    def careful(gram, change, wa):
        (gram,) = run(careful_kernel, [small], (change, xp, axp, wa), scratch=basis)
        return lax.psum(gram, ("gx", "gy", "gz")) * (1.0 / all_cells)

    def given(gram, change, wa):
        return gram

    gram = lax.cond(flag[0, 0] > 0.5, careful, given, gram, change, wa)
    xp, axp, *parts, zr, zl = run(mixed_kernel, nexts, (gram, change, xp, axp, wa, *weights))
    sent, far = exchange(parts, weights, zr, zl)
    wa, gram = search(parts, sent, far, sent_weights)
    gram = all_sum(gram) * (1.0 / all_cells)
    outs = [(VECS * FINE, LANES)] * 2
    x_out, p_out = run(last_kernel, outs, (gram, xp, wa), scratch=[(PAIR, wide)])
    return (x_out.reshape(x_block.shape), p_out.reshape(x_block.shape))


def solution(mesh):
    in_specs = (P(None, "gx", "gy", "gz"), P(None, "gx", "gy", "gz"), P("gx", "gy", "gz"), P())
    out_specs = (P(None, "gx", "gy", "gz"), P(None, "gx", "gy", "gz"))
    return jax.shard_map(
        on_device, mesh=mesh, in_specs=in_specs, out_specs=out_specs, check_vma=False
    )
```

```python
import jax
import jax.numpy as jnp
from jax import lax
from jax.experimental import pallas as pl
from jax.experimental.pallas import tpu as pltpu
from jax.sharding import PartitionSpec as P

VECS = 16
CLASSES = 8
ITERS = 2
INNER = 4
INTERPRET = False
GRANT = 24 * 1024 * 1024
PAIR = 2 * VECS
KEEP = 0.02

jacobi_weight = 2.0 / 3.0
mass_shift = 0.05

LX, LY, LANES = 8, 4, 128
MX, MY = LX // 2, LY // 2
CX, CY = LX // 4, LY // 4
FINE, MIDDLE, COARSE = LX * LY, MX * MY, CX * CY
SHAPE = jax.ShapeDtypeStruct
F32 = jnp.float32
HALF = LANES // 2


def tile(ref, index, rows=slice(None)):
    return ref[rows, index * LANES : (index + 1) * LANES]


def lanes_of(rows=8):
    return lax.broadcasted_iota(jnp.int32, (rows, LANES), 1)


def rows_of(rows):
    return lax.broadcasted_iota(jnp.int32, (rows, LANES), 0)


def turn(value, shift):
    shift = shift % LANES
    return value if shift == 0 else pltpu.roll(value, shift, 1)


def dot(left, right, contract=(1, 0)):
    return lax.dot_general(
        left,
        right,
        (((contract[0],), (contract[1],)), ((), ())),
        precision=lax.Precision.HIGHEST,
        preferred_element_type=F32,
    )


def pair_matrix(transposed):
    wide = lax.broadcasted_iota(jnp.int32, (LANES, LANES), 1 if transposed else 0)
    narrow = lax.broadcasted_iota(jnp.int32, (LANES, LANES), 0 if transposed else 1)
    return jnp.where(wide // 2 == narrow, 1.0, 0.0).astype(F32)


def stack(values):
    return jnp.concatenate(values, axis=0)


def run(body, outs, vmem, smem=(), scratch=()):
    in_specs = [pl.BlockSpec(memory_space=pltpu.SMEM)] * len(smem)
    in_specs += [pl.BlockSpec(memory_space=pltpu.VMEM)] * len(vmem)
    return pl.pallas_call(
        body,
        out_shape=[SHAPE(shape, F32) for shape in outs],
        in_specs=in_specs,
        out_specs=[pl.BlockSpec(memory_space=pltpu.VMEM)] * len(outs),
        scratch_shapes=[pltpu.VMEM(shape, F32) for shape in scratch],
        compiler_params=pltpu.CompilerParams(vmem_limit_bytes=GRANT),
        interpret=INTERPRET,
    )(*smem, *vmem)


def start_kernel(
    cond_ref, x_far, p_far, class_far, field_ref, zr, zl, yu, yd, xu, xd,
    x_ref, p_ref, class_ref, done,
):
    fetches = [
        pltpu.make_async_copy(far, near, done.at[k])
        for k, (far, near) in enumerate(
            ((class_far, class_ref), (x_far, x_ref), (p_far, p_ref))
        )
    ]
    for fetch in fetches:
        fetch.start()
    for fetch in fetches:
        fetch.wait()
    classes = class_ref[...]
    local = jnp.zeros(classes.shape, F32)
    for index in range(CLASSES):
        local = local + jnp.where(classes == index, cond_ref[index], 0.0)
    lane = lanes_of(40)
    right = jnp.zeros((40, LANES), F32)
    left = jnp.zeros((40, LANES), F32)
    for x in range(LX):
        for y in range(LY):
            p = x * LY + y
            cell = stack(
                [
                    x_ref[pl.ds(p, VECS, stride=FINE), :],
                    p_ref[pl.ds(p, VECS, stride=FINE), :],
                    jnp.broadcast_to(local[p : p + 1], (8, LANES)),
                ]
            )
            field_ref[:, p * LANES : (p + 1) * LANES] = cell
            right = jnp.where(lane == p, turn(cell, p + 1), right)
            left = jnp.where(lane == p, turn(cell, p), left)
            if y == LY - 1:
                yu[:, x * LANES : (x + 1) * LANES] = cell
            if y == 0:
                yd[:, x * LANES : (x + 1) * LANES] = cell
            if x == LX - 1:
                xu[:, y * LANES : (y + 1) * LANES] = cell
            if x == 0:
                xd[:, y * LANES : (y + 1) * LANES] = cell
    zr[...] = right
    zl[...] = left


def finish_weights(weights, shift_term):
    row = rows_of(8)
    weights = jnp.where(row < 6, weights, 0.0)
    diagonal = shift_term + jnp.sum(weights, axis=0, keepdims=True)
    return jnp.where(
        row < 6, weights, jnp.where(row == 6, diagonal, jacobi_weight / diagonal)
    )


def coarsen_weights(fine, size_x, size_y, shift_term, halve):
    row, lane = rows_of(8), lanes_of(8)
    sums = []
    for x in range(size_x):
        for y in range(size_y):
            total = jnp.zeros((8, LANES), F32)
            for i in range(2):
                for j in range(2):
                    keep = (row == i) | (row == 2 + j)
                    keep = keep | ((row == 4) & (lane % 2 == 0)) | ((row == 5) & (lane % 2 == 1))
                    total = total + jnp.where(keep, fine[2 * x + i, 2 * y + j], 0.0)
            sums.append(total)
    paired = dot(stack(sums), halve)
    return {
        (k // size_y, k % size_y): finish_weights(paired[8 * k : 8 * k + 8], shift_term)
        for k in range(size_x * size_y)
    }


def first_kernel(flag_ref, field_ref, zr, zl, yu, yd, xu, xd, xp_ref, axp_ref, cf, cm, cc, ef, em, ec, szr, szl):
    lane, row = lanes_of(8), rows_of(8)
    lane40 = lanes_of(40)
    from_low, from_high = zr[...], zl[...]
    flags = [flag_ref[k] for k in range(6)]
    ends = jnp.where((row == 4) & (lane == 0), flags[4], 1.0)
    ends = jnp.where((row == 5) & (lane == LANES - 1), flags[5], ends)
    fine = {}
    for x in range(LX):
        for y in range(LY):
            p = x * LY + y
            here = tile(field_ref, p)
            beside = [
                tile(field_ref, p - LY) if x > 0 else tile(xu, y),
                tile(field_ref, p + LY) if x < LX - 1 else tile(xd, y),
                tile(field_ref, p - 1) if y > 0 else tile(yu, x),
                tile(field_ref, p + 1) if y < LY - 1 else tile(yd, x),
                jnp.where(lane40 == 0, turn(from_low, -p), turn(here, 1)),
                jnp.where(lane40 == LANES - 1, turn(from_high, LANES - 1 - p), turn(here, -1)),
            ]
            around = stack([value[32:33] for value in beside] + [here[32:34]])
            own = here[32:40]
            keep = ends
            for side, at_end in enumerate((x == 0, x == LX - 1, y == 0, y == LY - 1)):
                if at_end:
                    keep = jnp.where(row == side, flags[side], keep)
            weights = finish_weights(2.0 * around * own / (around + own) * keep, mass_shift)
            fine[x, y] = weights
            cf[:, p * LANES : (p + 1) * LANES] = weights
            applied = weights[6:7] * here[:32]
            for side in range(6):
                applied = applied - weights[side : side + 1] * beside[side][:32]
            xp_ref[:, p * LANES : (p + 1) * LANES] = here[:32]
            axp_ref[:, p * LANES : (p + 1) * LANES] = applied
    halve = pair_matrix(False)
    middle = coarsen_weights(fine, MX, MY, 8.0 * mass_shift, halve)
    for (x, y), value in middle.items():
        k = x * MY + y
        cm[:, k * LANES : (k + 1) * LANES] = value
    coarse = coarsen_weights(middle, CX, CY, 64.0 * mass_shift, halve)
    for (x, y), value in coarse.items():
        cc[:, x * LANES : (x + 1) * LANES] = value
    level_parts(stack([xp_ref[:VECS], axp_ref[:VECS]]), cf, cm, cc, ef, em, ec)
    pack_z(ef, em, ec, cf, cm, cc, szr, szl)


def eliminate(rows, size, full):
    tiles = [rows[8 * i : 8 * i + 8] for i in range(rows.shape[0] // 8)]
    row = rows_of(8)
    kept = list(tiles)
    nothing = rows[:8] * 0.0
    for k in range(0, size, 2):
        at, sub = divmod(k, 8)
        spread_left = tiles[at][:, k : k + 1] + nothing
        spread_right = tiles[at][:, k + 1 : k + 2] + nothing

        def line(value, which):
            return jnp.broadcast_to(value[sub + which : sub + which + 1], (8, LANES))

        first, second = line(tiles[at], 0), line(tiles[at], 1)
        a, b = line(spread_left, 0), line(spread_right, 0)
        c, d = line(spread_left, 1), line(spread_right, 1)
        crossed = a * second - c * first
        inverse = 1.0 / (a * d - b * c)
        solved_first = (d * first - b * second) * inverse
        solved_second = crossed * inverse
        if not full:
            kept[at] = jnp.where(row == sub, first * (1.0 / jnp.sqrt(a)), kept[at])
            root = jnp.sqrt(inverse) * (1.0 / jnp.sqrt(a))
            kept[at] = jnp.where(row == sub + 1, crossed * root, kept[at])
        for i in range(len(tiles)):
            if i < at and not full:
                continue
            if i == at:
                left, right = spread_left, spread_right
            else:
                left, right = tiles[i][:, k : k + 1], tiles[i][:, k + 1 : k + 2]
            changed = tiles[i] - (left * solved_first + right * solved_second)
            if i == at:
                changed = jnp.where(row == sub, solved_first, changed)
                changed = jnp.where(row == sub + 1, solved_second, changed)
            tiles[i] = changed
    return stack(tiles if full else kept)


def lower_pad(matrix):
    missing = LANES - matrix.shape[0]
    return stack([matrix, jnp.zeros((missing, LANES), F32)])


def solve_projected(gram, cross):
    lane = lanes_of(VECS)
    on_diagonal = jnp.where((lane == rows_of(VECS)) & (lane < VECS), gram, 0.0)
    column = 1.0 / jnp.sqrt(jnp.sum(on_diagonal, axis=1, keepdims=True))
    across = jnp.sum(on_diagonal, axis=0, keepdims=True)
    across = jnp.where(lanes_of(1) < VECS, 1.0 / jnp.sqrt(across), 0.0)
    both = jnp.where(lane < HALF, gram * across, turn(cross, HALF)) * column
    return turn(eliminate(both, VECS, True), HALF) * column


def ritz(summed):
    size = 3 * VECS
    lane, row = lanes_of(size), rows_of(size)
    sym_b, sym_a = symmetric(summed)
    on_diagonal = jnp.where(lane == row, sym_b, 0.0)
    column = 1.0 / jnp.sqrt(jnp.sum(on_diagonal, axis=1, keepdims=True))
    across = jnp.sum(on_diagonal, axis=0, keepdims=True)
    across = jnp.where(lanes_of(1) < size, 1.0 / jnp.sqrt(across), 0.0)
    normed_b = sym_b * column * across
    normed_a = sym_a * column * across
    done = eliminate(jnp.where(lane < HALF, normed_a, turn(normed_b, HALF)), size, True)
    step = jnp.where(lane < size, turn(done, HALF), 0.0)
    weighed = dot(normed_b[:, :size], step)
    step_pad, weighed_pad = lower_pad(step), lower_pad(weighed)
    short_lane = lanes_of(VECS)

    def inner_step(_, basis):
        mapped = dot(basis, step_pad, (1, 1))
        product = dot(basis, weighed_pad, (1, 1))
        square = dot(product, lower_pad(mapped), (1, 1))
        done = eliminate(jnp.where(short_lane < HALF, square, turn(mapped, HALF)), VECS, False)
        return jnp.where(short_lane < size, turn(done, HALF), 0.0)

    basis = jnp.where(short_lane == rows_of(VECS), 1.0, 0.0).astype(F32)
    basis = lax.fori_loop(0, INNER, inner_step, basis)
    cross = dot(dot(basis, lower_pad(normed_a), (1, 1)), lower_pad(basis), (1, 1))
    return basis * across, cross


def level_parts(residual, cf, cm, cc, ef, em, ec):
    count = residual.shape[0]
    halve = pair_matrix(False)
    sums = []
    for mx in range(MX):
        for my in range(MY):
            total = jnp.zeros((count, LANES), F32)
            for i in range(2):
                for j in range(2):
                    p = (2 * mx + i) * LY + 2 * my + j
                    part = residual[:, p * LANES : (p + 1) * LANES]
                    total = total + part
                    ef[:, p * LANES : (p + 1) * LANES] = part * tile(cf, p, slice(7, 8))
            sums.append(total)
    paired = dot(stack(sums), halve)
    middle = [paired[count * k : count * (k + 1)] for k in range(MIDDLE)]
    for k in range(MIDDLE):
        em[:, k * LANES : (k + 1) * LANES] = middle[k] * tile(cm, k, slice(7, 8))
    sums = []
    for cx in range(CX):
        sums.append(sum(middle[(2 * cx + i) * MY + j] for i in range(2) for j in range(2)))
    paired = dot(stack(sums), halve)
    for k in range(COARSE):
        coarse = paired[count * k : count * (k + 1)]
        ec[:, k * LANES : (k + 1) * LANES] = coarse * tile(cc, k, slice(7, 8))


def pack_z(ef, em, ec, cf, cm, cc, zr, zl):
    rows = zr.shape[0]
    lane = lanes_of(rows)

    def cell(values, weights, k):
        here = tile(values, k)
        return stack([here, tile(weights, k)]) if rows > values.shape[0] else here

    right = jnp.zeros((rows, LANES), F32)
    left = jnp.zeros((rows, LANES), F32)
    levels = ((ef, cf, FINE, 0, 126), (em, cm, MIDDLE, 64, 62), (ec, cc, COARSE, 80, 30))
    for values, weights, count, base, last in levels:
        for k in range(count):
            here = cell(values, weights, k)
            spot = base + 2 * k
            right = jnp.where(lane // 2 == spot // 2, turn(here, spot - last), right)
            left = jnp.where(lane // 2 == spot // 2, turn(here, spot), left)
    zr[...] = right
    zl[...] = left


Y_TILES, X_TILES = 25, 17


def apart_tile(ref, base, k):
    return tile(ref, base + k // 4, slice(8 * (k % 4), 8 * (k % 4) + 8))


class Level:
    def __init__(
        self, own, low, high, rows, count, yu=None, yd=None, xu=None, xd=None,
        y2u=None, y2d=None, inner=slice(None), apart=False,
    ):
        self.own, self.inner, self.apart = own, inner, apart
        self.low, self.high = low[rows], high[rows]
        self.yu, self.yd, self.xu, self.xd, self.y2u, self.y2d = yu, yd, xu, xd, y2u, y2d
        self.lane = lanes_of(count)
        self.kept = {}

    def once(self, key, make):
        if key not in self.kept:
            self.kept[key] = make()
        return self.kept[key]

    def own_rows(self, ref, k):
        return tile(ref, k, self.inner)

    def fine(self, x, y):
        if 0 <= x < LX and 0 <= y < LY:
            return self.own_rows(self.own[0], x * LY + y)
        if 0 <= x < LX:
            ref, layer = (self.yu, y + 2) if y < 0 else (self.yd, y - LY)
            if self.apart:
                return apart_tile(ref, Y_TILES, x)
            return tile(ref, 2 * x + layer, self.inner)
        ref, near = (self.xu, x == -1) if x < 0 else (self.xd, x == LX)
        if self.apart:
            return apart_tile(ref, X_TILES, y)
        return tile(ref, y + 1 if near else 6 + y, self.inner)

    def fine_end(self, x, y):
        def make():
            if 0 <= x < LX and 0 <= y < LY:
                p = x * LY + y
                return jnp.where(
                    self.lane < HALF, turn(self.high, -2 * p), turn(self.low, 126 - 2 * p)
                )
            if 0 <= x < LX:
                return turn(tile(self.yu if y < 0 else self.yd, 16, self.inner), -(1 + 2 * x))
            return turn(tile(self.xu if x < 0 else self.xd, 10, self.inner), -(1 + 2 * y))

        return self.once(("end", x, y), make)

    def middle(self, x, y):
        def make():
            if 0 <= x < MX and 0 <= y < MY:
                k = x * MY + y
                beyond = jnp.where(
                    self.lane < 96, turn(self.high, -2 * k), turn(self.low, 62 - 2 * k)
                )
                return jnp.where(self.lane < 64, self.own_rows(self.own[1], k), beyond)
            if 0 <= x < MX:
                ref = self.yu if y < 0 else self.yd
                if self.apart:
                    return apart_tile(ref, Y_TILES, LX + x)
                if y in (-1, MY):
                    return tile(ref, 17 + x, self.inner)
                return turn(tile(ref, 21 + x // 2, self.inner), -64 * (x % 2))
            ref, near = (self.xu, x == -1) if x < 0 else (self.xd, x == MX)
            if self.apart:
                return apart_tile(ref, X_TILES, LY + y)
            if not near:
                return turn(tile(ref, 14, self.inner), -64 * y)
            if 0 <= y < MY:
                return tile(ref, 11 + y, self.inner)
            return turn(tile(ref, 13, self.inner), 0 if y < 0 else -64)

        return self.once(("middle", x, y), make)

    def coarse(self, x, y):
        def make():
            if 0 <= x < CX and y == 0:
                beyond = jnp.where(
                    self.lane < 64, turn(self.high, -48 - 2 * x), turn(self.low, 46 - 2 * x)
                )
                return jnp.where(self.lane < 32, self.own_rows(self.own[2], x), beyond)
            if 0 <= x < CX:
                if abs(y) == 2:
                    return tile(self.y2u if y < 0 else self.y2d, x, self.inner)
                ref = self.yu if y < 0 else self.yd
                if self.apart:
                    return apart_tile(ref, Y_TILES, LX + MX + x)
                return tile(ref, 23 + x, self.inner)
            ref, near = (self.xu, x == -1) if x < 0 else (self.xd, x == CX)
            if self.apart:
                return apart_tile(ref, X_TILES, LY + MY)
            if near and y == 0:
                return tile(ref, 15, self.inner)
            return turn(tile(ref, 16, self.inner), -64 if not near else 0 if y < 0 else -32)

        return self.once(("coarse", x, y), make)


def put(ref, index, value):
    ref[:, index * LANES : (index + 1) * LANES] = value


def pack_ends(values):
    rows = values[0].shape[0]
    lane = lanes_of(rows)
    packed = jnp.zeros((rows, LANES), F32)
    for k, value in enumerate(values):
        packed = jnp.where(lane // 2 == k, turn(value, 1 + 2 * k), packed)
    return packed


def halves(left, right):
    return jnp.where(lanes_of(left.shape[0]) < HALF, left, turn(right, HALF))


def put_apart(ref, base, weights):
    if ref.shape[1] == base * LANES:
        return
    for k in range(0, len(weights), 4):
        group = weights[k : k + 4]
        put(ref, base + k // 4, stack(group + group[:1] * (4 - len(group))))


def pack_y_kernel(ef, em, ec, cf, cm, cc, zr, zl, yu, yd):
    count = ef.shape[0]
    level = Level((ef, em, ec), zr, zl, slice(0, count), count)
    for ref, first, edge, near, far in ((yu, LY - 2, LY - 1, MY - 1, 0), (yd, 0, 0, 0, MY - 1)):
        for x in range(LX):
            for j in range(2):
                put(ref, 2 * x + j, level.fine(x, first + j))
        put(ref, 16, pack_ends([level.fine_end(x, edge) for x in range(LX)]))
        for x in range(MX):
            put(ref, 17 + x, level.middle(x, near))
        for k in range(MX // 2):
            put(ref, 21 + k, halves(level.middle(2 * k, far), level.middle(2 * k + 1, far)))
        for x in range(CX):
            put(ref, 23 + x, level.coarse(x, 0))
        weights = [tile(cf, x * LY + edge) for x in range(LX)]
        weights += [tile(cm, x * MY + near) for x in range(MX)]
        put_apart(ref, Y_TILES, weights + [tile(cc, x) for x in range(CX)])


def pack_x_kernel(ef, em, ec, cf, cm, cc, zr, zl, ryu, ryd, y2u, y2d, xu, xd):
    count = ef.shape[0]
    lane = lanes_of(count)
    level = Level((ef, em, ec), zr, zl, slice(0, count), count, ryu, ryd)
    for ref, up in ((xu, True), (xd, False)):
        near, far = (LX - 1, LX - 2) if up else (0, 1)
        for y in range(-1, LY + 1):
            put(ref, y + 1, level.fine(near, y))
        for y in range(LY):
            put(ref, 6 + y, level.fine(far, y))
        put(ref, 10, pack_ends([level.fine_end(near, y) for y in range(LY)]))
        weights = [tile(cf, near * LY + y) for y in range(LY)]
        near, far = (MX - 1, MX - 2) if up else (0, 1)
        for y in range(MY):
            put(ref, 11 + y, level.middle(near, y))
        put(ref, 13, halves(level.middle(near, -1), level.middle(near, MY)))
        put(ref, 14, halves(level.middle(far, 0), level.middle(far, 1)))
        weights += [tile(cm, near * MY + y) for y in range(MY)]
        near, far = (CX - 1, CX - 2) if up else (0, 1)
        put(ref, 15, level.coarse(near, 0))
        ends = jnp.where(lane < 32, level.coarse(near, -1), turn(level.coarse(near, 1), 32))
        put(ref, 16, halves(ends, level.coarse(far, 0)))
        put_apart(ref, X_TILES, weights + [tile(cc, near)])


def faces(size_x, size_y):
    own = [(x, y) for x in range(size_x) for y in range(size_y)]
    beyond = [(x, y) for x in (-1, size_x) for y in range(size_y)]
    beyond += [(x, y) for x in range(size_x) for y in (-1, size_y)]
    return own, beyond


def neighbours(x, y):
    return ((x - 1, y), (x + 1, y), (x, y - 1), (x, y + 1))


def spread(weights, values):
    total = weights[0:1] * values[0]
    for side in range(1, 6):
        total = total + weights[side : side + 1] * values[side]
    return total


def smooth_tile(weights, here, values):
    return (2.0 * jacobi_weight) * here + weights[7:8] * spread(weights, values)


def search_kernel(
    xp_ref, axp_ref, ef, em, ec, cf, cm, cc,
    zr, zl, yu, yd, xu, xd, y2u, y2d,
    wzr, wzl, wyu, wyd, wxu, wxd,
    wa_ref, gram, basis_ref,
):
    size = PAIR + ef.shape[0]
    basis_ref[:PAIR] = xp_ref[...]
    basis_ref[HALF : HALF + PAIR] = axp_ref[...]
    if size < HALF:
        blank = jnp.zeros((HALF - size, FINE * LANES), F32)
        basis_ref[size:HALF] = blank
        basis_ref[HALF + size :] = blank

    def rows_at(start, step):
        return slice(start + step * VECS, start + (step + 1) * VECS)

    for step in range((size - PAIR) // VECS):
        rows = rows_at(0, step)
        values = Level(
            (ef, em, ec), zr, zl, rows, VECS, yu, yd, xu, xd, y2u, y2d, rows
        )
        weights = Level(
            (cf, cm, cc), wzr, wzl, slice(PAIR, PAIR + 8), 8, wyu, wyd, wxu, wxd, apart=True
        )
        targets = (
            (wa_ref, rows, rows_at(ef.shape[0], step)),
            (basis_ref, rows_at(PAIR, step), rows_at(HALF + PAIR, step)),
        )
        smooth_block(values, weights, cf, targets)
    gram[...] = dot(basis_ref[:size], basis_ref[...], (1, 1))


def smooth_block(values, weights, cf, targets):
    lane = lanes_of(VECS)
    double = pair_matrix(True)

    own, beyond = faces(CX, CY)
    coarse_cells = own + beyond
    smoothed = []
    for cell in coarse_cells:
        here = values.coarse(*cell)
        around = [values.coarse(*other) for other in neighbours(*cell)]
        around += [turn(here, 1), turn(here, -1)]
        smoothed.append(smooth_tile(weights.coarse(*cell), here, around))
    doubled = dot(stack(smoothed), double)
    to_middle = {}
    for k, cell in enumerate(coarse_cells):
        ends = jnp.where(lane < 96, turn(smoothed[k], 32), smoothed[k])
        inner = doubled[VECS * k : VECS * (k + 1)]
        to_middle[cell] = jnp.where(lane < 64, inner, ends)

    own, beyond = faces(MX, MY)
    middle_cells = own + beyond
    smoothed = []
    for cell in middle_cells:
        here = values.middle(*cell)
        around = [values.middle(*other) for other in neighbours(*cell)]
        around += [turn(here, 1), turn(here, -1)]
        part = smooth_tile(weights.middle(*cell), here, around)
        smoothed.append(part + to_middle[cell[0] // 2, cell[1] // 2])
    doubled = dot(stack(smoothed), double)
    to_fine, to_end = {}, {}
    for k, cell in enumerate(middle_cells):
        to_fine[cell] = doubled[VECS * k : VECS * (k + 1)]
        to_end[cell] = jnp.where(lane < HALF, turn(smoothed[k], 64), smoothed[k])

    def zs(main, end):
        low = jnp.where(lane > 0, turn(main, 1), turn(end, 1))
        high = jnp.where(lane < LANES - 1, turn(main, -1), turn(end, -1))
        return [low, high]

    own, beyond = faces(LX, LY)
    found, found_end = {}, {}
    for cell in beyond + own:
        here, end = values.fine(*cell), values.fine_end(*cell)
        around = [values.fine(*other) for other in neighbours(*cell)] + zs(here, end)
        part = smooth_tile(weights.fine(*cell), here, around)
        found[cell] = part + to_fine[cell[0] // 2, cell[1] // 2]
    for cell in own:
        here, end = values.fine(*cell), values.fine_end(*cell)
        around = [values.fine_end(*other) for other in neighbours(*cell)] + zs(end, here)
        part = smooth_tile(weights.fine_end(*cell), end, around)
        found_end[cell] = part + to_end[cell[0] // 2, cell[1] // 2]
    for cell in own:
        k = cell[0] * LY + cell[1]
        here = found[cell]
        factors = tile(cf, k)
        around = [found[other] for other in neighbours(*cell)] + zs(here, found_end[cell])
        applied = factors[6:7] * here - spread(factors, around)
        columns = slice(k * LANES, (k + 1) * LANES)
        for ref, first, second in targets:
            ref[first, columns] = here
            ref[second, columns] = applied


def symmetric(summed):
    size = summed.shape[0]
    lane = lanes_of(size)
    flipped = lower_pad(summed).T
    sym_b = 0.5 * (summed + flipped[:size])
    sym_a = 0.5 * (turn(summed, HALF) + flipped[HALF : HALF + size])
    return jnp.where(lane < size, sym_b, 0.0), jnp.where(lane < size, sym_a, 0.0)


def judge_kernel(summed, gram, change, flag):
    size = 3 * VECS
    sym_b, sym_a = symmetric(summed[...])
    lane, row = lanes_of(VECS), rows_of(VECS)
    projected = solve_projected(
        jnp.where(lane < VECS, sym_b[:VECS], 0.0), jnp.where(lane < VECS, sym_a[:VECS], 0.0)
    )
    projected = jnp.where(lane < VECS, projected, 0.0)
    backward = turn(lower_pad(projected).T[:VECS], PAIR)
    direct = jnp.where(lanes_of(PAIR) == rows_of(PAIR), 1.0, 0.0).astype(F32)
    tail = jnp.where(lane == row + 3 * VECS, 1.0, 0.0).astype(F32) - backward
    mixing = stack([direct, tail])
    padded = lower_pad(mixing)
    small_b = dot(dot(mixing[:, :HALF], sym_b), padded, (1, 1))
    small_a = dot(dot(mixing[:, :HALF], sym_a), padded, (1, 1))
    gram[...] = jnp.where(lanes_of(size) < HALF, small_b, turn(small_a, HALF))
    change[...] = mixing
    lost = jnp.zeros((VECS, 1), F32)
    for small, full in ((small_b, sym_b), (small_a, sym_a)):
        after = jnp.where(lane == row + PAIR, small[PAIR:], 0.0)
        before = jnp.where(lane == row + 3 * VECS, full[3 * VECS :], 0.0)
        after = jnp.sum(after, axis=1, keepdims=True)
        before = jnp.sum(before, axis=1, keepdims=True)
        lost = jnp.maximum(lost, jnp.where(after > KEEP * before, 0.0, 1.0))
    flag[...] = jnp.broadcast_to(jnp.max(lost, axis=0, keepdims=True), (8, LANES))


def combine(coefficients, change, sources, targets):
    lane = lanes_of(VECS)
    both = stack([coefficients, jnp.where(lane >= VECS, coefficients, 0.0)])
    if change is not None:
        both = dot(both[:, : 3 * VECS], change)
    count = sources[0][1].stop - sources[0][1].start
    both = both[:, : PAIR + count]
    for (old, rows, found), target in zip(sources, targets):
        target[...] = dot(both, stack([old[...], found[rows]]))


def mixed_kernel(
    gram, change, xp_ref, axp_ref, wa_ref, cf, cm, cc, nxp, naxp, ef, em, ec, zr, zl
):
    coefficients, projected = ritz(gram[...])
    own, applied = slice(0, PAIR), slice(PAIR, 2 * PAIR)
    sources = ((xp_ref, own, wa_ref), (axp_ref, applied, wa_ref))
    combine(coefficients, change[...], sources, (nxp, naxp))
    residual = naxp[:VECS] - dot(projected[:, :VECS], nxp[:VECS], (0, 0))
    level_parts(residual, cf, cm, cc, ef, em, ec)
    pack_z(ef, em, ec, cf, cm, cc, zr, zl)


def careful_kernel(change, xp_ref, axp_ref, wide_ref, gram, basis_ref):
    part = change[PAIR:, PAIR:HALF]
    width = 2 * LANES
    blank = jnp.zeros((VECS, width), F32)

    def add(step, total):
        columns = pl.ds(pl.multiple_of(step * width, width), width)
        for at, values, first in ((0, xp_ref, 0), (HALF, axp_ref, PAIR)):
            basis_ref[at : at + PAIR, columns] = values[:, columns]
            found = dot(part, wide_ref[first : first + PAIR, columns])
            basis_ref[at + PAIR : at + 3 * VECS, columns] = found
            basis_ref[at + 3 * VECS : at + HALF, columns] = blank
        return total + dot(basis_ref[: 3 * VECS, columns], basis_ref[:, columns], (1, 1))

    total = jnp.zeros((3 * VECS, LANES), F32)
    gram[...] = lax.fori_loop(0, FINE * LANES // width, add, total)


def last_kernel(summed, xp_ref, wa_ref, x_out, p_out, moved):
    coefficients, _ = ritz(summed[...])
    combine(coefficients, None, ((xp_ref, slice(0, VECS), wa_ref),), (moved,))
    for k in range(FINE):
        x_out[pl.ds(k, VECS, stride=FINE), :] = tile(moved, k, slice(0, VECS))
        p_out[pl.ds(k, VECS, stride=FINE), :] = tile(moved, k, slice(VECS, PAIR))


def shifted(values, axis, by):
    peers = lax.axis_size(axis)
    return lax.ppermute(values, axis, [(i, (i + by) % peers) for i in range(peers)])


def masks_of(size):
    return {1: [], 2: [1], 4: [1, 3], 8: [1, 2, 6]}[size]


def all_sum(values):
    rounds = [(k, axis, m) for axis in ("gy", "gx", "gz") for k, m in enumerate(masks_of(lax.axis_size(axis)))]
    for _, axis, mask in sorted(rounds, key=lambda entry: entry[0]):
        pairs = [(i, i ^ mask) for i in range(lax.axis_size(axis))]
        values = values + lax.ppermute(values, axis, pairs)
    return values


def exchange(parts, weights, zr, zl):
    ec = parts[2]
    count = ec.shape[0]
    extra = (4, 2) if zr.shape[0] > count else (0, 0)
    zr, zl = shifted(zr, "gz", 1), shifted(zl, "gz", -1)
    y2u, y2d = shifted(ec, "gy", 2), shifted(ec, "gy", -2)
    shape = (count, (Y_TILES + extra[0]) * LANES)
    yu, yd = run(pack_y_kernel, [shape] * 2, (*parts, *weights, zr, zl))
    yu, yd = shifted(yu, "gy", 1), shifted(yd, "gy", -1)
    shape = (count, (X_TILES + extra[1]) * LANES)
    xu, xd = run(pack_x_kernel, [shape] * 2, (*parts, *weights, zr, zl, yu, yd, y2u, y2d))
    xu, xd = shifted(xu, "gx", 1), shifted(xd, "gx", -1)
    return (zr, zl, yu, yd, xu, xd), (y2u, y2d)


def on_device(x_block, p_block, voxel_class, conductance):
    sizes = [lax.axis_size(axis) for axis in ("gx", "gy", "gz")]
    all_cells = FINE * LANES * sizes[0] * sizes[1] * sizes[2]
    wide = FINE * LANES
    flags = []
    for axis, size in zip(("gx", "gy", "gz"), sizes):
        at = lax.axis_index(axis)
        flags += [at > 0, at < size - 1]
    flags = jnp.stack(flags).astype(F32)
    far = (
        x_block.reshape(VECS * FINE, LANES),
        p_block.reshape(VECS * FINE, LANES),
        voxel_class.reshape(FINE, LANES),
    )
    if not INTERPRET:
        far = [pltpu.with_memory_space_constraint(array, pltpu.HBM) for array in far]
    sides = [(40, wide)] + [(40, LANES)] * 2 + [(40, LX * LANES)] * 2 + [(40, LY * LANES)] * 2
    field, zr, zl, yu, yd, xu, xd = pl.pallas_call(
        start_kernel,
        out_shape=[SHAPE(shape, F32) for shape in sides],
        in_specs=[pl.BlockSpec(memory_space=pltpu.SMEM)]
        + [pl.BlockSpec(memory_space=pltpu.HBM)] * 3,
        out_specs=[pl.BlockSpec(memory_space=pltpu.VMEM)] * len(sides),
        scratch_shapes=[pltpu.VMEM((VECS * FINE, LANES), F32)] * 2
        + [pltpu.VMEM((FINE, LANES), jnp.int32), pltpu.SemaphoreType.DMA((3,))],
        compiler_params=pltpu.CompilerParams(vmem_limit_bytes=GRANT),
        interpret=INTERPRET,
    )(
        conductance,
        *far,
    )
    arrived = (
        shifted(zr, "gz", 1), shifted(zl, "gz", -1), shifted(yu, "gy", 1),
        shifted(yd, "gy", -1), shifted(xu, "gx", 1), shifted(xd, "gx", -1),
    )
    fields = [(PAIR, wide)] * 2
    weight_shapes = [(8, wide), (8, MIDDLE * LANES), (8, COARSE * LANES)]

    def part_shapes(rows):
        return [(rows, wide), (rows, MIDDLE * LANES), (rows, COARSE * LANES)]

    xp, axp, cf, cm, cc, *parts, zr, zl = run(
        first_kernel,
        fields + weight_shapes + part_shapes(PAIR) + [(PAIR + 8, LANES)] * 2,
        (field, *arrived),
        (flags,),
    )
    weights = (cf, cm, cc)
    basis = [(2 * HALF, wide)]

    def search(parts, sent, far, sent_weights):
        rows = parts[0].shape[0]
        inputs = (xp, axp, *parts, *weights, *sent, *far, *sent_weights)
        shapes = [(2 * rows, wide), (PAIR + rows, LANES)]
        return run(search_kernel, shapes, inputs, scratch=basis)

    sent_weights, far = exchange(parts, weights, zr, zl)
    wa, gram = search(parts, sent_weights, far, sent_weights)
    summed = all_sum(gram) * (1.0 / all_cells)
    small = (3 * VECS, LANES)
    gram, change, flag = run(judge_kernel, [small, small, (8, LANES)], (summed,))
    nexts = fields + part_shapes(VECS) + [(VECS, LANES)] * 2

    def careful(gram, change, wa):
        (gram,) = run(careful_kernel, [small], (change, xp, axp, wa), scratch=basis)
        return lax.psum(gram, ("gx", "gy", "gz")) * (1.0 / all_cells)

    def given(gram, change, wa):
        return gram

    gram = lax.cond(flag[0, 0] > 0.5, careful, given, gram, change, wa)
    xp, axp, *parts, zr, zl = run(mixed_kernel, nexts, (gram, change, xp, axp, wa, *weights))
    sent, far = exchange(parts, weights, zr, zl)
    wa, gram = search(parts, sent, far, sent_weights)
    gram = all_sum(gram) * (1.0 / all_cells)
    outs = [(VECS * FINE, LANES)] * 2
    x_out, p_out = run(last_kernel, outs, (gram, xp, wa), scratch=[(PAIR, wide)])
    return (x_out.reshape(x_block.shape), p_out.reshape(x_block.shape))


def solution(mesh):
    in_specs = (P(None, "gx", "gy", "gz"), P(None, "gx", "gy", "gz"), P("gx", "gy", "gz"), P())
    out_specs = (P(None, "gx", "gy", "gz"), P(None, "gx", "gy", "gz"))
    return jax.shard_map(
        on_device, mesh=mesh, in_specs=in_specs, out_specs=out_specs, check_vma=False
    )
```
